256 devices in a mesh: head: 4 (over x), blk: 64 (over y, z, core).
Axes of the slice: x: 4, y: 4, z: 8, core: 2. Of those that a mesh axis runs over, the one named last changes fastest.
Arguments:
- hidden_in: bfloat16 [16384, 1536], P('blk'), may hold values from -6 to 6
- attn_gain: float32 [1536], replicated, may hold values from 0.5 to 2
- w_query: bfloat16 [1536, 1536], P(None, 'head'), may hold values from -0.15625 to 0.15625
- w_keyval: bfloat16 [2, 1536, 256], replicated, may hold values from -0.375 to 0.375
- prefix_cache: bfloat16 [4096, 2, 256], P('blk'), may hold values from -490 to 490
- w_out: bfloat16 [1536, 1536], P('head'), may hold values from -0.15625 to 0.15625
- moe_gain: float32 [1536], replicated, may hold values from 0.5 to 2
- w_gateup: bfloat16 [64, 1536, 768], P('blk'), may hold values from -0.15625 to 0.15625
- w_down: bfloat16 [64, 384, 1536], P('blk'), may hold values from -0.21875 to 0.21875
- routes: int32 [16384, 4], P('blk'), may hold values from 0 to 31, all different within a row; in each aligned block of 64 rows (0 to 63, 64 to 127, ...) at most 16 rows name the same one
- route_weights: float32 [16384, 4], P('blk'), may hold values from 0.1 to 1
- lengths: int32 [32], replicated, may hold values from 1 to 2048, 16384 in all
Outputs:
- layer_out: bfloat16 [16384, 1536], P('blk', 'head')
The draws below stay inside these ranges and needn't reach their ends.
Inputs may be any that keep to these rules, and one draw needn't show every extreme that they name: The lengths sum to 16384; the longest is exactly 2048. `routes`: each row names 4 different experts. In each aligned block of 64 rows no expert is named by more than 16 rows, a bound that some block reaches.
All inputs are finite; a program needn't handle non-finite values.
Results may differ from the reference program's by a relative error of at most 0.02.
The reference program's roundings to bfloat16 on the way count: a program that leaves them out, or rounds other values in their place, can miss the bound.
Values may be sent and summed in bfloat16 or wider, within the bound.
A program may use at most 128 MiB of HBM per device.

```python
import math
import jax
import jax.numpy as jnp
import numpy as np
from jax import lax

D = 1536
QH = 12
KVH = 2
HD = 128
FF = 768
TOPK = 4
EXPERTS = 32
FF_HALF = 384
SUFFIX = 16384
PREFIX = 4096
MOST = 2048
REQS = 32
MOE_ROWS = 64
CAP = 16


def draw_prefix_cache(key, part):
    base = jax.random.truncated_normal(key, -4.0, 4.0, (PREFIX, KVH, 2 * HD), jnp.float32) * 2.4
    return base.astype(jnp.bfloat16)


def level_of(key, shape, cuts, low, largest):
    factor_of = 1.0
    for dim, parts in cuts:
        steps = jax.random.uniform(jax.random.fold_in(jax.random.fold_in(key, 6), dim), (parts,), jnp.float32, low / len(cuts), largest / len(cuts))
        factor_of = factor_of * jnp.repeat(jnp.exp(steps), shape[dim] // parts).reshape((-1,) + (1,) * (len(shape) - 1 - dim))
    return factor_of


def length_profile(count, total, bound, lean):
    portions = [(1 << 20) // math.isqrt(rank ** lean) + 1 for rank in range(2, count + 1)]
    spare, counts = total - bound - (count - 1), [1] * (count - 1)
    while spare > 0:
        movable = [i for i in range(count - 1) if counts[i] < bound]
        mass, budget = sum([portions[i] for i in movable]), spare
        for i in movable:
            addition = min(bound - counts[i], max(1, budget * portions[i] // mass), spare)
            counts[i] = counts[i] + addition
            spare = spare - addition
    return np.array([bound] + counts)


def ragged(rng, amount, total, bound, skew):
    if amount == 2:
        one = jax.random.randint(rng, (), max(1, total - bound), min(bound, total - 1) + 1)
        return jnp.stack([one, total - one])
    tallies = jnp.asarray(length_profile(amount, total, bound, skew), jnp.int32)
    twos = (amount - 1) // 2
    source_of, taker = tallies[1:1 + 2 * twos:2], tallies[2:2 + 2 * twos:2]
    margin = jnp.minimum(source_of - 1, bound - taker)
    moved = jax.random.randint(jax.random.fold_in(rng, 1), (twos,), 0, 1 << 20) % (margin + 1)
    tallies = tallies.at[1:1 + 2 * twos:2].set(source_of - moved).at[2:2 + 2 * twos:2].set(taker + moved)
    return tallies[jax.random.permutation(jax.random.fold_in(rng, 2), amount)]


def assign_block(stream_key, own, number, rows, amount, top, most, slope):
    ranking = jax.random.permutation(stream_key, amount)
    crowded, usual = load_shares(amount, rows * top, most, slope, True), load_shares(amount, rows * top, most, slope, False)
    places = jnp.arange(amount)

    def named(sizes, rotation):
        used = int((sizes > 0).sum())
        fixed = max(1, used // 4)
        shifted = fixed + (places - fixed + rotation * (used - fixed)) % max(1, amount - fixed)
        return jnp.zeros((amount,), jnp.int32).at[ranking[jnp.where(places < fixed, places, shifted)]].set(jnp.asarray(sizes, jnp.int32))

    sizes = jnp.where(number % 4 == 0, named(crowded, number // 4), named(usual, number - number // 4 - 1))
    mixed = jax.random.permutation(jax.random.fold_in(own, 3), amount)
    giver, receiver = mixed[0:amount // 2 * 2:2], mixed[1:amount // 2 * 2:2]
    margin = jnp.minimum(sizes[giver] - 1, most - sizes[receiver]) // 2
    margin = jnp.where((giver == ranking[0]) | (receiver == ranking[0]) | (sizes[receiver] == 0), 0, jnp.maximum(margin, 0))
    shifted = jax.random.randint(jax.random.fold_in(own, 4), (amount // 2,), 0, 1 << 20) % (margin + 1)
    sizes = sizes.at[giver].add(-shifted).at[receiver].add(shifted)
    items = jnp.searchsorted(jnp.cumsum(sizes), jnp.arange(rows * top), side="right").astype(jnp.int32)
    table = items.reshape(top, rows).T
    table = table[jax.random.permutation(jax.random.fold_in(own, 1), rows)]
    rotation = jax.random.randint(jax.random.fold_in(own, 2), (rows, 1), 0, top)
    return jnp.take_along_axis(table, (jnp.arange(top)[None, :] + rotation) % top, axis=1)


def load_shares(amount, total, reach, slope, full):
    loads = [(1 << 20) // math.isqrt(standing ** slope) + 1 for standing in range(1, amount + 1)]
    largest = reach if full else min(reach, max(-(-total // amount), total * loads[0] // sum(loads)))
    least = 1 if total - largest >= amount - 1 else 0
    given, spare = [largest] + [least] * (amount - 1), total - largest - least * (amount - 1)
    while spare > 0:
        free = [i for i in range(1, amount) if given[i] < largest] or [i for i in range(1, amount) if given[i] < reach]
        mass, budget = sum([loads[i] for i in free]), spare
        for i in free:
            addition = min(reach - given[i], max(1, budget * loads[i] // mass), spare)
            given[i] = given[i] + addition
            spare = spare - addition
    return np.array(given)


def normal_values(key, extent, deviation, reach, cuts=(), kind=jnp.bfloat16):
    result = deviation * jax.random.normal(key, extent, jnp.float32)
    if cuts:
        result = result * level_of(key, extent, cuts, -0.22, 0.18)
    return jnp.clip(result, -reach, reach).astype(kind)


def setup_inputs(seed: int = 0) -> dict:
    key_list = jax.random.split(jax.random.key(seed), 13)
    hidden_in = normal_values(key_list[0], (SUFFIX, D), 1.0, 6.0, ((0, 64),))
    attn_gain = jnp.clip(jnp.exp(jax.random.uniform(key_list[1], (D,), jnp.float32, math.log(0.5), math.log(2.0))), 0.5, 2.0)
    w_query = normal_values(key_list[2], (D, QH * HD), D ** -0.5, 0.15625, ((1, 4),))
    w_keyval = normal_values(key_list[3], (KVH, D, 2 * HD), (D // 6) ** -0.5, 0.375)
    prefix_cache = draw_prefix_cache(jax.random.fold_in(key_list[12], 71), 0)
    w_out = normal_values(key_list[5], (QH * HD, D), (QH * HD) ** -0.5, 0.15625, ((0, 4),))
    moe_gain = jnp.clip(jnp.exp(jax.random.uniform(key_list[6], (D,), jnp.float32, math.log(0.5), math.log(2.0))), 0.5, 2.0)
    w_gateup = normal_values(key_list[7], (2 * EXPERTS, D, FF), D ** -0.5, 0.15625, ((0, 64),))
    w_down = normal_values(key_list[8], (2 * EXPERTS, FF_HALF, D), FF ** -0.5, 0.21875, ((0, 64),))
    routes_keys = jax.random.split(jax.random.fold_in(key_list[9], 1), SUFFIX // MOE_ROWS)
    routes_turns = jax.random.permutation(jax.random.fold_in(key_list[9], 3), SUFFIX // MOE_ROWS)
    routes = jax.vmap(lambda own, number: assign_block(jax.random.fold_in(key_list[9], 2), own, number, MOE_ROWS, EXPERTS, TOPK, CAP, 2))(routes_keys, routes_turns).reshape((SUFFIX, TOPK))
    route_weights = jnp.clip(jnp.exp(math.log(1.0) - 2.3025851 * jax.random.uniform(key_list[10], (SUFFIX, TOPK), jnp.float32) ** level_of(key_list[10], (SUFFIX, TOPK), ((0, 64),), -0.2, 0.2)), 0.1, 1.0)
    lengths = ragged(key_list[11], REQS, SUFFIX, MOST, 2).astype(jnp.int32)
    return {"hidden_in": hidden_in, "attn_gain": attn_gain, "w_query": w_query, "w_keyval": w_keyval, "prefix_cache": prefix_cache, "w_out": w_out, "moe_gain": moe_gain, "w_gateup": w_gateup, "w_down": w_down, "routes": routes, "route_weights": route_weights, "lengths": lengths}


def rms_norm(values, gain):
    wide = values.astype(jnp.float32)
    return wide * lax.rsqrt(lax.optimization_barrier(jnp.mean(wide * wide, axis=-1, keepdims=True)) + 1e-05) * gain

def rotate(vectors, positions):
    half = vectors.shape[-1] // 2
    freqs = 10000.0 ** (-2.0 * jnp.arange(half, dtype=jnp.float32) / vectors.shape[-1])
    angle = positions[:, None] * freqs[None, :]
    cosine = jnp.cos(angle)[:, None, :]
    sine = jnp.sin(angle)[:, None, :]
    first = vectors[..., :half]
    second = vectors[..., half:]
    return jnp.concatenate([first * cosine - second * sine, second * cosine + first * sine], axis=-1)

def request_info(index, lengths):
    ends = jnp.cumsum(lengths).astype(jnp.int32)
    seg = lax.optimization_barrier(jnp.sum((index[:, None] >= ends[None, :]).astype(jnp.int32), axis=1)).astype(jnp.int32)
    starts = (ends - lengths).astype(jnp.int32)
    count = lengths.shape[0]
    begin = lax.optimization_barrier(jnp.sum(jnp.where(seg[:, None] == jnp.arange(count, dtype=jnp.int32)[None, :], starts[None, :], 0), axis=1)).astype(jnp.int32)
    return (seg, (index - begin).astype(jnp.int32))

def reference(hidden_in, attn_gain, w_query, w_keyval, prefix_cache, w_out, moe_gain, w_gateup, w_down, routes, route_weights, lengths):
    token_index = jnp.arange(SUFFIX, dtype=jnp.int32)
    seg_all, offset_all = request_info(token_index, lengths)
    positions = (PREFIX + offset_all).astype(jnp.float32)
    normed = rms_norm(hidden_in, attn_gain).astype(jnp.bfloat16)
    queries = jnp.dot(normed, w_query, preferred_element_type=jnp.float32).reshape(SUFFIX, QH, HD)
    queries = (rotate(queries, positions) * HD ** (-0.5)).astype(jnp.bfloat16)
    keyval = jnp.stack([jnp.dot(normed, w_keyval[g], preferred_element_type=jnp.float32) for g in range(KVH)], axis=1)
    new_keys = rotate(keyval[..., :HD], positions).astype(jnp.bfloat16)
    new_values = keyval[..., HD:].astype(jnp.bfloat16)
    cached_keys = prefix_cache[..., :HD]
    cached_values = prefix_cache[..., HD:]
    block = min(256, SUFFIX)
    window = min(MOST + block, SUFFIX)
    group = QH // KVH

    def one_block(block_id):
        first = (block_id * block).astype(jnp.int32)
        query_rows = lax.dynamic_slice_in_dim(queries, first, block, 0).astype(jnp.float32).reshape(block, KVH, group, HD)
        lowest = jnp.clip(first - MOST, 0, SUFFIX - window).astype(jnp.int32)
        keys_win = lax.dynamic_slice_in_dim(new_keys, lowest, window, 0)
        values_win = lax.dynamic_slice_in_dim(new_values, lowest, window, 0)
        keys_all = jnp.concatenate([cached_keys, keys_win], axis=0).astype(jnp.float32)
        values_all = jnp.concatenate([cached_values, values_win], axis=0).astype(jnp.float32)
        scores = jnp.einsum('tgjd,kgd->tgjk', query_rows, keys_all)
        query_index = first + jnp.arange(block, dtype=jnp.int32)
        key_index = lowest + jnp.arange(window, dtype=jnp.int32)
        query_seg, unused_q = request_info(query_index, lengths)
        key_seg, unused_k = request_info(key_index, lengths)
        valid_new = (query_seg[:, None] == key_seg[None, :]) & (key_index[None, :] <= query_index[:, None])
        valid = jnp.concatenate([jnp.ones((block, PREFIX), dtype=bool), valid_new], axis=1)[:, None, None, :]
        scores = jnp.where(valid, scores, -1e+30)
        highest = lax.optimization_barrier(jnp.max(scores, axis=-1, keepdims=True))
        weights = jnp.where(valid, jnp.exp(scores - highest), 0.0)
        total = lax.optimization_barrier(jnp.sum(weights, axis=-1))
        rounded = weights.astype(jnp.bfloat16).astype(jnp.float32)
        context = jnp.einsum('tgjk,kgd->tgjd', rounded, values_all) / total[..., None]
        return context.astype(jnp.bfloat16).reshape(block, QH * HD)
    context = lax.map(one_block, jnp.arange(SUFFIX // block, dtype=jnp.int32)).reshape(SUFFIX, QH * HD)
    attn = jnp.dot(context, w_out, preferred_element_type=jnp.float32)
    middle = (hidden_in.astype(jnp.float32) + attn).astype(jnp.bfloat16)
    moe_in = rms_norm(middle, moe_gain).astype(jnp.bfloat16)
    flat_ids = routes.reshape(-1)
    flat_weights = route_weights.reshape(-1)
    limit = min(SUFFIX * TOPK, SUFFIX // MOE_ROWS * CAP)

    def expert_step(expert, mixed):
        hit = flat_ids == expert
        order = jnp.argsort(jnp.where(hit, 0, 1).astype(jnp.int32), stable=True)[:limit].astype(jnp.int32)
        token_rows = (order // TOPK).astype(jnp.int32)
        rows = moe_in[token_rows]
        summed = jnp.zeros((limit, D), jnp.float32)
        for side in range(2):
            gate_up = lax.dynamic_index_in_dim(w_gateup, (2 * expert + side).astype(jnp.int32), 0, keepdims=False)
            down = lax.dynamic_index_in_dim(w_down, (2 * expert + side).astype(jnp.int32), 0, keepdims=False)
            both = jnp.dot(rows, gate_up, preferred_element_type=jnp.float32)
            hidden = (jax.nn.relu(both[:, :FF_HALF]) * both[:, FF_HALF:]).astype(jnp.bfloat16)
            summed = summed + jnp.dot(hidden, down, preferred_element_type=jnp.float32)
        output = summed.astype(jnp.bfloat16).astype(jnp.float32)
        coeff = jnp.where(hit[order], flat_weights[order], 0.0)
        return mixed.at[token_rows].add(coeff[:, None] * output)
    mixed = lax.fori_loop(0, EXPERTS, expert_step, jnp.zeros((SUFFIX, D), jnp.float32))
    return (middle.astype(jnp.float32) + mixed).astype(jnp.bfloat16)
```

```python
import functools
import jax
import jax.numpy as jnp
from jax import lax
from jax.experimental import pallas as pl
from jax.experimental.pallas import tpu as pltpu
from jax.sharding import PartitionSpec as P

KVH = 2
HD = 128
TOPK = 4


def passed_along(value, axis, by):
    devices = lax.axis_size(axis)
    pairs = [(i, i + by) for i in range(devices) if 0 <= i + by < devices]
    return lax.ppermute(value, axis, pairs)


def rms_norm(values, gain):
    wide = values.astype(jnp.float32)
    return wide * lax.rsqrt(jnp.mean(wide * wide, axis=-1, keepdims=True) + 1e-05) * gain


def rotate(vectors, positions):
    half = vectors.shape[-1] // 2
    freqs = 10000.0 ** (-2.0 * jnp.arange(half, dtype=jnp.float32) / vectors.shape[-1])
    angle = positions[:, None] * freqs[None, :]
    cosine = jnp.cos(angle)[:, None, :]
    sine = jnp.sin(angle)[:, None, :]
    first = vectors[..., :half]
    second = vectors[..., half:]
    return jnp.concatenate(
        [first * cosine - second * sine, second * cosine + first * sine], axis=-1
    )


def request_info(index, lengths):
    ends = jnp.cumsum(lengths)
    seg = jnp.sum((index[:, None] >= ends[None, :]).astype(jnp.int32), axis=1)
    starts = ends - lengths
    count = lengths.shape[0]
    begin = jnp.sum(
        jnp.where(seg[:, None] == jnp.arange(count, dtype=jnp.int32)[None, :], starts[None, :], 0),
        axis=1,
    )
    return (seg, index - begin)


def matmul(left, right):
    return jnp.dot(left, right, preferred_element_type=jnp.float32)


def attend(state, queries, piece, valid):
    best, total, accum = state
    keys = piece[:, :HD]
    values = piece[:, HD:]
    scores = lax.dot_general(
        queries, keys, (((1,), (1,)), ((), ())), preferred_element_type=jnp.float32
    )
    if valid is not None:
        scores = jnp.where(valid, scores, -1e30)
    new_best = jnp.maximum(best, jnp.max(scores, axis=1))
    weights = jnp.exp(scores - new_best[:, None])
    if valid is not None:
        weights = jnp.where(valid, weights, 0.0)
    rescale = jnp.exp(best - new_best)
    total = total * rescale + jnp.sum(weights, axis=1)
    accum = accum * rescale[:, None] + matmul(weights.astype(jnp.bfloat16), values)
    return (new_best, total, accum)


def attend_blocks(state, queries, piece, key_start, masker):
    count = piece.shape[0]
    width = 2048 if count > 2048 and count % 2048 == 0 else count

    def one_part(number, current):
        part = lax.dynamic_slice_in_dim(piece, number * width, width, 0)
        valid = masker(key_start + number * width, width) if masker is not None else None
        return attend(current, queries, part, valid)

    if width == count:
        return one_part(0, state)
    return lax.fori_loop(0, count // width, one_part, state)


MESH = pl.DeviceIdType.MESH
CORES = 2
ROWS_BLOCK = 64
PIECE = 16
ORDER = (0, 7, 1, 6, 2, 5, 3, 4)
PLACE = {rel: at for at, rel in enumerate(ORDER)}


def moe_kernel(
    sizes,
    mid_ref,
    gain_ref,
    routes_ref,
    weights_ref,
    gateup_ref,
    down_ref,
    out_ref,
    tokens,
    table,
    tables,
    packed,
    rows,
    outs,
    backs,
    gate_up,
    down,
    partial,
    sums_r,
    sums_l,
    got_r,
    got_l,
    final,
    landed,
    local_sem,
    wsend,
    wrecv,
    tsend,
    trecv,
    zsend,
    zrecv,
    ysend,
    yrecv,
    bsend,
    brecv,
    ssend,
    srecv,
    xsend,
    xrecv,
):
    xs, ys, zs = sizes
    head = lax.axis_index("head")
    blk = lax.axis_index("blk")
    core = blk % CORES
    z = (blk // CORES) % zs
    y = blk // (CORES * zs)
    width = mid_ref.shape[1]
    half_units = down.shape[1]
    chunk = ROWS_BLOCK // 2

    def at(dx=0, dy=0, dz=0, other=False):
        hx = (head + dx) % xs
        yy = (y + dy) % ys
        zz = (z + dz) % zs
        cc = 1 - core if other else core
        return (hx, (yy * zs + zz) * CORES + cc)

    peers = (
        [at(other=True)]
        + [at(dz=d) for d in range(1, zs)]
        + [at(dy=d) for d in range(1, ys)]
        + [at(dx=d) for d in range(1, xs)]
    )
    barrier = pltpu.get_barrier_semaphore()
    for peer in peers:
        pl.semaphore_signal(barrier, inc=1, device_id=peer, device_id_type=MESH)

    own_copies = [
        pltpu.make_async_copy(gateup_ref.at[0], gate_up.at[0], local_sem.at[0]),
        pltpu.make_async_copy(down_ref.at[0], down.at[0], local_sem.at[1]),
    ]
    for copy in own_copies:
        copy.start()
    wide = mid_ref[...].astype(jnp.float32)
    scale = lax.rsqrt(jnp.mean(wide * wide, axis=-1, keepdims=True) + 1e-05)
    tokens[0] = (wide * scale * gain_ref[...]).astype(jnp.bfloat16)
    lanes = routes_ref.shape[1]
    row = lax.broadcasted_iota(jnp.int32, (zs * 2 * ys, lanes), 0)
    part = row % (2 * ys)
    expert = ((y + part % ys) % ys) * zs + row // (2 * ys)
    hit = jnp.zeros((zs * 2 * ys, lanes), jnp.float32)
    weight = jnp.zeros((zs * 2 * ys, lanes), jnp.float32)
    for k in range(routes_ref.shape[0]):
        same = routes_ref[k : k + 1, :] == expert
        hit = hit + jnp.where(same, 1.0, 0.0)
        weight = weight + jnp.where(same, weights_ref[k : k + 1, :], 0.0)
    before = jnp.where(
        lax.broadcasted_iota(jnp.int32, (lanes, lanes), 0)
        < lax.broadcasted_iota(jnp.int32, (lanes, lanes), 1),
        1.0,
        0.0,
    )
    rank = jnp.dot(
        hit.astype(jnp.bfloat16),
        before.astype(jnp.bfloat16),
        preferred_element_type=jnp.float32,
    )
    code = jnp.where(hit > 0.5, rank, -1.0)
    table[...] = jnp.where(part < ys, code, weight).reshape(zs, 2 * ys, lanes)
    pl.semaphore_wait(barrier, len(peers))

    table_copies = {}
    for d in range(1, zs):
        table_copies[d] = pltpu.make_async_remote_copy(
            src_ref=table.at[(z + d) % zs],
            dst_ref=tables.at[PLACE[zs - d]],
            send_sem=tsend.at[d],
            recv_sem=trecv.at[zs - d],
            device_id=at(dz=d),
            device_id_type=MESH,
        )
        table_copies[d].start()

    def token_copy(direction, step, piece):
        held = (-step * direction) % zs
        there = (held - direction) % zs
        number = step * 2 + piece
        side = 0 if direction == 1 else 1
        return pltpu.make_async_remote_copy(
            src_ref=tokens.at[PLACE[held], pl.ds(piece * chunk, chunk)],
            dst_ref=tokens.at[PLACE[there], pl.ds(piece * chunk, chunk)],
            send_sem=zsend.at[side, number],
            recv_sem=zrecv.at[side, number],
            device_id=at(dz=direction),
            device_id_type=MESH,
        )

    reach = zs // 2
    flow = {}
    for direction in (1, -1):
        for step in range(reach):
            for piece in range(2):
                if step < reach - 1 or piece == (0 if direction == 1 else 1):
                    flow[direction, step, piece] = token_copy(direction, step, piece)

    for piece in range(2):
        flow[1, 0, piece].start()
        flow[-1, 0, piece].start()

    weight_copies = [
        pltpu.make_async_remote_copy(
            src_ref=gateup_ref.at[0],
            dst_ref=gate_up.at[1],
            send_sem=wsend.at[0],
            recv_sem=wrecv.at[0],
            device_id=at(other=True),
            device_id_type=MESH,
        ),
        pltpu.make_async_remote_copy(
            src_ref=down_ref.at[0],
            dst_ref=down.at[1],
            send_sem=wsend.at[1],
            recv_sem=wrecv.at[1],
            device_id=at(other=True),
            device_id_type=MESH,
        ),
    ]
    for copy in weight_copies:
        copy.start()

    slot = lax.broadcasted_iota(jnp.int32, (ys * PIECE, lanes), 0) % PIECE
    slot = slot.astype(jnp.float32)

    def spread(place, first):
        return jnp.concatenate(
            [
                jnp.broadcast_to(tables[place, first + dy : first + dy + 1, :], (PIECE, lanes))
                for dy in range(ys)
            ],
            axis=0,
        )

    def piece_copy(place, dy):
        return pltpu.make_async_remote_copy(
            src_ref=packed.at[place, dy],
            dst_ref=rows.at[place, ys - dy],
            send_sem=ysend.at[place, dy],
            recv_sem=yrecv.at[place, ys - dy],
            device_id=at(dy=dy),
            device_id_type=MESH,
        )

    def back_copy(place, dy):
        return pltpu.make_async_remote_copy(
            src_ref=outs.at[place, dy],
            dst_ref=backs.at[place, ys - dy],
            send_sem=bsend.at[place, dy],
            recv_sem=brecv.at[place, ys - dy],
            device_id=at(dy=dy),
            device_id_type=MESH,
        )

    def arrival(make, sems, place, dy):
        copy = make(place, ys - dy)
        copy.wait_recv()

    def pack(place):
        if place > 0:
            table_copies[(zs - ORDER[place])].wait_recv()
        chosen = jnp.where(spread(place, 0) == slot, 1.0, 0.0).astype(jnp.bfloat16)
        value = jnp.dot(
            chosen[:, :ROWS_BLOCK], tokens[place], preferred_element_type=jnp.float32
        ).astype(jnp.bfloat16)
        value = value.reshape(ys, PIECE, width)
        packed[place, 1:] = value[1:]
        rows[place, 0] = value[0]
        for dy in (2, 1, 3):
            piece_copy(place, dy).start()

    def experts(first, count):
        for place in range(first, first + count):
            for dy in range(1, ys):
                arrival(piece_copy, yrecv, place, dy)
        taken = rows[first : first + count].reshape(count * ys * PIECE, width)
        total = None
        for side in range(2):
            both = jnp.dot(taken, gate_up[side], preferred_element_type=jnp.float32)
            hidden = jax.nn.relu(both[:, :half_units]) * both[:, half_units:]
            term = jnp.dot(
                hidden.astype(jnp.bfloat16), down[side], preferred_element_type=jnp.float32
            )
            total = term if total is None else total + term
        value = total.astype(jnp.bfloat16).reshape(count, ys, PIECE, width)
        outs[first : first + count, 1:] = value[:, 1:]
        backs[first : first + count, 0] = value[:, 0]
        for place in range(first, first + count):
            for dy in (2, 1, 3):
                back_copy(place, dy).start()

    def combine(place):
        for dy in range(1, ys):
            arrival(back_copy, brecv, place, dy)
        mixing = jnp.where(spread(place, 0) == slot, spread(place, ys), 0.0)
        mixing = mixing.astype(jnp.bfloat16)[:, :ROWS_BLOCK]
        partial[place] = lax.dot_general(
            mixing,
            backs[place].reshape(ys * PIECE, width),
            (((0,), (0,)), ((), ())),
            preferred_element_type=jnp.float32,
        )

    tables[0] = table[z]
    pack(0)
    for step in range(1, reach + 1):
        for piece in range(2):
            for direction in (1, -1):
                if (direction, step - 1, piece) in flow:
                    flow[direction, step - 1, piece].wait_recv()
                if (direction, step, piece) in flow:
                    flow[direction, step, piece].start()
        if step < reach:
            pack(PLACE[zs - step])
            pack(PLACE[step])
        else:
            pack(PLACE[reach])
        if step == 1:
            for copy in own_copies:
                copy.wait()
            for copy in weight_copies:
                copy.wait_recv()
            experts(0, 1)
        else:
            experts(PLACE[zs - step + 1], 2)
    experts(PLACE[reach], 1)
    for place in range(5):
        combine(place)

    def sum_copy(direction, held, piece):
        side = 0 if direction == 1 else 1
        number = (held if direction == 1 else zs - held) * 2 + piece
        source, target = (sums_r, got_r) if direction == 1 else (sums_l, got_l)
        return pltpu.make_async_remote_copy(
            src_ref=source.at[number],
            dst_ref=target.at[number],
            send_sem=ssend.at[side, number],
            recv_sem=srecv.at[side, number],
            device_id=at(dz=direction),
            device_id_type=MESH,
        )

    returned = {}

    def pass_on(direction, distance, piece):
        held = distance if direction == 1 else zs - distance
        number = distance * 2 + piece
        value = partial[PLACE[held], pl.ds(piece * chunk, chunk)]
        source, target = (sums_r, got_r) if direction == 1 else (sums_l, got_l)
        if (direction, distance + 1, piece) in returned:
            returned[direction, distance + 1, piece].wait_recv()
            value = value + target[number + 2].astype(jnp.float32)
        source[number] = value.astype(jnp.bfloat16)
        copy = sum_copy(direction, held, piece)
        returned[direction, distance, piece] = copy
        copy.start()

    combine(PLACE[reach - 1])
    pass_on(1, reach - 1, 1)
    combine(PLACE[zs - reach + 1])
    pass_on(-1, reach - 1, 0)
    combine(PLACE[reach])
    pass_on(1, reach, 0)
    pass_on(-1, reach, 1)
    for distance in range(reach - 1, 0, -1):
        if distance < reach - 1:
            pass_on(1, distance, 1)
            pass_on(-1, distance, 0)
        pass_on(1, distance, 0)
        pass_on(-1, distance, 1)
    for piece in (1, 0):
        spot = pl.ds(piece * chunk, chunk)
        returned[1, 1, piece].wait_recv()
        returned[-1, 1, piece].wait_recv()
        value = (
            mid_ref[spot].astype(jnp.float32)
            + partial[0, spot]
            + got_r[2 + piece].astype(jnp.float32)
            + got_l[2 + piece].astype(jnp.float32)
        ).astype(jnp.bfloat16)
        share = width // xs
        for part_x in range(xs):
            final[part_x, spot] = value[:, part_x * share : (part_x + 1) * share]

    last = []
    for dx in range(1, xs):
        copy = pltpu.make_async_remote_copy(
            src_ref=final.at[(head + dx) % xs],
            dst_ref=landed.at[head],
            send_sem=xsend.at[dx],
            recv_sem=xrecv.at[xs - dx],
            device_id=at(dx=dx),
            device_id_type=MESH,
        )
        copy.start()
        last.append(copy)
    out_ref[head] = final[head]
    for dx in range(1, xs):
        last[xs - dx - 1].wait_recv()
        out_ref[(head + dx) % xs] = landed[(head + dx) % xs]

    for copy in weight_copies + list(table_copies.values()) + list(flow.values()):
        copy.wait_send()
    for place in range(zs):
        for dy in range(1, ys):
            piece_copy(place, dy).wait_send()
            back_copy(place, dy).wait_send()
    for copy in list(returned.values()) + last:
        copy.wait_send()


def moe(sizes, middle, gain, routes, weights, w_gateup, w_down):
    xs, ys, zs = sizes
    count, width = middle.shape
    lanes = 128
    routes_t = jnp.pad(routes, ((0, lanes - count), (0, 0)), constant_values=-1).T
    weights_t = jnp.pad(weights, ((0, lanes - count), (0, 0))).T
    bf16, f32 = jnp.bfloat16, jnp.float32
    dma = pltpu.SemaphoreType.DMA
    vmem = pl.BlockSpec(memory_space=pltpu.VMEM)
    hbm = pl.BlockSpec(memory_space=pl.ANY)
    out = pl.pallas_call(
        functools.partial(moe_kernel, sizes),
        out_shape=jax.ShapeDtypeStruct((xs, count, width // xs), bf16),
        in_specs=[vmem, vmem, vmem, vmem, hbm, hbm],
        out_specs=vmem,
        scratch_shapes=[
            pltpu.VMEM((zs, count, width), bf16),
            pltpu.VMEM((zs, 2 * ys, lanes), f32),
            pltpu.VMEM((zs, 2 * ys, lanes), f32),
            pltpu.VMEM((zs, ys, PIECE, width), bf16),
            pltpu.VMEM((zs, ys, PIECE, width), bf16),
            pltpu.VMEM((zs, ys, PIECE, width), bf16),
            pltpu.VMEM((zs, ys, PIECE, width), bf16),
            pltpu.VMEM((2,) + w_gateup.shape[1:], bf16),
            pltpu.VMEM((2,) + w_down.shape[1:], bf16),
            pltpu.VMEM((zs, count, width), f32),
            pltpu.VMEM((zs + 2, count // 2, width), bf16),
            pltpu.VMEM((zs + 2, count // 2, width), bf16),
            pltpu.VMEM((zs + 2, count // 2, width), bf16),
            pltpu.VMEM((zs + 2, count // 2, width), bf16),
            pltpu.VMEM((xs, count, width // xs), bf16),
            pltpu.VMEM((xs, count, width // xs), bf16),
            dma((2,)),
            dma((2,)),
            dma((2,)),
            dma((zs,)),
            dma((zs,)),
            dma((2, zs)),
            dma((2, zs)),
            dma((zs, ys)),
            dma((zs, ys)),
            dma((zs, ys)),
            dma((zs, ys)),
            dma((2, zs + 2)),
            dma((2, zs + 2)),
            dma((xs,)),
            dma((xs,)),
        ],
        compiler_params=pltpu.CompilerParams(
            collective_id=1, has_side_effects=True, vmem_limit_bytes=60 * 2**20
        ),
    )(middle, gain.reshape(1, width), routes_t, weights_t, w_gateup, w_down)
    return out.reshape(xs * count, width // xs)


def shards(
    hidden_in,
    attn_gain,
    w_query,
    w_keyval,
    prefix_cache,
    w_out,
    moe_gain,
    w_gateup,
    w_down,
    routes,
    route_weights,
    lengths,
):
    tok_rows = hidden_in.shape[0]
    head_index = lax.axis_index("head")
    block_index = lax.axis_index("blk")
    head_count = lax.axis_size("head")
    block_count = lax.axis_size("blk")
    local_heads = w_query.shape[1] // HD
    kv_head = head_index // (head_count // KVH)
    prefix_total = prefix_cache.shape[0] * block_count
    normed = rms_norm(hidden_in, attn_gain).astype(jnp.bfloat16)
    token_index = block_index * tok_rows + jnp.arange(tok_rows, dtype=jnp.int32)
    seg_query, offset_query = request_info(token_index, lengths)
    positions = (prefix_total + offset_query).astype(jnp.float32)
    queries = matmul(normed, w_query).reshape(tok_rows, local_heads, HD)
    queries = (
        (rotate(queries, positions) * HD ** (-0.5))
        .astype(jnp.bfloat16)
        .reshape(tok_rows * local_heads, HD)
    )
    own_weights = lax.dynamic_index_in_dim(w_keyval, kv_head, 0, keepdims=False)
    keyval = matmul(normed, own_weights)
    new_keys = rotate(keyval[:, None, :HD], positions)[:, 0, :]
    own_block = jnp.concatenate([new_keys, keyval[:, HD:]], axis=1).astype(jnp.bfloat16)
    cached = lax.dynamic_index_in_dim(prefix_cache, kv_head, 1, keepdims=False)
    row_index = jnp.repeat(token_index, local_heads)
    row_seg = jnp.repeat(seg_query, local_heads)
    row_total = tok_rows * local_heads

    def suffix_mask(key_start, count):
        key_index = key_start + jnp.arange(count, dtype=jnp.int32)
        key_seg, unused = request_info(key_index, lengths)
        return (
            (row_seg[:, None] == key_seg[None, :])
            & (key_index[None, :] <= row_index[:, None])
            & (key_index[None, :] >= 0)
        )

    state = (
        jnp.full((row_total,), -1e30, jnp.float32),
        jnp.zeros((row_total,), jnp.float32),
        jnp.zeros((row_total, HD), jnp.float32),
    )
    state = attend_blocks(
        state, queries, lax.all_gather(cached, "blk", axis=0, tiled=True), jnp.int32(0), None
    )
    state = attend_blocks(state, queries, own_block, block_index * tok_rows, suffix_mask)
    travelling = own_block
    reach = min(8, block_count // 2)
    for distance in range(reach):
        travelling = passed_along(travelling, "blk", 1)
        state = attend_blocks(
            state, queries, travelling, (block_index - distance - 1) * tok_rows, suffix_mask
        )
    best, total, accum = state
    context = (accum / total[:, None]).astype(jnp.bfloat16).reshape(tok_rows, local_heads * HD)
    quarter = tok_rows // head_count
    attn_share = lax.psum_scatter(
        matmul(context, w_out).astype(jnp.bfloat16), "head", scatter_dimension=0, tiled=True
    ).astype(jnp.float32)
    resid = lax.dynamic_slice_in_dim(hidden_in, head_index * quarter, quarter, 0)
    middle = (resid.astype(jnp.float32) + attn_share).astype(jnp.bfloat16)
    my_routes = lax.dynamic_slice_in_dim(routes, head_index * quarter, quarter, 0)
    my_weights = lax.dynamic_slice_in_dim(route_weights, head_index * quarter, quarter, 0)
    chips_z = 8
    sizes = (head_count, block_count // (CORES * chips_z), chips_z)
    return moe(sizes, middle, moe_gain, my_routes, my_weights, w_gateup, w_down)


def solution(mesh):
    return jax.shard_map(
        shards,
        mesh=mesh,
        in_specs=(
            P("blk", None),
            P(),
            P(None, "head"),
            P(),
            P("blk", None, None),
            P("head", None),
            P(),
            P("blk", None, None),
            P("blk", None, None),
            P("blk", None),
            P("blk", None),
            P(),
        ),
        out_specs=P("blk", "head"),
        check_vma=False,
    )
```

```python
import functools
import jax
import jax.numpy as jnp
import numpy as np
from jax import lax
from jax.experimental import pallas as pl
from jax.experimental.pallas import tpu as pltpu
from jax.sharding import PartitionSpec as P

KVH = 2
HD = 128


MESH = pl.DeviceIdType.MESH
CORES = 2
ROWS_BLOCK = 64
PIECE = 16
ORDER = (0, 7, 1, 6, 2, 5, 3, 4)
PLACE = {rel: at for at, rel in enumerate(ORDER)}


def moe_kernel(
    sizes,
    mid_ref,
    gain_ref,
    routes_ref,
    weights_ref,
    gateup_ref,
    down_ref,
    out_ref,
    tokens,
    table,
    tables,
    packed,
    rows,
    outs,
    backs,
    gate_up,
    down,
    partial,
    sums_r,
    sums_l,
    got_r,
    got_l,
    final,
    landed,
    local_sem,
    wsend,
    wrecv,
    tsend,
    trecv,
    zsend,
    zrecv,
    ysend,
    yrecv,
    bsend,
    brecv,
    ssend,
    srecv,
    xsend,
    xrecv,
):
    xs, ys, zs = sizes
    head = lax.axis_index("head")
    blk = lax.axis_index("blk")
    core = blk % CORES
    z = (blk // CORES) % zs
    y = blk // (CORES * zs)
    width = mid_ref.shape[1]
    half_units = down.shape[1]
    chunk = ROWS_BLOCK // 2

    def at(dx=0, dy=0, dz=0, other=False):
        hx = (head + dx) % xs
        yy = (y + dy) % ys
        zz = (z + dz) % zs
        cc = 1 - core if other else core
        return (hx, (yy * zs + zz) * CORES + cc)

    peers = (
        [at(other=True)]
        + [at(dz=d) for d in range(1, zs)]
        + [at(dy=d) for d in range(1, ys)]
        + [at(dx=d) for d in range(1, xs)]
    )
    barrier = pltpu.get_barrier_semaphore()
    for peer in peers:
        pl.semaphore_signal(barrier, inc=1, device_id=peer, device_id_type=MESH)

    own_copies = [
        pltpu.make_async_copy(gateup_ref.at[0], gate_up.at[0], local_sem.at[0]),
        pltpu.make_async_copy(down_ref.at[0], down.at[0], local_sem.at[1]),
    ]
    for copy in own_copies:
        copy.start()
    wide = mid_ref[...].astype(jnp.float32)
    scale = lax.rsqrt(jnp.mean(wide * wide, axis=-1, keepdims=True) + 1e-05)
    tokens[0] = (wide * scale * gain_ref[...]).astype(jnp.bfloat16)
    lanes = routes_ref.shape[1]
    row = lax.broadcasted_iota(jnp.int32, (zs * 2 * ys, lanes), 0)
    part = row % (2 * ys)
    expert = ((y + part % ys) % ys) * zs + row // (2 * ys)
    hit = jnp.zeros((zs * 2 * ys, lanes), jnp.float32)
    weight = jnp.zeros((zs * 2 * ys, lanes), jnp.float32)
    for k in range(routes_ref.shape[0]):
        same = routes_ref[k : k + 1, :] == expert
        hit = hit + jnp.where(same, 1.0, 0.0)
        weight = weight + jnp.where(same, weights_ref[k : k + 1, :], 0.0)
    before = jnp.where(
        lax.broadcasted_iota(jnp.int32, (lanes, lanes), 0)
        < lax.broadcasted_iota(jnp.int32, (lanes, lanes), 1),
        1.0,
        0.0,
    )
    rank = jnp.dot(
        hit.astype(jnp.bfloat16),
        before.astype(jnp.bfloat16),
        preferred_element_type=jnp.float32,
    )
    code = jnp.where(hit > 0.5, rank, -1.0)
    table[...] = jnp.where(part < ys, code, weight).reshape(zs, 2 * ys, lanes)
    pl.semaphore_wait(barrier, len(peers))

    table_copies = {}
    for d in range(1, zs):
        table_copies[d] = pltpu.make_async_remote_copy(
            src_ref=table.at[(z + d) % zs],
            dst_ref=tables.at[PLACE[zs - d]],
            send_sem=tsend.at[d],
            recv_sem=trecv.at[zs - d],
            device_id=at(dz=d),
            device_id_type=MESH,
        )
        table_copies[d].start()

    def token_copy(direction, step, piece):
        held = (-step * direction) % zs
        there = (held - direction) % zs
        number = step * 2 + piece
        side = 0 if direction == 1 else 1
        return pltpu.make_async_remote_copy(
            src_ref=tokens.at[PLACE[held], pl.ds(piece * chunk, chunk)],
            dst_ref=tokens.at[PLACE[there], pl.ds(piece * chunk, chunk)],
            send_sem=zsend.at[side, number],
            recv_sem=zrecv.at[side, number],
            device_id=at(dz=direction),
            device_id_type=MESH,
        )

    reach = zs // 2
    flow = {}
    for direction in (1, -1):
        for step in range(reach):
            for piece in range(2):
                if step < reach - 1 or piece == (0 if direction == 1 else 1):
                    flow[direction, step, piece] = token_copy(direction, step, piece)

    for piece in range(2):
        flow[1, 0, piece].start()
        flow[-1, 0, piece].start()

    weight_copies = [
        pltpu.make_async_remote_copy(
            src_ref=gateup_ref.at[0],
            dst_ref=gate_up.at[1],
            send_sem=wsend.at[0],
            recv_sem=wrecv.at[0],
            device_id=at(other=True),
            device_id_type=MESH,
        ),
        pltpu.make_async_remote_copy(
            src_ref=down_ref.at[0],
            dst_ref=down.at[1],
            send_sem=wsend.at[1],
            recv_sem=wrecv.at[1],
            device_id=at(other=True),
            device_id_type=MESH,
        ),
    ]
    for copy in weight_copies:
        copy.start()

    slot = lax.broadcasted_iota(jnp.int32, (ys * PIECE, lanes), 0) % PIECE
    slot = slot.astype(jnp.float32)

    def spread(place, first):
        return jnp.concatenate(
            [
                jnp.broadcast_to(tables[place, first + dy : first + dy + 1, :], (PIECE, lanes))
                for dy in range(ys)
            ],
            axis=0,
        )

    def piece_copy(place, dy):
        return pltpu.make_async_remote_copy(
            src_ref=packed.at[place, dy],
            dst_ref=rows.at[place, ys - dy],
            send_sem=ysend.at[place, dy],
            recv_sem=yrecv.at[place, ys - dy],
            device_id=at(dy=dy),
            device_id_type=MESH,
        )

    def back_copy(place, dy):
        return pltpu.make_async_remote_copy(
            src_ref=outs.at[place, dy],
            dst_ref=backs.at[place, ys - dy],
            send_sem=bsend.at[place, dy],
            recv_sem=brecv.at[place, ys - dy],
            device_id=at(dy=dy),
            device_id_type=MESH,
        )

    def arrival(make, sems, place, dy):
        copy = make(place, ys - dy)
        copy.wait_recv()

    def pack(place):
        if place > 0:
            table_copies[(zs - ORDER[place])].wait_recv()
        chosen = jnp.where(spread(place, 0) == slot, 1.0, 0.0).astype(jnp.bfloat16)
        value = jnp.dot(
            chosen[:, :ROWS_BLOCK], tokens[place], preferred_element_type=jnp.float32
        ).astype(jnp.bfloat16)
        value = value.reshape(ys, PIECE, width)
        packed[place, 1:] = value[1:]
        rows[place, 0] = value[0]
        for dy in (2, 1, 3):
            piece_copy(place, dy).start()

    def experts(first, count):
        for place in range(first, first + count):
            for dy in range(1, ys):
                arrival(piece_copy, yrecv, place, dy)
        taken = rows[first : first + count].reshape(count * ys * PIECE, width)
        total = None
        for side in range(2):
            both = jnp.dot(taken, gate_up[side], preferred_element_type=jnp.float32)
            hidden = jax.nn.relu(both[:, :half_units]) * both[:, half_units:]
            term = jnp.dot(
                hidden.astype(jnp.bfloat16), down[side], preferred_element_type=jnp.float32
            )
            total = term if total is None else total + term
        value = total.astype(jnp.bfloat16).reshape(count, ys, PIECE, width)
        outs[first : first + count, 1:] = value[:, 1:]
        backs[first : first + count, 0] = value[:, 0]
        for place in range(first, first + count):
            for dy in (2, 1, 3):
                back_copy(place, dy).start()

    def combine(place):
        for dy in range(1, ys):
            arrival(back_copy, brecv, place, dy)
        mixing = jnp.where(spread(place, 0) == slot, spread(place, ys), 0.0)
        mixing = mixing.astype(jnp.bfloat16)[:, :ROWS_BLOCK]
        partial[place] = lax.dot_general(
            mixing,
            backs[place].reshape(ys * PIECE, width),
            (((0,), (0,)), ((), ())),
            preferred_element_type=jnp.float32,
        )

    tables[0] = table[z]
    pack(0)
    for step in range(1, reach + 1):
        for piece in range(2):
            for direction in (1, -1):
                if (direction, step - 1, piece) in flow:
                    flow[direction, step - 1, piece].wait_recv()
                if (direction, step, piece) in flow:
                    flow[direction, step, piece].start()
        if step < reach:
            pack(PLACE[zs - step])
            pack(PLACE[step])
        else:
            pack(PLACE[reach])
        if step == 1:
            for copy in own_copies:
                copy.wait()
            for copy in weight_copies:
                copy.wait_recv()
            experts(0, 1)
        else:
            experts(PLACE[zs - step + 1], 2)
    experts(PLACE[reach], 1)
    for place in range(5):
        combine(place)

    def sum_copy(direction, held, piece):
        side = 0 if direction == 1 else 1
        number = (held if direction == 1 else zs - held) * 2 + piece
        source, target = (sums_r, got_r) if direction == 1 else (sums_l, got_l)
        return pltpu.make_async_remote_copy(
            src_ref=source.at[number],
            dst_ref=target.at[number],
            send_sem=ssend.at[side, number],
            recv_sem=srecv.at[side, number],
            device_id=at(dz=direction),
            device_id_type=MESH,
        )

    returned = {}

    def pass_on(direction, distance, piece):
        held = distance if direction == 1 else zs - distance
        number = distance * 2 + piece
        value = partial[PLACE[held], pl.ds(piece * chunk, chunk)]
        source, target = (sums_r, got_r) if direction == 1 else (sums_l, got_l)
        if (direction, distance + 1, piece) in returned:
            returned[direction, distance + 1, piece].wait_recv()
            value = value + target[number + 2].astype(jnp.float32)
        source[number] = value.astype(jnp.bfloat16)
        copy = sum_copy(direction, held, piece)
        returned[direction, distance, piece] = copy
        copy.start()

    combine(PLACE[reach - 1])
    pass_on(1, reach - 1, 1)
    combine(PLACE[zs - reach + 1])
    pass_on(-1, reach - 1, 0)
    combine(PLACE[reach])
    pass_on(1, reach, 0)
    pass_on(-1, reach, 1)
    for distance in range(reach - 1, 0, -1):
        if distance < reach - 1:
            pass_on(1, distance, 1)
            pass_on(-1, distance, 0)
        pass_on(1, distance, 0)
        pass_on(-1, distance, 1)
    for piece in (1, 0):
        spot = pl.ds(piece * chunk, chunk)
        returned[1, 1, piece].wait_recv()
        returned[-1, 1, piece].wait_recv()
        value = (
            mid_ref[spot].astype(jnp.float32)
            + partial[0, spot]
            + got_r[2 + piece].astype(jnp.float32)
            + got_l[2 + piece].astype(jnp.float32)
        ).astype(jnp.bfloat16)
        share = width // xs
        for part_x in range(xs):
            final[part_x, spot] = value[:, part_x * share : (part_x + 1) * share]

    last = []
    for dx in range(1, xs):
        copy = pltpu.make_async_remote_copy(
            src_ref=final.at[(head + dx) % xs],
            dst_ref=landed.at[head],
            send_sem=xsend.at[dx],
            recv_sem=xrecv.at[xs - dx],
            device_id=at(dx=dx),
            device_id_type=MESH,
        )
        copy.start()
        last.append(copy)
    out_ref[head] = final[head]
    for dx in range(1, xs):
        last[xs - dx - 1].wait_recv()
        out_ref[(head + dx) % xs] = landed[(head + dx) % xs]

    for copy in weight_copies + list(table_copies.values()) + list(flow.values()):
        copy.wait_send()
    for place in range(zs):
        for dy in range(1, ys):
            piece_copy(place, dy).wait_send()
            back_copy(place, dy).wait_send()
    for copy in list(returned.values()) + last:
        copy.wait_send()


def moe(sizes, middle, gain, routes, weights, w_gateup, w_down):
    xs, ys, zs = sizes
    count, width = middle.shape
    lanes = 128
    routes_t = jnp.pad(routes, ((0, lanes - count), (0, 0)), constant_values=-1).T
    weights_t = jnp.pad(weights, ((0, lanes - count), (0, 0))).T
    bf16, f32 = jnp.bfloat16, jnp.float32
    dma = pltpu.SemaphoreType.DMA
    vmem = pl.BlockSpec(memory_space=pltpu.VMEM)
    hbm = pl.BlockSpec(memory_space=pl.ANY)
    out = pl.pallas_call(
        functools.partial(moe_kernel, sizes),
        out_shape=jax.ShapeDtypeStruct((xs, count, width // xs), bf16),
        in_specs=[vmem, vmem, vmem, vmem, hbm, hbm],
        out_specs=vmem,
        scratch_shapes=[
            pltpu.VMEM((zs, count, width), bf16),
            pltpu.VMEM((zs, 2 * ys, lanes), f32),
            pltpu.VMEM((zs, 2 * ys, lanes), f32),
            pltpu.VMEM((zs, ys, PIECE, width), bf16),
            pltpu.VMEM((zs, ys, PIECE, width), bf16),
            pltpu.VMEM((zs, ys, PIECE, width), bf16),
            pltpu.VMEM((zs, ys, PIECE, width), bf16),
            pltpu.VMEM((2,) + w_gateup.shape[1:], bf16),
            pltpu.VMEM((2,) + w_down.shape[1:], bf16),
            pltpu.VMEM((zs, count, width), f32),
            pltpu.VMEM((zs + 2, count // 2, width), bf16),
            pltpu.VMEM((zs + 2, count // 2, width), bf16),
            pltpu.VMEM((zs + 2, count // 2, width), bf16),
            pltpu.VMEM((zs + 2, count // 2, width), bf16),
            pltpu.VMEM((xs, count, width // xs), bf16),
            pltpu.VMEM((xs, count, width // xs), bf16),
            dma((2,)),
            dma((2,)),
            dma((2,)),
            dma((zs,)),
            dma((zs,)),
            dma((2, zs)),
            dma((2, zs)),
            dma((zs, ys)),
            dma((zs, ys)),
            dma((zs, ys)),
            dma((zs, ys)),
            dma((2, zs + 2)),
            dma((2, zs + 2)),
            dma((xs,)),
            dma((xs,)),
        ],
        compiler_params=pltpu.CompilerParams(
            collective_id=1, has_side_effects=True, vmem_limit_bytes=60 * 2**20
        ),
    )(middle, gain.reshape(1, width), routes_t, weights_t, w_gateup, w_down)
    return out.reshape(xs * count, width // xs)


PAST = 4
SPLIT = 5


def attention_kernel(
    sizes,
    lengths_ref,
    hidden_ref,
    gain_ref,
    freqs_ref,
    w_query_ref,
    w_keyval_ref,
    prefix_ref,
    w_out_ref,
    mid_ref,
    w_kv,
    cached,
    fresh,
    out_weights,
    query,
    begin,
    best,
    total,
    accum,
    context,
    contexts,
    local_sem,
    pz_send,
    pz_recv,
    py_send,
    py_recv,
    pc_send,
    pc_recv,
    nz_send,
    nz_recv,
    nc_send,
    nc_recv,
    wx_send,
    wx_recv,
    wc_send,
    wc_recv,
    cx_send,
    cx_recv,
):
    xs, ys, zs = sizes
    head = lax.axis_index("head")
    blk = lax.axis_index("blk")
    core = blk % CORES
    chip = blk // CORES
    z = chip % zs
    y = chip // zs
    count, width = hidden_ref.shape
    heads = query.shape[0]
    part = count // xs
    half = w_out_ref.shape[0] // CORES

    def at(dx=0, dy=0, dz=0, other=False):
        cc = 1 - core if other else core
        return (
            (head + dx) % xs,
            (((y + dy) % ys) * zs + (z + dz) % zs) * CORES + cc,
        )

    def along(step):
        return (head, ((chip + step) % (ys * zs)) * CORES + core)

    peers = (
        [at(other=True), at(dz=1), at(dz=zs - 1), at(dy=1), at(dy=ys - 1)]
        + [at(dx=d) for d in range(1, xs)]
        + [along(1), along(ys * zs - 1)]
    )
    barrier = pltpu.get_barrier_semaphore()
    for peer in peers:
        pl.semaphore_signal(barrier, inc=1, device_id=peer, device_id_type=MESH)

    def remote(source, target, send, recv, device):
        return pltpu.make_async_remote_copy(
            src_ref=source,
            dst_ref=target,
            send_sem=send,
            recv_sem=recv,
            device_id=device,
            device_id_type=MESH,
        )

    kv_copy = pltpu.make_async_copy(w_keyval_ref.at[head // (xs // KVH)], w_kv, local_sem.at[0])
    kv_copy.start()
    out_copy = pltpu.make_async_copy(w_out_ref, out_weights.at[0], local_sem.at[1])
    out_copy.start()
    cached[0, 0, 0] = prefix_ref[...]
    pl.semaphore_wait(barrier, len(peers))

    sent = []

    def go(copy):
        copy.start()
        sent.append(copy)
        return copy

    def prefix_z(direction, step):
        held = (-step * direction) % zs
        there = (held - direction) % zs
        side = 0 if direction == 1 else 1
        return remote(
            cached.at[0, 0, PLACE[held]],
            cached.at[0, 0, PLACE[there]],
            pz_send.at[side, step],
            pz_recv.at[side, step],
            at(dz=direction),
        )

    batches = (pl.ds(0, SPLIT), pl.ds(SPLIT, zs - SPLIT))

    def prefix_y(held, direction, batch):
        there = (held - direction) % ys
        return remote(
            cached.at[0, held, batches[batch]],
            cached.at[0, there, batches[batch]],
            py_send.at[there, batch],
            py_recv.at[there, batch],
            at(dy=direction),
        )

    def prefix_core(held, batch):
        return remote(
            cached.at[0, held, batches[batch]],
            cached.at[1, held, batches[batch]],
            pc_send.at[held, batch],
            pc_recv.at[held, batch],
            at(other=True),
        )

    flow = {}
    flow[1, 0] = go(prefix_z(1, 0))
    flow[-1, 0] = go(prefix_z(-1, 0))

    mine = pl.ds(pl.multiple_of(core * half, 64), half)

    def weights_x(held, direction):
        there = (held - direction) % xs
        rows = mine
        if held != 0:
            offset = 0 if direction == 1 else half // 2
            rows = pl.ds(pl.multiple_of(core * half + offset, 32), half // 2)
        number = there if held == 0 else (0 if direction == 1 else 2)
        source = w_out_ref.at[rows] if held == 0 else out_weights.at[held, rows]
        return remote(
            source,
            out_weights.at[there, rows],
            wx_send.at[number],
            wx_recv.at[number],
            at(dx=direction),
        )

    def weights_core(held):
        return remote(
            out_weights.at[held, mine],
            out_weights.at[held, mine],
            wc_send.at[held],
            wc_recv.at[held],
            at(other=True),
        )

    go(weights_x(0, 1))
    go(weights_x(0, -1))

    token = blk * count + lax.broadcasted_iota(jnp.int32, (count, HD), 0)
    start = jnp.zeros((count, HD), jnp.int32)
    end = jnp.int32(0)
    for r in range(lengths_ref.shape[0]):
        end = end + lengths_ref[r]
        start = jnp.where(token >= end, end, start)
    begin[...] = start
    prefix_total = cached.shape[0] * ys * zs * prefix_ref.shape[0]
    angle = (prefix_total + token - start).astype(jnp.float32) * freqs_ref[...]
    cosine = jnp.cos(angle)
    sine = jnp.sin(angle)
    lane = lax.broadcasted_iota(jnp.int32, (count, HD), 1)
    sine = jnp.where(lane < HD // 2, -sine, sine)

    def turned(vectors):
        return vectors * cosine + pltpu.roll(vectors, HD // 2, 1) * sine

    wide = hidden_ref[...].astype(jnp.float32)
    scale = lax.rsqrt(jnp.mean(wide * wide, axis=-1, keepdims=True) + 1e-05)
    normed = (wide * scale * gain_ref[...]).astype(jnp.bfloat16)
    kv_copy.wait()
    keyval = jnp.dot(normed, w_kv[...], preferred_element_type=jnp.float32)
    fresh[0, 0, 0] = turned(keyval[:, :HD]).astype(jnp.bfloat16)
    fresh[0, 1, 0] = keyval[:, HD:].astype(jnp.bfloat16)

    def fresh_next(distance, kind):
        return remote(
            fresh.at[distance, kind, 0],
            fresh.at[distance + 1, kind, 0],
            nz_send.at[distance, kind],
            nz_recv.at[distance, kind],
            along(1),
        )

    def fresh_core(distance, kind):
        return remote(
            fresh.at[distance, kind, 0],
            fresh.at[distance, kind, 1],
            nc_send.at[distance, kind],
            nc_recv.at[distance, kind],
            at(other=True),
        )

    chain = {}
    shared = {}
    for kind in range(2):
        chain[0, kind] = go(fresh_next(0, kind))
    for kind in range(2):
        shared[0, kind] = go(fresh_core(0, kind))

    def prefix_step(step):
        for direction in (1, -1):
            if (direction, step - 1) in flow:
                flow[direction, step - 1].wait_recv()
            if step < zs // 2 - (0 if direction == 1 else 1):
                flow[direction, step] = go(prefix_z(direction, step))

    def fresh_step(distance):
        for kind in range(2):
            chain[distance - 1, kind].wait_recv()
            if distance < PAST:
                chain[distance, kind] = go(fresh_next(distance, kind))
            shared[distance, kind] = go(fresh_core(distance, kind))

    prefix_step(1)
    queries = jnp.dot(normed, w_query_ref[...], preferred_element_type=jnp.float32)
    for j in range(heads):
        query[j] = (turned(queries[:, j * HD : (j + 1) * HD]) * HD ** (-0.5)).astype(jnp.bfloat16)
    best[...] = jnp.full(best.shape, -1e30, jnp.float32)
    total[...] = jnp.zeros(total.shape, jnp.float32)
    accum[...] = jnp.zeros(accum.shape, jnp.float32)

    def attend(keys, values, distance=None):
        length = keys.shape[0]
        if distance is not None:
            place = lax.broadcasted_iota(jnp.int32, (1, length), 1)
            own_block = (blk - CORES * distance) * count
            other_block = (blk + 1 - 2 * core - CORES * distance) * count
            where = jnp.where(place < count, own_block + place, other_block + place - count)

        def one_head(j, carry):
            scores = lax.dot_general(
                query[j], keys, (((1,), (1,)), ((), ())), preferred_element_type=jnp.float32
            )
            if distance is not None:
                valid = where >= begin[:, :1]
                if distance == 0:
                    row = blk * count + lax.broadcasted_iota(jnp.int32, (count, 1), 0)
                    valid = valid & (where <= row)
                scores = jnp.where(valid, scores, -1e30)
            old = best[j]
            new = jnp.maximum(old, jnp.max(scores, axis=1, keepdims=True))
            weights = jnp.exp(scores - new[:, :1])
            rescale = jnp.exp(old - new)
            best[j] = new
            total[j] = total[j] * rescale + jnp.sum(weights, axis=1, keepdims=True)
            accum[j] = accum[j] * rescale + jnp.dot(
                weights.astype(jnp.bfloat16), values, preferred_element_type=jnp.float32
            )
            return carry

        lax.fori_loop(0, heads, one_head, 0)

    def attend_fresh(distance):
        for kind in range(2):
            shared[distance, kind].wait_recv()
        attend(
            fresh[distance, 0].reshape(CORES * count, HD),
            fresh[distance, 1].reshape(CORES * count, HD),
            distance,
        )

    def attend_cached(side, held):
        piece = cached[side, held].reshape(zs * prefix_ref.shape[0], 2 * HD)
        attend(piece[:, :HD], piece[:, HD:])

    ride = {}
    onchip = {}

    def prefix_share(held, batch):
        onchip[held, batch] = go(prefix_core(held, batch))

    def prefix_row(batch):
        for direction in (1, -1):
            ride[(-direction) % ys, batch] = go(prefix_y(0, direction, batch))
        prefix_share(0, batch)

    def prefix_arrived(batch):
        ride[ys - 1, batch].wait_recv()
        if batch == 0:
            ride[2, batch] = go(prefix_y(ys - 1, 1, batch))
        ride[1, batch].wait_recv()
        if batch == 1:
            ride[2, batch] = go(prefix_y(1, -1, batch))
        prefix_share(ys - 1, batch)
        prefix_share(1, batch)

    def other_side(held):
        for batch in range(2):
            onchip[held, batch].wait_recv()

    prefix_step(2)
    prefix_row(0)
    attend_fresh(0)
    prefix_step(3)
    fresh_step(1)
    prefix_step(4)
    prefix_row(1)
    attend_cached(0, 0)
    prefix_arrived(0)
    other_side(0)
    attend_cached(1, 0)
    fresh_step(2)
    prefix_arrived(1)
    attend_fresh(1)
    attend_cached(0, ys - 1)
    fresh_step(3)
    attend_cached(0, 1)
    ride[2, 0].wait_recv()
    prefix_share(2, 0)
    ride[2, 1].wait_recv()
    prefix_share(2, 1)
    attend_fresh(2)
    fresh_step(4)
    other_side(ys - 1)
    attend_cached(1, ys - 1)
    out_ring = {3: weights_x(0, 1), 1: weights_x(0, -1)}
    out_ring[3].wait_recv()
    relay_right = go(weights_x(3, 1))
    out_ring[1].wait_recv()
    relay_left = go(weights_x(1, -1))
    out_shared = {held: go(weights_core(held)) for held in (3, 1)}
    other_side(1)
    attend_cached(1, 1)
    attend_cached(0, 2)
    attend_fresh(3)
    other_side(2)
    attend_cached(1, 2)
    attend_fresh(4)

    for j in range(heads):
        value = (accum[j] / total[j]).astype(jnp.bfloat16)
        context[:, :, j * HD : (j + 1) * HD] = value.reshape(xs, part, HD)
    crossing = {}
    for dx in (2, 1, 3):
        crossing[xs - dx] = go(
            remote(
                context.at[(head + dx) % xs],
                contexts.at[xs - dx],
                cx_send.at[dx],
                cx_recv.at[xs - dx],
                at(dx=dx),
            )
        )
    contexts[0] = context[head]
    relay_right.wait_recv()
    relay_left.wait_recv()
    out_shared[2] = go(weights_core(2))
    out_copy.wait()

    def term(held):
        return jnp.dot(contexts[held], out_weights[held], preferred_element_type=jnp.float32)

    value = hidden_ref[pl.ds(pl.multiple_of(head * part, part), part)].astype(jnp.float32)
    attn = term(0)
    for held in (3, 1, 2):
        out_shared[held].wait_recv()
        crossing[held].wait_recv()
        attn = attn + term(held)
    mid_ref[...] = (value + attn).astype(jnp.bfloat16)
    for copy in sent:
        copy.wait_send()


def attention(sizes, hidden, gain, w_query, w_keyval, prefix, w_out, lengths):
    xs, ys, zs = sizes
    count, width = hidden.shape
    heads = w_query.shape[1] // HD
    columns = w_query.shape[1]
    bf16, f32 = jnp.bfloat16, jnp.float32
    half = np.arange(HD // 2, dtype=np.float32)
    freqs = (10000.0 ** (-2.0 * half / HD)).astype(np.float32)
    freqs = jnp.asarray(np.concatenate([freqs, freqs])[None, :])
    dma = pltpu.SemaphoreType.DMA
    vmem = pl.BlockSpec(memory_space=pltpu.VMEM)
    smem = pl.BlockSpec(memory_space=pltpu.SMEM)
    hbm = pl.BlockSpec(memory_space=pl.ANY)
    return pl.pallas_call(
        functools.partial(attention_kernel, sizes),
        out_shape=jax.ShapeDtypeStruct((count // xs, width), bf16),
        in_specs=[smem, vmem, vmem, vmem, vmem, hbm, vmem, hbm],
        out_specs=vmem,
        scratch_shapes=[
            pltpu.VMEM(w_keyval.shape[1:], bf16),
            pltpu.VMEM((CORES, ys, zs) + prefix.shape, bf16),
            pltpu.VMEM((PAST + 1, 2, CORES, count, HD), bf16),
            pltpu.VMEM((xs,) + w_out.shape, bf16),
            pltpu.VMEM((heads, count, HD), bf16),
            pltpu.VMEM((count, HD), jnp.int32),
            pltpu.VMEM((heads, count, HD), f32),
            pltpu.VMEM((heads, count, HD), f32),
            pltpu.VMEM((heads, count, HD), f32),
            pltpu.VMEM((xs, count // xs, columns), bf16),
            pltpu.VMEM((xs, count // xs, columns), bf16),
            dma((2,)),
            dma((2, zs // 2)),
            dma((2, zs // 2)),
            dma((ys, 2)),
            dma((ys, 2)),
            dma((ys, 2)),
            dma((ys, 2)),
            dma((PAST, 2)),
            dma((PAST, 2)),
            dma((PAST + 1, 2)),
            dma((PAST + 1, 2)),
            dma((xs,)),
            dma((xs,)),
            dma((xs,)),
            dma((xs,)),
            dma((xs,)),
            dma((xs,)),
        ],
        compiler_params=pltpu.CompilerParams(
            collective_id=0, has_side_effects=True, vmem_limit_bytes=60 * 2**20
        ),
    )(lengths, hidden, gain.reshape(1, width), freqs, w_query, w_keyval, prefix, w_out)


def shards(
    hidden_in,
    attn_gain,
    w_query,
    w_keyval,
    prefix_cache,
    w_out,
    moe_gain,
    w_gateup,
    w_down,
    routes,
    route_weights,
    lengths,
):
    head_index = lax.axis_index("head")
    head_count = lax.axis_size("head")
    block_count = lax.axis_size("blk")
    quarter = hidden_in.shape[0] // head_count
    chips_z = 8
    sizes = (head_count, block_count // (CORES * chips_z), chips_z)
    kv_head = head_index // (head_count // KVH)
    cached = lax.dynamic_index_in_dim(prefix_cache, kv_head, 1, keepdims=False)
    middle = attention(
        sizes, hidden_in, attn_gain, w_query, w_keyval, cached, w_out, lengths
    )
    my_routes = lax.dynamic_slice_in_dim(routes, head_index * quarter, quarter, 0)
    my_weights = lax.dynamic_slice_in_dim(route_weights, head_index * quarter, quarter, 0)
    return moe(sizes, middle, moe_gain, my_routes, my_weights, w_gateup, w_down)


def solution(mesh):
    return jax.shard_map(
        shards,
        mesh=mesh,
        in_specs=(
            P("blk", None),
            P(),
            P(None, "head"),
            P(),
            P("blk", None, None),
            P("head", None),
            P(),
            P("blk", None, None),
            P("blk", None, None),
            P("blk", None),
            P("blk", None),
            P(),
        ),
        out_specs=P("blk", "head"),
        check_vma=False,
    )
```

```python
import functools
import jax
import jax.numpy as jnp
import numpy as np
from jax import lax
from jax.experimental import pallas as pl
from jax.experimental.pallas import tpu as pltpu
from jax.sharding import PartitionSpec as P

KVH = 2
HD = 128
PAST = 4
SPLIT = 4
MESH = pl.DeviceIdType.MESH
CORES = 2
ROWS_BLOCK = 64
PIECE = 16
ORDER = (0, 7, 1, 6, 2, 5, 3, 4)
PLACE = {rel: at for at, rel in enumerate(ORDER)}


def layer_kernel(
    sizes,
    lengths_ref,
    hidden_ref,
    gain_ref,
    freqs_ref,
    w_query_ref,
    w_keyval_ref,
    prefix_ref,
    w_out_ref,
    moe_gain_ref,
    routes_ref,
    weights_ref,
    gateup_ref,
    down_ref,
    out_ref,
    w_kv,
    cached,
    fresh,
    out_weights,
    query,
    begin,
    best,
    total,
    accum,
    context,
    contexts,
    mid_ref,
    tokens,
    table,
    tables,
    packed,
    rows,
    outs,
    backs,
    way_out,
    way_back,
    gate_up,
    down,
    partial,
    sums_r,
    sums_l,
    got_r,
    got_l,
    final,
    landed,
    local_sem,
    pz_send,
    pz_recv,
    py_send,
    py_recv,
    pc_send,
    pc_recv,
    nz_send,
    nz_recv,
    nc_send,
    nc_recv,
    wx_send,
    wx_recv,
    wc_send,
    wc_recv,
    cx_send,
    cx_recv,
    ws_send,
    ws_recv,
    tsend,
    trecv,
    zsend,
    zrecv,
    ysend,
    yrecv,
    bsend,
    brecv,
    vsend,
    vrecv,
    ssend,
    srecv,
    xsend,
    xrecv,
):
    xs, ys, zs = sizes
    head = lax.axis_index("head")
    blk = lax.axis_index("blk")
    core = blk % CORES
    chip = blk // CORES
    z = chip % zs
    y = chip // zs
    count, width = hidden_ref.shape
    heads = query.shape[0]
    part = count // xs
    half = w_out_ref.shape[0] // CORES

    def at(dx=0, dy=0, dz=0, other=False):
        cc = 1 - core if other else core
        return (
            (head + dx) % xs,
            (((y + dy) % ys) * zs + (z + dz) % zs) * CORES + cc,
        )

    def along(step):
        return (head, ((chip + step) % (ys * zs)) * CORES + core)

    peers = (
        [at(other=True)]
        + [at(dz=d) for d in range(1, zs)]
        + [at(dy=d) for d in range(1, ys)]
        + [at(dx=d) for d in range(1, xs)]
        + [along(1), along(ys * zs - 1)]
    )
    barrier = pltpu.get_barrier_semaphore()
    for peer in peers:
        pl.semaphore_signal(barrier, inc=1, device_id=peer, device_id_type=MESH)

    def remote(source, target, send, recv, device):
        return pltpu.make_async_remote_copy(
            src_ref=source,
            dst_ref=target,
            send_sem=send,
            recv_sem=recv,
            device_id=device,
            device_id_type=MESH,
        )

    kv_copy = pltpu.make_async_copy(w_keyval_ref.at[head // (xs // KVH)], w_kv, local_sem.at[0])
    kv_copy.start()
    out_copy = pltpu.make_async_copy(w_out_ref, out_weights.at[0], local_sem.at[1])
    out_copy.start()
    own_copies = [
        pltpu.make_async_copy(gateup_ref.at[0], gate_up.at[0], local_sem.at[2]),
        pltpu.make_async_copy(down_ref.at[0], down.at[0], local_sem.at[3]),
    ]
    for copy in own_copies:
        copy.start()
    kv_head = head // (xs // KVH)
    piece = prefix_ref[:, 0, :]
    for g in range(1, KVH):
        piece = jnp.where(kv_head == g, prefix_ref[:, g, :], piece)
    cached[0, 0, 0] = piece
    pl.semaphore_wait(barrier, len(peers))

    sent = []

    def go(copy):
        copy.start()
        sent.append(copy)
        return copy

    def prefix_z(direction, step):
        held = (-step * direction) % zs
        there = (held - direction) % zs
        side = 0 if direction == 1 else 1
        return remote(
            cached.at[0, 0, PLACE[held]],
            cached.at[0, 0, PLACE[there]],
            pz_send.at[side, step],
            pz_recv.at[side, step],
            at(dz=direction),
        )

    batches = (pl.ds(0, SPLIT), pl.ds(SPLIT, zs - SPLIT))

    def prefix_y(held, direction, batch):
        there = (held - direction) % ys
        return remote(
            cached.at[0, held, batches[batch]],
            cached.at[0, there, batches[batch]],
            py_send.at[there, batch],
            py_recv.at[there, batch],
            at(dy=direction),
        )

    def prefix_core(held, batch):
        return remote(
            cached.at[0, held, batches[batch]],
            cached.at[1, held, batches[batch]],
            pc_send.at[held, batch],
            pc_recv.at[held, batch],
            at(other=True),
        )

    flow = {}
    flow[1, 0] = go(prefix_z(1, 0))
    flow[-1, 0] = go(prefix_z(-1, 0))

    mine = pl.ds(pl.multiple_of(core * half, 64), half)

    def weights_x(held, direction):
        there = (held - direction) % xs
        rows = mine
        if held != 0:
            offset = 0 if direction == 1 else half // 2
            rows = pl.ds(pl.multiple_of(core * half + offset, 32), half // 2)
        number = there if held == 0 else (0 if direction == 1 else 2)
        source = w_out_ref.at[rows] if held == 0 else out_weights.at[held, rows]
        return remote(
            source,
            out_weights.at[there, rows],
            wx_send.at[number],
            wx_recv.at[number],
            at(dx=direction),
        )

    def weights_core(held):
        return remote(
            out_weights.at[held, mine],
            out_weights.at[held, mine],
            wc_send.at[held],
            wc_recv.at[held],
            at(other=True),
        )

    out_ring = {3: go(weights_x(0, 1)), 1: go(weights_x(0, -1))}

    token = blk * count + lax.broadcasted_iota(jnp.int32, (count, HD), 0)
    start = jnp.zeros((count, HD), jnp.int32)
    end = jnp.int32(0)
    for r in range(lengths_ref.shape[0]):
        end = end + lengths_ref[r]
        start = jnp.where(token >= end, end, start)
    begin[...] = start
    prefix_total = cached.shape[0] * ys * zs * prefix_ref.shape[0]
    angle = (prefix_total + token - start).astype(jnp.float32) * freqs_ref[...]
    cosine = jnp.cos(angle)
    sine = jnp.sin(angle)
    lane = lax.broadcasted_iota(jnp.int32, (count, HD), 1)
    sine = jnp.where(lane < HD // 2, -sine, sine)

    def turned(vectors):
        return vectors * cosine + pltpu.roll(vectors, HD // 2, 1) * sine

    wide = hidden_ref[...].astype(jnp.float32)
    scale = lax.rsqrt(jnp.mean(wide * wide, axis=-1, keepdims=True) + 1e-05)
    normed = (wide * scale * gain_ref[...].reshape(1, width)).astype(jnp.bfloat16)
    kv_copy.wait()
    keyval = jnp.dot(normed, w_kv[...], preferred_element_type=jnp.float32)
    fresh[0, 0, 0] = turned(keyval[:, :HD]).astype(jnp.bfloat16)
    fresh[0, 1, 0] = keyval[:, HD:].astype(jnp.bfloat16)

    def fresh_next(distance, kind):
        return remote(
            fresh.at[distance, kind, 0],
            fresh.at[distance + 1, kind, 0],
            nz_send.at[distance, kind],
            nz_recv.at[distance, kind],
            along(1),
        )

    def fresh_core(distance, kind):
        return remote(
            fresh.at[distance, kind, 0],
            fresh.at[distance, kind, 1],
            nc_send.at[distance, kind],
            nc_recv.at[distance, kind],
            at(other=True),
        )

    chain = {}
    shared = {}
    for kind in range(2):
        chain[0, kind] = go(fresh_next(0, kind))
    for kind in range(2):
        shared[0, kind] = go(fresh_core(0, kind))

    def prefix_step(step):
        for direction in (1, -1):
            if (direction, step - 1) in flow:
                flow[direction, step - 1].wait_recv()
            if step < zs // 2 - (0 if direction == 1 else 1):
                flow[direction, step] = go(prefix_z(direction, step))

    def fresh_step(distance, kind):
        chain[distance - 1, kind].wait_recv()
        if distance < PAST:
            chain[distance, kind] = go(fresh_next(distance, kind))
        shared[distance, kind] = go(fresh_core(distance, kind))

    prefix_step(1)
    queries = jnp.dot(normed, w_query_ref[...], preferred_element_type=jnp.float32)
    for j in range(heads):
        query[j] = (turned(queries[:, j * HD : (j + 1) * HD]) * HD ** (-0.5)).astype(jnp.bfloat16)
    lanes = table.shape[2]
    wanted = routes_ref[pl.ds(pl.multiple_of(head * part, part), part), :]
    given = weights_ref[pl.ds(pl.multiple_of(head * part, part), part), :]
    column = lax.broadcasted_iota(jnp.int32, (part, lanes), 1)
    group = column % (2 * ys)
    expert = ((y + group % ys) % ys) * zs + column // (2 * ys)
    hit = jnp.zeros((part, lanes), jnp.float32)
    weight = jnp.zeros((part, lanes), jnp.float32)
    for k in range(routes_ref.shape[1]):
        same = wanted[:, k : k + 1] == expert
        hit = hit + jnp.where(same, 1.0, 0.0)
        weight = weight + jnp.where(same, given[:, k : k + 1], 0.0)
    before = jnp.where(
        lax.broadcasted_iota(jnp.int32, (part, part), 1)
        < lax.broadcasted_iota(jnp.int32, (part, part), 0),
        1.0,
        0.0,
    )
    rank = jnp.dot(
        before.astype(jnp.bfloat16),
        hit.astype(jnp.bfloat16),
        preferred_element_type=jnp.float32,
    )
    code = jnp.where(group < ys, jnp.where(hit > 0.5, rank, -1.0), weight)
    code = jnp.concatenate([code, jnp.full((lanes - part, lanes), -1.0, jnp.float32)], axis=0)
    table[...] = jnp.transpose(code)[: zs * 2 * ys].reshape(zs, 2 * ys, lanes)
    tables[0] = table[z]
    table_copies = {}
    for d in range(1, zs):
        table_copies[d] = go(
            remote(
                table.at[(z + d) % zs],
                tables.at[PLACE[zs - d]],
                tsend.at[d],
                trecv.at[zs - d],
                at(dz=d),
            )
        )

    best[...] = jnp.full(best.shape, -1e30, jnp.float32)
    total[...] = jnp.zeros(total.shape, jnp.float32)
    accum[...] = jnp.zeros(accum.shape, jnp.float32)

    def attend(pieces, distance=None):
        if distance is not None:
            length = pieces[0][0].shape[0]
            place = lax.broadcasted_iota(jnp.int32, (1, length), 1)
            own_block = (blk - CORES * distance) * count
            other_block = (blk + 1 - 2 * core - CORES * distance) * count
            where = jnp.where(place < count, own_block + place, other_block + place - count)

        def one_head(j, carry):
            parts = [
                lax.dot_general(
                    query[j], keys, (((1,), (1,)), ((), ())), preferred_element_type=jnp.float32
                )
                for keys, unused in pieces
            ]
            if distance is not None:
                valid = where >= begin[:, :1]
                if distance == 0:
                    row = blk * count + lax.broadcasted_iota(jnp.int32, (count, 1), 0)
                    valid = valid & (where <= row)
                parts = [jnp.where(valid, parts[0], -1e30)]
            old = best[j]
            new = old
            for scores in parts:
                new = jnp.maximum(new, jnp.max(scores, axis=1, keepdims=True))
            rescale = jnp.exp(old - new)
            best[j] = new
            summed = total[j] * rescale
            mixed = accum[j] * rescale
            for scores, (unused, values) in zip(parts, pieces):
                weights = jnp.exp(scores - new[:, :1])
                summed = summed + jnp.sum(weights, axis=1, keepdims=True)
                mixed = mixed + jnp.dot(
                    weights.astype(jnp.bfloat16), values, preferred_element_type=jnp.float32
                )
            total[j] = summed
            accum[j] = mixed
            return carry

        lax.fori_loop(0, heads, one_head, 0)

    def attend_fresh(distance):
        for kind in range(2):
            shared[distance, kind].wait_recv()
        attend(
            [
                (
                    fresh[distance, 0].reshape(CORES * count, HD),
                    fresh[distance, 1].reshape(CORES * count, HD),
                )
            ],
            distance,
        )

    def attend_cached(*names):
        pieces = []
        for side, held, batch in names:
            if side == 1:
                onchip[held, batch].wait_recv()
            piece = cached[side, held, batches[batch]]
            piece = piece.reshape(batches[batch].size * prefix_ref.shape[0], 2 * HD)
            pieces.append((piece[:, :HD], piece[:, HD:]))
        attend(pieces)

    ride = {}
    onchip = {}

    def prefix_share(held, batch):
        onchip[held, batch] = go(prefix_core(held, batch))

    def prefix_row(batch):
        for direction in (1, -1):
            ride[(-direction) % ys, batch] = go(prefix_y(0, direction, batch))
        prefix_share(0, batch)

    def prefix_arrived(batch):
        ride[ys - 1, batch].wait_recv()
        if batch == 0:
            ride[2, batch] = go(prefix_y(ys - 1, 1, batch))
        ride[1, batch].wait_recv()
        if batch == 1:
            ride[2, batch] = go(prefix_y(1, -1, batch))
        prefix_share(ys - 1, batch)
        prefix_share(1, batch)

    attend_fresh(0)
    prefix_step(2)
    prefix_row(0)
    fresh_step(1, 0)
    fresh_step(1, 1)
    attend_cached((0, 0, 0), (1, 0, 0))
    prefix_step(3)
    attend_fresh(1)
    fresh_step(2, 0)
    fresh_step(2, 1)
    prefix_step(4)
    prefix_row(1)
    prefix_arrived(0)
    attend_cached((0, ys - 1, 0), (0, 1, 0))
    attend_cached((0, 0, 1), (1, 0, 1))
    fresh_step(3, 0)
    fresh_step(3, 1)
    attend_fresh(2)
    prefix_arrived(1)
    out_ring[3].wait_recv()
    relay_right = go(weights_x(3, 1))
    out_ring[1].wait_recv()
    relay_left = go(weights_x(1, -1))
    out_shared = {held: go(weights_core(held)) for held in (3, 1)}
    attend_cached((1, ys - 1, 0), (1, 1, 0))
    fresh_step(4, 0)
    fresh_step(4, 1)
    attend_cached((0, ys - 1, 1), (0, 1, 1))
    ride[2, 0].wait_recv()
    prefix_share(2, 0)
    attend_cached((1, ys - 1, 1), (1, 1, 1))
    ride[2, 1].wait_recv()
    prefix_share(2, 1)
    attend_fresh(3)
    weight_copies = [
        go(remote(gateup_ref.at[0], gate_up.at[1], ws_send.at[0], ws_recv.at[0], at(other=True))),
        go(remote(down_ref.at[0], down.at[1], ws_send.at[1], ws_recv.at[1], at(other=True))),
    ]
    attend_cached((0, 2, 0), (0, 2, 1))
    attend_fresh(4)
    relay_right.wait_recv()
    relay_left.wait_recv()
    out_shared[2] = go(weights_core(2))
    attend_cached((1, 2, 0), (1, 2, 1))

    for j in range(heads):
        value = (accum[j] / total[j]).astype(jnp.bfloat16)
        context[:, :, j * HD : (j + 1) * HD] = value.reshape(xs, part, HD)
    crossing = {}
    for dx in (2, 1, 3):
        crossing[xs - dx] = go(
            remote(
                context.at[(head + dx) % xs],
                contexts.at[xs - dx],
                cx_send.at[dx],
                cx_recv.at[xs - dx],
                at(dx=dx),
            )
        )
    contexts[0] = context[head]
    out_copy.wait()

    def term(held):
        return jnp.dot(contexts[held], out_weights[held], preferred_element_type=jnp.float32)

    value = hidden_ref[pl.ds(pl.multiple_of(head * part, part), part)].astype(jnp.float32)
    attn = term(0)
    for held in (3, 1, 2):
        out_shared[held].wait_recv()
        crossing[held].wait_recv()
        attn = attn + term(held)
    middle = (value + attn).astype(jnp.bfloat16)
    mid_ref[...] = middle
    wide = middle.astype(jnp.float32)
    scale = lax.rsqrt(jnp.mean(wide * wide, axis=-1, keepdims=True) + 1e-05)
    tokens[0] = (wide * scale * moe_gain_ref[...].reshape(1, width)).astype(jnp.bfloat16)
    half_units = down.shape[1]
    chunk = ROWS_BLOCK // 2

    def token_copy(direction, step, piece):
        held = (-step * direction) % zs
        there = (held - direction) % zs
        number = step * 2 + piece
        side = 0 if direction == 1 else 1
        return pltpu.make_async_remote_copy(
            src_ref=tokens.at[PLACE[held], pl.ds(piece * chunk, chunk)],
            dst_ref=tokens.at[PLACE[there], pl.ds(piece * chunk, chunk)],
            send_sem=zsend.at[side, number],
            recv_sem=zrecv.at[side, number],
            device_id=at(dz=direction),
            device_id_type=MESH,
        )

    reach = zs // 2
    flow = {}
    for direction in (1, -1):
        for step in range(reach):
            for piece in range(2):
                if step < reach - 1 or piece == (0 if direction == 1 else 1):
                    flow[direction, step, piece] = token_copy(direction, step, piece)

    for piece in range(2):
        go(flow[1, 0, piece])
        go(flow[-1, 0, piece])

    slot = lax.broadcasted_iota(jnp.int32, (ys * PIECE, lanes), 0) % PIECE
    slot = slot.astype(jnp.float32)

    def spread(place, first):
        return jnp.concatenate(
            [
                jnp.broadcast_to(tables[place, first + dy : first + dy + 1, :], (PIECE, lanes))
                for dy in range(ys)
            ],
            axis=0,
        )

    def side_of(place):
        return 1 if place % 2 == 0 else -1

    def y_copies(source, target, way, number, send, recv):
        def direct(place, dy):
            return remote(
                source.at[place, dy],
                target.at[place, ys - dy],
                send.at[place, dy],
                recv.at[place, ys - dy],
                at(dy=dy),
            )

        def first_leg(place):
            return remote(
                source.at[place, 2],
                way.at[place],
                vsend.at[number, place],
                vrecv.at[number, place],
                at(dy=side_of(place)),
            )

        def second_leg(place):
            return remote(
                way.at[place],
                target.at[place, 2],
                send.at[place, 2],
                recv.at[place, 2],
                at(dy=side_of(place)),
            )

        def start(place):
            go(first_leg(place))
            go(direct(place, 1))
            go(direct(place, ys - 1))

        def relay(*places):
            for place in places:
                first_leg(place).wait_recv()
                go(second_leg(place))

        def arrived(place):
            direct(place, 1).wait_recv()
            direct(place, ys - 1).wait_recv()
            second_leg(place).wait_recv()

        return start, relay, arrived

    send_pieces, relay_pieces, pieces_here = y_copies(packed, rows, way_out, 0, ysend, yrecv)
    send_backs, relay_backs, backs_here = y_copies(outs, backs, way_back, 1, bsend, brecv)

    def pack(place):
        if place > 0:
            table_copies[(zs - ORDER[place])].wait_recv()
        chosen = jnp.where(spread(place, 0) == slot, 1.0, 0.0).astype(jnp.bfloat16)
        value = jnp.dot(
            chosen[:, :ROWS_BLOCK], tokens[place], preferred_element_type=jnp.float32
        ).astype(jnp.bfloat16)
        value = value.reshape(ys, PIECE, width)
        packed[place, 1:] = value[1:]
        rows[place, 0] = value[0]
        send_pieces(place)

    def experts(first, count):
        for place in range(first, first + count):
            pieces_here(place)
        taken = rows[first : first + count].reshape(count * ys * PIECE, width)
        total = None
        for side in range(2):
            both = jnp.dot(taken, gate_up[side], preferred_element_type=jnp.float32)
            hidden = jax.nn.relu(both[:, :half_units]) * both[:, half_units:]
            term = jnp.dot(
                hidden.astype(jnp.bfloat16), down[side], preferred_element_type=jnp.float32
            )
            total = term if total is None else total + term
        value = total.astype(jnp.bfloat16).reshape(count, ys, PIECE, width)
        outs[first : first + count, 1:] = value[:, 1:]
        backs[first : first + count, 0] = value[:, 0]
        for place in range(first, first + count):
            send_backs(place)

    def combine(place):
        backs_here(place)
        mixing = jnp.where(spread(place, 0) == slot, spread(place, ys), 0.0)
        mixing = mixing.astype(jnp.bfloat16)[:, :ROWS_BLOCK]
        partial[place] = lax.dot_general(
            mixing,
            backs[place].reshape(ys * PIECE, width),
            (((0,), (0,)), ((), ())),
            preferred_element_type=jnp.float32,
        )

    def tokens_step(step):
        for piece in range(2):
            for direction in (1, -1):
                if (direction, step - 1, piece) in flow:
                    flow[direction, step - 1, piece].wait_recv()
                if (direction, step, piece) in flow:
                    go(flow[direction, step, piece])

    pack(0)
    tokens_step(1)
    relay_pieces(0)
    pack(1)
    pack(2)
    for copy in own_copies:
        copy.wait()
    for copy in weight_copies:
        copy.wait_recv()
    tokens_step(2)
    relay_pieces(1, 2)
    pack(3)
    pack(4)
    experts(0, 1)
    tokens_step(3)
    relay_pieces(3, 4)
    pack(5)
    pack(6)
    relay_backs(0)
    experts(1, 2)
    tokens_step(4)
    relay_pieces(5, 6)
    pack(7)
    relay_backs(1, 2)
    experts(3, 2)
    relay_pieces(7)
    combine(0)
    relay_backs(3, 4)
    experts(5, 2)
    combine(1)
    combine(2)
    experts(7, 1)
    relay_backs(5, 6)
    combine(3)
    combine(4)

    def sum_copy(direction, held, piece):
        side = 0 if direction == 1 else 1
        number = (held if direction == 1 else zs - held) * 2 + piece
        source, target = (sums_r, got_r) if direction == 1 else (sums_l, got_l)
        return pltpu.make_async_remote_copy(
            src_ref=source.at[number],
            dst_ref=target.at[number],
            send_sem=ssend.at[side, number],
            recv_sem=srecv.at[side, number],
            device_id=at(dz=direction),
            device_id_type=MESH,
        )

    returned = {}

    def pass_on(direction, distance, piece):
        held = distance if direction == 1 else zs - distance
        number = distance * 2 + piece
        value = partial[PLACE[held], pl.ds(piece * chunk, chunk)]
        source, target = (sums_r, got_r) if direction == 1 else (sums_l, got_l)
        if (direction, distance + 1, piece) in returned:
            returned[direction, distance + 1, piece].wait_recv()
            value = value + target[number + 2].astype(jnp.float32)
        source[number] = value.astype(jnp.bfloat16)
        copy = sum_copy(direction, held, piece)
        returned[direction, distance, piece] = go(copy)

    combine(PLACE[reach - 1])
    pass_on(1, reach - 1, 1)
    combine(PLACE[zs - reach + 1])
    pass_on(-1, reach - 1, 0)
    relay_backs(7)
    combine(PLACE[reach])
    pass_on(1, reach, 0)
    pass_on(-1, reach, 1)
    for distance in range(reach - 1, 0, -1):
        if distance < reach - 1:
            pass_on(1, distance, 1)
            pass_on(-1, distance, 0)
        pass_on(1, distance, 0)
        pass_on(-1, distance, 1)
    for piece in (1, 0):
        spot = pl.ds(piece * chunk, chunk)
        returned[1, 1, piece].wait_recv()
        returned[-1, 1, piece].wait_recv()
        value = (
            mid_ref[spot].astype(jnp.float32)
            + partial[0, spot]
            + got_r[2 + piece].astype(jnp.float32)
            + got_l[2 + piece].astype(jnp.float32)
        ).astype(jnp.bfloat16)
        share = width // xs
        for part_x in range(xs):
            final[part_x, spot] = value[:, part_x * share : (part_x + 1) * share]

    last = []
    for dx in range(1, xs):
        copy = pltpu.make_async_remote_copy(
            src_ref=final.at[(head + dx) % xs],
            dst_ref=landed.at[head],
            send_sem=xsend.at[dx],
            recv_sem=xrecv.at[xs - dx],
            device_id=at(dx=dx),
            device_id_type=MESH,
        )
        go(copy)
        last.append(copy)
    out_ref[head] = final[head]
    for dx in range(1, xs):
        last[xs - dx - 1].wait_recv()
        out_ref[(head + dx) % xs] = landed[(head + dx) % xs]

    for copy in sent:
        copy.wait_send()


def layer(
    sizes,
    hidden,
    gain,
    w_query,
    w_keyval,
    prefix,
    w_out,
    moe_gain,
    w_gateup,
    w_down,
    routes,
    weights,
    lengths,
):
    xs, ys, zs = sizes
    count, width = hidden.shape
    heads = w_query.shape[1] // HD
    part = count // xs
    lanes = 128
    bf16, f32 = jnp.bfloat16, jnp.float32
    half = np.arange(HD // 2, dtype=np.float32)
    freqs = (10000.0 ** (-2.0 * half / HD)).astype(np.float32)
    freqs = jnp.asarray(np.concatenate([freqs, freqs])[None, :])
    dma = pltpu.SemaphoreType.DMA
    vmem = pl.BlockSpec(memory_space=pltpu.VMEM)
    smem = pl.BlockSpec(memory_space=pltpu.SMEM)
    hbm = pl.BlockSpec(memory_space=pl.ANY)
    out = pl.pallas_call(
        functools.partial(layer_kernel, sizes),
        out_shape=jax.ShapeDtypeStruct((xs, part, width // xs), bf16),
        in_specs=[smem, vmem, vmem, vmem, vmem, hbm, vmem, hbm, vmem, vmem, vmem, hbm, hbm],
        out_specs=vmem,
        scratch_shapes=[
            pltpu.VMEM(w_keyval.shape[1:], bf16),
            pltpu.VMEM((CORES, ys, zs, prefix.shape[0], 2 * HD), bf16),
            pltpu.VMEM((PAST + 1, 2, CORES, count, HD), bf16),
            pltpu.VMEM((xs,) + w_out.shape, bf16),
            pltpu.VMEM((heads, count, HD), bf16),
            pltpu.VMEM((count, HD), jnp.int32),
            pltpu.VMEM((heads, count, HD), f32),
            pltpu.VMEM((heads, count, HD), f32),
            pltpu.VMEM((heads, count, HD), f32),
            pltpu.VMEM((xs, part, heads * HD), bf16),
            pltpu.VMEM((xs, part, heads * HD), bf16),
            pltpu.VMEM((part, width), bf16),
            pltpu.VMEM((zs, part, width), bf16),
            pltpu.VMEM((zs, 2 * ys, lanes), f32),
            pltpu.VMEM((zs, 2 * ys, lanes), f32),
            pltpu.VMEM((zs, ys, PIECE, width), bf16),
            pltpu.VMEM((zs, ys, PIECE, width), bf16),
            pltpu.VMEM((zs, ys, PIECE, width), bf16),
            pltpu.VMEM((zs, ys, PIECE, width), bf16),
            pltpu.VMEM((zs, PIECE, width), bf16),
            pltpu.VMEM((zs, PIECE, width), bf16),
            pltpu.VMEM((2,) + w_gateup.shape[1:], bf16),
            pltpu.VMEM((2,) + w_down.shape[1:], bf16),
            pltpu.VMEM((zs, part, width), f32),
            pltpu.VMEM((zs + 2, part // 2, width), bf16),
            pltpu.VMEM((zs + 2, part // 2, width), bf16),
            pltpu.VMEM((zs + 2, part // 2, width), bf16),
            pltpu.VMEM((zs + 2, part // 2, width), bf16),
            pltpu.VMEM((xs, part, width // xs), bf16),
            pltpu.VMEM((xs, part, width // xs), bf16),
            dma((4,)),
            dma((2, zs // 2)),
            dma((2, zs // 2)),
            dma((ys, 2)),
            dma((ys, 2)),
            dma((ys, 2)),
            dma((ys, 2)),
            dma((PAST, 2)),
            dma((PAST, 2)),
            dma((PAST + 1, 2)),
            dma((PAST + 1, 2)),
            dma((xs,)),
            dma((xs,)),
            dma((xs,)),
            dma((xs,)),
            dma((xs,)),
            dma((xs,)),
            dma((2,)),
            dma((2,)),
            dma((zs,)),
            dma((zs,)),
            dma((2, zs)),
            dma((2, zs)),
            dma((zs, ys)),
            dma((zs, ys)),
            dma((zs, ys)),
            dma((zs, ys)),
            dma((2, zs)),
            dma((2, zs)),
            dma((2, zs + 2)),
            dma((2, zs + 2)),
            dma((xs,)),
            dma((xs,)),
        ],
        compiler_params=pltpu.CompilerParams(
            collective_id=0, has_side_effects=True, vmem_limit_bytes=62 * 2**20
        ),
    )(
        lengths,
        hidden,
        gain,
        freqs,
        w_query,
        w_keyval,
        prefix,
        w_out,
        moe_gain,
        routes,
        weights,
        w_gateup,
        w_down,
    )
    return out.reshape(count, width // xs)


def shards(
    hidden_in,
    attn_gain,
    w_query,
    w_keyval,
    prefix_cache,
    w_out,
    moe_gain,
    w_gateup,
    w_down,
    routes,
    route_weights,
    lengths,
):
    chips_z = 8
    sizes = (lax.axis_size("head"), lax.axis_size("blk") // (CORES * chips_z), chips_z)
    return layer(
        sizes,
        hidden_in,
        attn_gain,
        w_query,
        w_keyval,
        prefix_cache,
        w_out,
        moe_gain,
        w_gateup,
        w_down,
        routes,
        route_weights,
        lengths,
    )


def solution(mesh):
    return jax.shard_map(
        shards,
        mesh=mesh,
        in_specs=(
            P("blk", None),
            P(),
            P(None, "head"),
            P(),
            P("blk", None, None),
            P("head", None),
            P(),
            P("blk", None, None),
            P("blk", None, None),
            P("blk", None),
            P("blk", None),
            P(),
        ),
        out_specs=P("blk", "head"),
        check_vma=False,
    )
```

```python
import functools
import jax
import jax.numpy as jnp
import numpy as np
from jax import lax
from jax.experimental import pallas as pl
from jax.experimental.pallas import tpu as pltpu
from jax.sharding import PartitionSpec as P

KVH = 2
HD = 128
PAST = 4
SPLIT = 4
MESH = pl.DeviceIdType.MESH
CORES = 2
ROWS_BLOCK = 64
PIECE = 16
ORDER = (0, 7, 1, 6, 2, 5, 3, 4)
PLACE = {rel: at for at, rel in enumerate(ORDER)}


def layer_kernel(
    sizes,
    lengths_ref,
    hidden_ref,
    gain_ref,
    freqs_ref,
    w_query_ref,
    w_keyval_ref,
    prefix_ref,
    w_out_ref,
    moe_gain_ref,
    routes_ref,
    weights_ref,
    gateup_ref,
    down_ref,
    out_ref,
    w_kv,
    cached,
    fresh,
    out_weights,
    query,
    begin,
    best,
    total,
    accum,
    context,
    contexts,
    mid_ref,
    tokens,
    table,
    tables,
    packed,
    rows,
    outs,
    backs,
    way_out,
    way_back,
    gate_up,
    down,
    partial,
    sums_r,
    sums_l,
    got_r,
    got_l,
    final,
    landed,
    local_sem,
    pz_send,
    pz_recv,
    py_send,
    py_recv,
    pc_send,
    pc_recv,
    nz_send,
    nz_recv,
    nc_send,
    nc_recv,
    wx_send,
    wx_recv,
    wc_send,
    wc_recv,
    cx_send,
    cx_recv,
    ws_send,
    ws_recv,
    tsend,
    trecv,
    zsend,
    zrecv,
    ysend,
    yrecv,
    bsend,
    brecv,
    vsend,
    vrecv,
    ssend,
    srecv,
    xsend,
    xrecv,
):
    xs, ys, zs = sizes
    head = lax.axis_index("head")
    blk = lax.axis_index("blk")
    core = blk % CORES
    chip = blk // CORES
    z = chip % zs
    y = chip // zs
    count, width = hidden_ref.shape
    heads = query.shape[0]
    part = count // xs
    half = w_out_ref.shape[0] // CORES

    def at(dx=0, dy=0, dz=0, other=False):
        cc = 1 - core if other else core
        return (
            (head + dx) % xs,
            (((y + dy) % ys) * zs + (z + dz) % zs) * CORES + cc,
        )

    def along(step):
        return (head, ((chip + step) % (ys * zs)) * CORES + core)

    peers = (
        [at(other=True)]
        + [at(dz=d) for d in range(1, zs)]
        + [at(dy=d) for d in range(1, ys)]
        + [at(dx=d) for d in range(1, xs)]
        + [along(1), along(ys * zs - 1)]
    )
    barrier = pltpu.get_barrier_semaphore()
    for peer in peers:
        pl.semaphore_signal(barrier, inc=1, device_id=peer, device_id_type=MESH)

    def remote(source, target, send, recv, device):
        return pltpu.make_async_remote_copy(
            src_ref=source,
            dst_ref=target,
            send_sem=send,
            recv_sem=recv,
            device_id=device,
            device_id_type=MESH,
        )

    kv_copy = pltpu.make_async_copy(w_keyval_ref.at[head // (xs // KVH)], w_kv, local_sem.at[0])
    kv_copy.start()
    out_copy = pltpu.make_async_copy(w_out_ref, out_weights.at[0], local_sem.at[1])
    out_copy.start()
    own_copies = [
        pltpu.make_async_copy(gateup_ref.at[0], gate_up.at[0], local_sem.at[2]),
        pltpu.make_async_copy(down_ref.at[0], down.at[0], local_sem.at[3]),
    ]
    for copy in own_copies:
        copy.start()
    kv_head = head // (xs // KVH)
    piece = prefix_ref[:, 0, :]
    for g in range(1, KVH):
        piece = jnp.where(kv_head == g, prefix_ref[:, g, :], piece)
    cached[0, 0, 0] = piece
    pl.semaphore_wait(barrier, len(peers))

    sent = []

    def go(copy):
        copy.start()
        sent.append(copy)
        return copy

    def prefix_z(direction, step):
        held = (-step * direction) % zs
        there = (held - direction) % zs
        side = 0 if direction == 1 else 1
        return remote(
            cached.at[0, 0, PLACE[held]],
            cached.at[0, 0, PLACE[there]],
            pz_send.at[side, step],
            pz_recv.at[side, step],
            at(dz=direction),
        )

    batches = (pl.ds(0, SPLIT), pl.ds(SPLIT, zs - SPLIT))

    def prefix_y(held, direction, batch):
        there = (held - direction) % ys
        return remote(
            cached.at[0, held, batches[batch]],
            cached.at[0, there, batches[batch]],
            py_send.at[there, batch],
            py_recv.at[there, batch],
            at(dy=direction),
        )

    def prefix_core(held, batch):
        return remote(
            cached.at[0, held, batches[batch]],
            cached.at[1, held, batches[batch]],
            pc_send.at[held, batch],
            pc_recv.at[held, batch],
            at(other=True),
        )

    flow = {}
    flow[1, 0] = go(prefix_z(1, 0))
    flow[-1, 0] = go(prefix_z(-1, 0))

    mine = pl.ds(pl.multiple_of(core * half, 64), half)

    def weights_x(held, direction):
        there = (held - direction) % xs
        rows = mine
        if held != 0:
            offset = 0 if direction == 1 else half // 2
            rows = pl.ds(pl.multiple_of(core * half + offset, 32), half // 2)
        number = there if held == 0 else (0 if direction == 1 else 2)
        source = w_out_ref.at[rows] if held == 0 else out_weights.at[held, rows]
        return remote(
            source,
            out_weights.at[there, rows],
            wx_send.at[number],
            wx_recv.at[number],
            at(dx=direction),
        )

    def weights_core(held):
        return remote(
            out_weights.at[held, mine],
            out_weights.at[held, mine],
            wc_send.at[held],
            wc_recv.at[held],
            at(other=True),
        )

    out_ring = {3: go(weights_x(0, 1)), 1: go(weights_x(0, -1))}

    token = blk * count + lax.broadcasted_iota(jnp.int32, (count, HD), 0)
    start = jnp.zeros((count, HD), jnp.int32)
    end = jnp.int32(0)
    for r in range(lengths_ref.shape[0]):
        end = end + lengths_ref[r]
        start = jnp.where(token >= end, end, start)
    lane_token = blk * count + lax.broadcasted_iota(jnp.int32, (1, count), 1)
    lane_start = jnp.zeros((1, count), jnp.int32)
    end = jnp.int32(0)
    for r in range(lengths_ref.shape[0]):
        end = end + lengths_ref[r]
        lane_start = jnp.where(lane_token >= end, end, lane_start)
    begin[...] = lane_start
    prefix_total = cached.shape[0] * ys * zs * prefix_ref.shape[0]
    angle = (prefix_total + token - start).astype(jnp.float32) * freqs_ref[...]
    cosine = jnp.cos(angle)
    sine = jnp.sin(angle)
    lane = lax.broadcasted_iota(jnp.int32, (count, HD), 1)
    sine = jnp.where(lane < HD // 2, -sine, sine)

    def turned(vectors):
        return vectors * cosine + pltpu.roll(vectors, HD // 2, 1) * sine

    wide = hidden_ref[...].astype(jnp.float32)
    scale = lax.rsqrt(jnp.mean(wide * wide, axis=-1, keepdims=True) + 1e-05)
    normed = (wide * scale * gain_ref[...].reshape(1, width)).astype(jnp.bfloat16)
    kv_copy.wait()
    keyval = jnp.dot(normed, w_kv[...], preferred_element_type=jnp.float32)
    fresh[0, 0, 0] = turned(keyval[:, :HD]).astype(jnp.bfloat16)
    fresh[0, 1, 0] = keyval[:, HD:].astype(jnp.bfloat16)

    def fresh_next(distance, kind):
        return remote(
            fresh.at[distance, kind, 0],
            fresh.at[distance + 1, kind, 0],
            nz_send.at[distance, kind],
            nz_recv.at[distance, kind],
            along(1),
        )

    def fresh_core(distance, kind):
        return remote(
            fresh.at[distance, kind, 0],
            fresh.at[distance, kind, 1],
            nc_send.at[distance, kind],
            nc_recv.at[distance, kind],
            at(other=True),
        )

    chain = {}
    shared = {}
    for kind in range(2):
        chain[0, kind] = go(fresh_next(0, kind))
    for kind in range(2):
        shared[0, kind] = go(fresh_core(0, kind))

    def prefix_step(step):
        for direction in (1, -1):
            if (direction, step - 1) in flow:
                flow[direction, step - 1].wait_recv()
            if step < zs // 2 - (0 if direction == 1 else 1):
                flow[direction, step] = go(prefix_z(direction, step))

    def fresh_step(distance, kind):
        chain[distance - 1, kind].wait_recv()
        if distance < PAST:
            chain[distance, kind] = go(fresh_next(distance, kind))
        shared[distance, kind] = go(fresh_core(distance, kind))

    prefix_step(1)
    queries = jnp.dot(normed, w_query_ref[...], preferred_element_type=jnp.float32)
    for j in range(heads):
        query[j] = (turned(queries[:, j * HD : (j + 1) * HD]) * HD ** (-0.5)).astype(jnp.bfloat16)
    lanes = table.shape[2]
    def quarter_of(ref):
        return pltpu.roll(ref[...], (xs - head) % xs * part, 1)[:, :lanes]

    row = lax.broadcasted_iota(jnp.int32, (zs * 2 * ys, lanes), 0)
    wanted = quarter_of(routes_ref)
    wanted = jnp.where(lax.broadcasted_iota(jnp.int32, wanted.shape, 1) < part, wanted, -1)
    given = quarter_of(weights_ref)
    group = row % (2 * ys)
    expert = ((y + group % ys) % ys) * zs + row // (2 * ys)
    hit = jnp.zeros((zs * 2 * ys, lanes), jnp.float32)
    weight = jnp.zeros((zs * 2 * ys, lanes), jnp.float32)
    for k in range(routes_ref.shape[0]):
        same = wanted[k : k + 1, :] == expert
        hit = hit + jnp.where(same, 1.0, 0.0)
        weight = weight + jnp.where(same, given[k : k + 1, :], 0.0)
    before = jnp.where(
        lax.broadcasted_iota(jnp.int32, (lanes, lanes), 0)
        < lax.broadcasted_iota(jnp.int32, (lanes, lanes), 1),
        1.0,
        0.0,
    )
    rank = jnp.dot(
        hit.astype(jnp.bfloat16),
        before.astype(jnp.bfloat16),
        preferred_element_type=jnp.float32,
    )
    code = jnp.where(group < ys, jnp.where(hit > 0.5, rank, -1.0), weight)
    table[...] = code.reshape(zs, 2 * ys, lanes)
    tables[0] = table[z]
    table_copies = {}
    for d in range(1, zs):
        table_copies[d] = go(
            remote(
                table.at[(z + d) % zs],
                tables.at[PLACE[zs - d]],
                tsend.at[d],
                trecv.at[zs - d],
                at(dz=d),
            )
        )

    best[...] = jnp.full(best.shape, -1e30, jnp.float32)
    total[...] = jnp.zeros(total.shape, jnp.float32)
    accum[...] = jnp.zeros(accum.shape, jnp.float32)

    def attend(keys, values, distance=None):
        length = keys.shape[0]
        turned_values = jnp.transpose(values)
        if distance is not None:
            place = lax.broadcasted_iota(jnp.int32, (length, 1), 0)
            own_block = (blk - CORES * distance) * count
            other_block = (blk + 1 - 2 * core - CORES * distance) * count
            where = jnp.where(place < count, own_block + place, other_block + place - count)

        def one_head(j, carry):
            scores = lax.dot_general(
                keys, query[j], (((1,), (1,)), ((), ())), preferred_element_type=jnp.float32
            )
            if distance is not None:
                valid = where >= begin[...]
                if distance == 0:
                    valid = valid & (where <= lane_token)
                scores = jnp.where(valid, scores, -1e30)
            old = best[j]
            new = jnp.maximum(old, jnp.max(scores, axis=0, keepdims=True))
            weights = jnp.exp(scores - new)
            rescale = jnp.exp(old - new)
            best[j] = new
            total[j] = total[j] * rescale + jnp.sum(weights, axis=0, keepdims=True)
            accum[j] = accum[j] * rescale + jnp.dot(
                turned_values, weights.astype(jnp.bfloat16), preferred_element_type=jnp.float32
            )
            return carry

        lax.fori_loop(0, heads, one_head, 0)

    def attend_fresh(distance):
        for kind in range(2):
            shared[distance, kind].wait_recv()
        attend(
            fresh[distance, 0].reshape(CORES * count, HD),
            fresh[distance, 1].reshape(CORES * count, HD),
            distance,
        )

    def attend_cached(*names):
        pieces = []
        for side, held, batch in names:
            if side == 1:
                onchip[held, batch].wait_recv()
            piece = cached[side, held, batches[batch]]
            piece = piece.reshape(batches[batch].size * prefix_ref.shape[0], 2 * HD)
            pieces.append(piece)
        whole = jnp.concatenate(pieces, axis=0)
        attend(whole[:, :HD], whole[:, HD:])

    ride = {}
    onchip = {}

    def prefix_share(held, batch):
        onchip[held, batch] = go(prefix_core(held, batch))

    def prefix_row(batch):
        for direction in (1, -1):
            ride[(-direction) % ys, batch] = go(prefix_y(0, direction, batch))
        prefix_share(0, batch)

    def prefix_arrived(batch):
        ride[ys - 1, batch].wait_recv()
        if batch == 0:
            ride[2, batch] = go(prefix_y(ys - 1, 1, batch))
        ride[1, batch].wait_recv()
        if batch == 1:
            ride[2, batch] = go(prefix_y(1, -1, batch))
        prefix_share(ys - 1, batch)
        prefix_share(1, batch)

    attend_fresh(0)
    prefix_step(2)
    prefix_row(0)
    fresh_step(1, 0)
    fresh_step(1, 1)
    attend_cached((0, 0, 0), (1, 0, 0))
    prefix_step(3)
    attend_fresh(1)
    fresh_step(2, 0)
    fresh_step(2, 1)
    prefix_step(4)
    prefix_row(1)
    prefix_arrived(0)
    attend_cached((0, ys - 1, 0), (0, 1, 0))
    attend_cached((0, 0, 1), (1, 0, 1))
    fresh_step(3, 0)
    fresh_step(3, 1)
    attend_fresh(2)
    prefix_arrived(1)
    out_ring[3].wait_recv()
    relay_right = go(weights_x(3, 1))
    out_ring[1].wait_recv()
    relay_left = go(weights_x(1, -1))
    out_shared = {held: go(weights_core(held)) for held in (3, 1)}
    attend_cached((1, ys - 1, 0), (1, 1, 0))
    fresh_step(4, 0)
    fresh_step(4, 1)
    attend_cached((0, ys - 1, 1), (0, 1, 1))
    ride[2, 0].wait_recv()
    prefix_share(2, 0)
    attend_cached((1, ys - 1, 1), (1, 1, 1))
    ride[2, 1].wait_recv()
    prefix_share(2, 1)
    attend_fresh(3)
    weight_copies = [
        go(remote(gateup_ref.at[0], gate_up.at[1], ws_send.at[0], ws_recv.at[0], at(other=True))),
        go(remote(down_ref.at[0], down.at[1], ws_send.at[1], ws_recv.at[1], at(other=True))),
    ]
    attend_cached((0, 2, 0), (0, 2, 1))
    attend_fresh(4)
    relay_right.wait_recv()
    relay_left.wait_recv()
    out_shared[2] = go(weights_core(2))
    attend_cached((1, 2, 0), (1, 2, 1))

    for j in range(heads):
        value = jnp.transpose(accum[j] / total[j]).astype(jnp.bfloat16)
        context[:, :, j * HD : (j + 1) * HD] = value.reshape(xs, part, HD)
    crossing = {}
    for dx in (2, 1, 3):
        crossing[xs - dx] = go(
            remote(
                context.at[(head + dx) % xs],
                contexts.at[xs - dx],
                cx_send.at[dx],
                cx_recv.at[xs - dx],
                at(dx=dx),
            )
        )
    contexts[0] = context[head]
    out_copy.wait()

    def term(held):
        return jnp.dot(contexts[held], out_weights[held], preferred_element_type=jnp.float32)

    value = hidden_ref[pl.ds(pl.multiple_of(head * part, part), part)].astype(jnp.float32)
    attn = term(0)
    for held in (3, 1, 2):
        out_shared[held].wait_recv()
        crossing[held].wait_recv()
        attn = attn + term(held)
    middle = (value + attn).astype(jnp.bfloat16)
    mid_ref[...] = middle
    wide = middle.astype(jnp.float32)
    scale = lax.rsqrt(jnp.mean(wide * wide, axis=-1, keepdims=True) + 1e-05)
    tokens[0] = (wide * scale * moe_gain_ref[...].reshape(1, width)).astype(jnp.bfloat16)
    half_units = down.shape[1]
    chunk = ROWS_BLOCK // 2

    def token_copy(direction, step, piece):
        held = (-step * direction) % zs
        there = (held - direction) % zs
        number = step * 2 + piece
        side = 0 if direction == 1 else 1
        return pltpu.make_async_remote_copy(
            src_ref=tokens.at[PLACE[held], pl.ds(piece * chunk, chunk)],
            dst_ref=tokens.at[PLACE[there], pl.ds(piece * chunk, chunk)],
            send_sem=zsend.at[side, number],
            recv_sem=zrecv.at[side, number],
            device_id=at(dz=direction),
            device_id_type=MESH,
        )

    reach = zs // 2
    flow = {}
    for direction in (1, -1):
        for step in range(reach):
            for piece in range(2):
                if step < reach - 1 or piece == (0 if direction == 1 else 1):
                    flow[direction, step, piece] = token_copy(direction, step, piece)

    for piece in range(2):
        go(flow[1, 0, piece])
        go(flow[-1, 0, piece])

    slot = lax.broadcasted_iota(jnp.int32, (ys * PIECE, lanes), 0) % PIECE
    slot = slot.astype(jnp.float32)

    def spread(place, first):
        return jnp.concatenate(
            [
                jnp.broadcast_to(tables[place, first + dy : first + dy + 1, :], (PIECE, lanes))
                for dy in range(ys)
            ],
            axis=0,
        )

    def side_of(place):
        return 1 if place % 2 == 0 else -1

    def y_copies(source, target, way, number, send, recv):
        def direct(place, dy):
            return remote(
                source.at[place, dy],
                target.at[place, ys - dy],
                send.at[place, dy],
                recv.at[place, ys - dy],
                at(dy=dy),
            )

        def first_leg(place):
            return remote(
                source.at[place, 2],
                way.at[place],
                vsend.at[number, place],
                vrecv.at[number, place],
                at(dy=side_of(place)),
            )

        def second_leg(place):
            return remote(
                way.at[place],
                target.at[place, 2],
                send.at[place, 2],
                recv.at[place, 2],
                at(dy=side_of(place)),
            )

        def start(place):
            go(direct(place, 2) if place == zs - 1 else first_leg(place))
            go(direct(place, 1))
            go(direct(place, ys - 1))

        def relay(*places):
            for place in places:
                first_leg(place).wait_recv()
                go(second_leg(place))

        def arrived(place):
            direct(place, 1).wait_recv()
            direct(place, ys - 1).wait_recv()
            (direct if place == zs - 1 else lambda at_place, dy: second_leg(at_place))(place, 2).wait_recv()

        return start, relay, arrived

    send_pieces, relay_pieces, pieces_here = y_copies(packed, rows, way_out, 0, ysend, yrecv)
    send_backs, relay_backs, backs_here = y_copies(outs, backs, way_back, 1, bsend, brecv)

    def pack(place):
        if place > 0:
            table_copies[(zs - ORDER[place])].wait_recv()
        chosen = jnp.where(spread(place, 0) == slot, 1.0, 0.0).astype(jnp.bfloat16)
        value = jnp.dot(
            chosen[:, :ROWS_BLOCK], tokens[place], preferred_element_type=jnp.float32
        ).astype(jnp.bfloat16)
        value = value.reshape(ys, PIECE, width)
        packed[place, 1:] = value[1:]
        rows[place, 0] = value[0]
        send_pieces(place)

    def experts(first, count):
        for place in range(first, first + count):
            pieces_here(place)
        taken = rows[first : first + count].reshape(count * ys * PIECE, width)
        total = None
        for side in range(2):
            both = jnp.dot(taken, gate_up[side], preferred_element_type=jnp.float32)
            hidden = jax.nn.relu(both[:, :half_units]) * both[:, half_units:]
            term = jnp.dot(
                hidden.astype(jnp.bfloat16), down[side], preferred_element_type=jnp.float32
            )
            total = term if total is None else total + term
        value = total.astype(jnp.bfloat16).reshape(count, ys, PIECE, width)
        outs[first : first + count, 1:] = value[:, 1:]
        backs[first : first + count, 0] = value[:, 0]
        for place in range(first, first + count):
            send_backs(place)

    def combine(place):
        backs_here(place)
        mixing = jnp.where(spread(place, 0) == slot, spread(place, ys), 0.0)
        mixing = mixing.astype(jnp.bfloat16)[:, :ROWS_BLOCK]
        partial[place] = lax.dot_general(
            mixing,
            backs[place].reshape(ys * PIECE, width),
            (((0,), (0,)), ((), ())),
            preferred_element_type=jnp.float32,
        )

    def tokens_step(step):
        for piece in range(2):
            for direction in (1, -1):
                if (direction, step - 1, piece) in flow:
                    flow[direction, step - 1, piece].wait_recv()
                if (direction, step, piece) in flow:
                    go(flow[direction, step, piece])

    pack(0)
    tokens_step(1)
    relay_pieces(0)
    pack(1)
    pack(2)
    for copy in own_copies:
        copy.wait()
    for copy in weight_copies:
        copy.wait_recv()
    tokens_step(2)
    relay_pieces(1, 2)
    pack(3)
    pack(4)
    tokens_step(3)
    relay_pieces(3, 4)
    pack(5)
    pack(6)
    experts(0, 3)
    tokens_step(4)
    relay_pieces(5, 6)
    pack(7)
    relay_backs(0, 1, 2)
    experts(3, 2)
    combine(0)
    combine(1)
    combine(2)
    relay_backs(3, 4)
    experts(5, 3)
    relay_backs(5, 6)
    combine(3)
    combine(4)

    def sum_copy(direction, held, piece):
        side = 0 if direction == 1 else 1
        number = (held if direction == 1 else zs - held) * 2 + piece
        source, target = (sums_r, got_r) if direction == 1 else (sums_l, got_l)
        return pltpu.make_async_remote_copy(
            src_ref=source.at[number],
            dst_ref=target.at[number],
            send_sem=ssend.at[side, number],
            recv_sem=srecv.at[side, number],
            device_id=at(dz=direction),
            device_id_type=MESH,
        )

    returned = {}

    def pass_on(direction, distance, piece):
        held = distance if direction == 1 else zs - distance
        number = distance * 2 + piece
        value = partial[PLACE[held], pl.ds(piece * chunk, chunk)]
        source, target = (sums_r, got_r) if direction == 1 else (sums_l, got_l)
        if (direction, distance + 1, piece) in returned:
            returned[direction, distance + 1, piece].wait_recv()
            value = value + target[number + 2].astype(jnp.float32)
        source[number] = value.astype(jnp.bfloat16)
        copy = sum_copy(direction, held, piece)
        returned[direction, distance, piece] = go(copy)

    combine(PLACE[reach - 1])
    pass_on(1, reach - 1, 1)
    combine(PLACE[zs - reach + 1])
    pass_on(-1, reach - 1, 0)
    combine(PLACE[reach])
    pass_on(1, reach, 0)
    pass_on(-1, reach, 1)
    for distance in range(reach - 1, 0, -1):
        if distance < reach - 1:
            pass_on(1, distance, 1)
            pass_on(-1, distance, 0)
        pass_on(1, distance, 0)
        pass_on(-1, distance, 1)
    for piece in (1, 0):
        spot = pl.ds(piece * chunk, chunk)
        returned[1, 1, piece].wait_recv()
        returned[-1, 1, piece].wait_recv()
        value = (
            mid_ref[spot].astype(jnp.float32)
            + partial[0, spot]
            + got_r[2 + piece].astype(jnp.float32)
            + got_l[2 + piece].astype(jnp.float32)
        ).astype(jnp.bfloat16)
        share = width // xs
        for part_x in range(xs):
            final[part_x, spot] = value[:, part_x * share : (part_x + 1) * share]

    last = []
    for dx in range(1, xs):
        copy = pltpu.make_async_remote_copy(
            src_ref=final.at[(head + dx) % xs],
            dst_ref=landed.at[head],
            send_sem=xsend.at[dx],
            recv_sem=xrecv.at[xs - dx],
            device_id=at(dx=dx),
            device_id_type=MESH,
        )
        go(copy)
        last.append(copy)
    out_ref[head] = final[head]
    for dx in range(1, xs):
        last[xs - dx - 1].wait_recv()
        out_ref[(head + dx) % xs] = landed[(head + dx) % xs]

    for copy in sent:
        copy.wait_send()


def layer(
    sizes,
    hidden,
    gain,
    w_query,
    w_keyval,
    prefix,
    w_out,
    moe_gain,
    w_gateup,
    w_down,
    routes,
    weights,
    lengths,
):
    xs, ys, zs = sizes
    count, width = hidden.shape
    heads = w_query.shape[1] // HD
    part = count // xs
    lanes = 128
    bf16, f32 = jnp.bfloat16, jnp.float32
    half = np.arange(HD // 2, dtype=np.float32)
    freqs = (10000.0 ** (-2.0 * half / HD)).astype(np.float32)
    freqs = jnp.asarray(np.concatenate([freqs, freqs])[None, :])
    dma = pltpu.SemaphoreType.DMA
    vmem = pl.BlockSpec(memory_space=pltpu.VMEM)
    smem = pl.BlockSpec(memory_space=pltpu.SMEM)
    hbm = pl.BlockSpec(memory_space=pl.ANY)
    out = pl.pallas_call(
        functools.partial(layer_kernel, sizes),
        out_shape=jax.ShapeDtypeStruct((xs, part, width // xs), bf16),
        in_specs=[smem, vmem, vmem, vmem, vmem, hbm, vmem, hbm, vmem, vmem, vmem, hbm, hbm],
        out_specs=vmem,
        scratch_shapes=[
            pltpu.VMEM(w_keyval.shape[1:], bf16),
            pltpu.VMEM((CORES, ys, zs, prefix.shape[0], 2 * HD), bf16),
            pltpu.VMEM((PAST + 1, 2, CORES, count, HD), bf16),
            pltpu.VMEM((xs,) + w_out.shape, bf16),
            pltpu.VMEM((heads, count, HD), bf16),
            pltpu.VMEM((1, count), jnp.int32),
            pltpu.VMEM((heads, 1, count), f32),
            pltpu.VMEM((heads, 1, count), f32),
            pltpu.VMEM((heads, HD, count), f32),
            pltpu.VMEM((xs, part, heads * HD), bf16),
            pltpu.VMEM((xs, part, heads * HD), bf16),
            pltpu.VMEM((part, width), bf16),
            pltpu.VMEM((zs, part, width), bf16),
            pltpu.VMEM((zs, 2 * ys, lanes), f32),
            pltpu.VMEM((zs, 2 * ys, lanes), f32),
            pltpu.VMEM((zs, ys, PIECE, width), bf16),
            pltpu.VMEM((zs, ys, PIECE, width), bf16),
            pltpu.VMEM((zs, ys, PIECE, width), bf16),
            pltpu.VMEM((zs, ys, PIECE, width), bf16),
            pltpu.VMEM((zs, PIECE, width), bf16),
            pltpu.VMEM((zs, PIECE, width), bf16),
            pltpu.VMEM((2,) + w_gateup.shape[1:], bf16),
            pltpu.VMEM((2,) + w_down.shape[1:], bf16),
            pltpu.VMEM((zs, part, width), f32),
            pltpu.VMEM((zs + 2, part // 2, width), bf16),
            pltpu.VMEM((zs + 2, part // 2, width), bf16),
            pltpu.VMEM((zs + 2, part // 2, width), bf16),
            pltpu.VMEM((zs + 2, part // 2, width), bf16),
            pltpu.VMEM((xs, part, width // xs), bf16),
            pltpu.VMEM((xs, part, width // xs), bf16),
            dma((4,)),
            dma((2, zs // 2)),
            dma((2, zs // 2)),
            dma((ys, 2)),
            dma((ys, 2)),
            dma((ys, 2)),
            dma((ys, 2)),
            dma((PAST, 2)),
            dma((PAST, 2)),
            dma((PAST + 1, 2)),
            dma((PAST + 1, 2)),
            dma((xs,)),
            dma((xs,)),
            dma((xs,)),
            dma((xs,)),
            dma((xs,)),
            dma((xs,)),
            dma((2,)),
            dma((2,)),
            dma((zs,)),
            dma((zs,)),
            dma((2, zs)),
            dma((2, zs)),
            dma((zs, ys)),
            dma((zs, ys)),
            dma((zs, ys)),
            dma((zs, ys)),
            dma((2, zs)),
            dma((2, zs)),
            dma((2, zs + 2)),
            dma((2, zs + 2)),
            dma((xs,)),
            dma((xs,)),
        ],
        compiler_params=pltpu.CompilerParams(
            collective_id=0, has_side_effects=True, vmem_limit_bytes=62 * 2**20
        ),
    )(
        lengths,
        hidden,
        gain,
        freqs,
        w_query,
        w_keyval,
        prefix,
        w_out,
        moe_gain,
        routes.T,
        weights.T,
        w_gateup,
        w_down,
    )
    return out.reshape(count, width // xs)


def shards(
    hidden_in,
    attn_gain,
    w_query,
    w_keyval,
    prefix_cache,
    w_out,
    moe_gain,
    w_gateup,
    w_down,
    routes,
    route_weights,
    lengths,
):
    chips_z = 8
    sizes = (lax.axis_size("head"), lax.axis_size("blk") // (CORES * chips_z), chips_z)
    return layer(
        sizes,
        hidden_in,
        attn_gain,
        w_query,
        w_keyval,
        prefix_cache,
        w_out,
        moe_gain,
        w_gateup,
        w_down,
        routes,
        route_weights,
        lengths,
    )


def solution(mesh):
    return jax.shard_map(
        shards,
        mesh=mesh,
        in_specs=(
            P("blk", None),
            P(),
            P(None, "head"),
            P(),
            P("blk", None, None),
            P("head", None),
            P(),
            P("blk", None, None),
            P("blk", None, None),
            P("blk", None),
            P("blk", None),
            P(),
        ),
        out_specs=P("blk", "head"),
        check_vma=False,
    )
```

```python
import functools
import jax
import jax.numpy as jnp
import numpy as np
from jax import lax
from jax.experimental import pallas as pl
from jax.experimental.pallas import tpu as pltpu
from jax.sharding import PartitionSpec as P

KVH = 2
HD = 128
PAST = 4
SPLIT = 4
MESH = pl.DeviceIdType.MESH
CORES = 2
ROWS_BLOCK = 64
PIECE = 16
ORDER = (0, 7, 1, 6, 2, 5, 3, 4)
PLACE = {rel: at for at, rel in enumerate(ORDER)}


def layer_kernel(
    sizes,
    lengths_ref,
    hidden_ref,
    gain_ref,
    freqs_ref,
    w_query_ref,
    w_keyval_ref,
    prefix_ref,
    w_out_ref,
    moe_gain_ref,
    routes_ref,
    weights_ref,
    gateup_ref,
    down_ref,
    out_ref,
    w_kv,
    cached,
    fresh,
    out_weights,
    query,
    begin,
    best,
    total,
    accum,
    context,
    contexts,
    mid_ref,
    tokens,
    table,
    tables,
    packed,
    rows,
    outs,
    backs,
    way_out,
    way_back,
    gate_up,
    down,
    partial,
    sums,
    got,
    final,
    landed,
    local_sem,
    pz_send,
    pz_recv,
    py_send,
    py_recv,
    pc_send,
    pc_recv,
    nz_send,
    nz_recv,
    nc_send,
    nc_recv,
    wx_send,
    wx_recv,
    wc_send,
    wc_recv,
    cx_send,
    cx_recv,
    ws_send,
    ws_recv,
    tsend,
    trecv,
    zsend,
    zrecv,
    ysend,
    yrecv,
    bsend,
    brecv,
    vsend,
    vrecv,
    ssend,
    srecv,
    xsend,
    xrecv,
):
    xs, ys, zs = sizes
    head = lax.axis_index("head")
    blk = lax.axis_index("blk")
    core = blk % CORES
    chip = blk // CORES
    z = chip % zs
    y = chip // zs
    count, width = hidden_ref.shape
    heads = query.shape[0]
    part = count // xs
    half = w_out_ref.shape[0] // CORES

    def at(dx=0, dy=0, dz=0, other=False):
        cc = 1 - core if other else core
        return (
            (head + dx) % xs,
            (((y + dy) % ys) * zs + (z + dz) % zs) * CORES + cc,
        )

    def along(step):
        return (head, ((chip + step) % (ys * zs)) * CORES + core)

    peers = (
        [at(other=True)]
        + [at(dz=d) for d in range(1, zs)]
        + [at(dy=d) for d in range(1, ys)]
        + [at(dx=d) for d in range(1, xs)]
        + [along(1), along(ys * zs - 1)]
    )
    barrier = pltpu.get_barrier_semaphore()
    for peer in peers:
        pl.semaphore_signal(barrier, inc=1, device_id=peer, device_id_type=MESH)

    def remote(source, target, send, recv, device):
        return pltpu.make_async_remote_copy(
            src_ref=source,
            dst_ref=target,
            send_sem=send,
            recv_sem=recv,
            device_id=device,
            device_id_type=MESH,
        )

    kv_copy = pltpu.make_async_copy(w_keyval_ref.at[head // (xs // KVH)], w_kv, local_sem.at[0])
    kv_copy.start()
    out_copy = pltpu.make_async_copy(w_out_ref, out_weights.at[0], local_sem.at[1])
    out_copy.start()
    own_copies = [
        pltpu.make_async_copy(gateup_ref.at[0], gate_up.at[0], local_sem.at[2]),
        pltpu.make_async_copy(down_ref.at[0], down.at[0], local_sem.at[3]),
    ]
    for copy in own_copies:
        copy.start()
    kv_head = head // (xs // KVH)
    piece = prefix_ref[:, 0, :]
    for g in range(1, KVH):
        piece = jnp.where(kv_head == g, prefix_ref[:, g, :], piece)
    cached[0, 0, 0] = piece
    pl.semaphore_wait(barrier, len(peers))

    sent = []

    def go(copy):
        copy.start()
        sent.append(copy)
        return copy

    def prefix_z(direction, step):
        held = (-step * direction) % zs
        there = (held - direction) % zs
        side = 0 if direction == 1 else 1
        return remote(
            cached.at[0, 0, PLACE[held]],
            cached.at[0, 0, PLACE[there]],
            pz_send.at[side, step],
            pz_recv.at[side, step],
            at(dz=direction),
        )

    batches = (pl.ds(0, SPLIT), pl.ds(SPLIT, zs - SPLIT))

    def prefix_y(held, direction, batch):
        there = (held - direction) % ys
        return remote(
            cached.at[0, held, batches[batch]],
            cached.at[0, there, batches[batch]],
            py_send.at[there, batch],
            py_recv.at[there, batch],
            at(dy=direction),
        )

    def prefix_core(held, batch):
        return remote(
            cached.at[0, held, batches[batch]],
            cached.at[1, held, batches[batch]],
            pc_send.at[held, batch],
            pc_recv.at[held, batch],
            at(other=True),
        )

    flow = {}
    flow[1, 0] = go(prefix_z(1, 0))
    flow[-1, 0] = go(prefix_z(-1, 0))

    mine = pl.ds(pl.multiple_of(core * half, 64), half)

    def weights_x(held, direction):
        there = (held - direction) % xs
        rows = mine
        if held != 0:
            offset = 0 if direction == 1 else half // 2
            rows = pl.ds(pl.multiple_of(core * half + offset, 32), half // 2)
        number = there if held == 0 else (0 if direction == 1 else 2)
        source = w_out_ref.at[rows] if held == 0 else out_weights.at[held, rows]
        return remote(
            source,
            out_weights.at[there, rows],
            wx_send.at[number],
            wx_recv.at[number],
            at(dx=direction),
        )

    def weights_core(held):
        return remote(
            out_weights.at[held, mine],
            out_weights.at[held, mine],
            wc_send.at[held],
            wc_recv.at[held],
            at(other=True),
        )

    out_ring = {3: go(weights_x(0, 1)), 1: go(weights_x(0, -1))}

    token = blk * count + lax.broadcasted_iota(jnp.int32, (count, HD), 0)
    start = jnp.zeros((count, HD), jnp.int32)
    end = jnp.int32(0)
    for r in range(lengths_ref.shape[0]):
        end = end + lengths_ref[r]
        start = jnp.where(token >= end, end, start)
    lane_token = blk * count + lax.broadcasted_iota(jnp.int32, (1, count), 1)
    lane_start = jnp.zeros((1, count), jnp.int32)
    end = jnp.int32(0)
    for r in range(lengths_ref.shape[0]):
        end = end + lengths_ref[r]
        lane_start = jnp.where(lane_token >= end, end, lane_start)
    begin[...] = lane_start
    prefix_total = cached.shape[0] * ys * zs * prefix_ref.shape[0]
    angle = (prefix_total + token - start).astype(jnp.float32) * freqs_ref[...]
    cosine = jnp.cos(angle)
    sine = jnp.sin(angle)
    lane = lax.broadcasted_iota(jnp.int32, (count, HD), 1)
    sine = jnp.where(lane < HD // 2, -sine, sine)

    def turned(vectors):
        return vectors * cosine + pltpu.roll(vectors, HD // 2, 1) * sine

    wide = hidden_ref[...].astype(jnp.float32)
    scale = lax.rsqrt(jnp.mean(wide * wide, axis=-1, keepdims=True) + 1e-05)
    normed = (wide * scale * gain_ref[...].reshape(1, width)).astype(jnp.bfloat16)
    kv_copy.wait()
    keyval = jnp.dot(normed, w_kv[...], preferred_element_type=jnp.float32)
    fresh[0, 0, 0] = turned(keyval[:, :HD]).astype(jnp.bfloat16)
    fresh[0, 1, 0] = keyval[:, HD:].astype(jnp.bfloat16)

    def fresh_next(distance, kind):
        return remote(
            fresh.at[distance, kind, 0],
            fresh.at[distance + 1, kind, 0],
            nz_send.at[distance, kind],
            nz_recv.at[distance, kind],
            along(1),
        )

    def fresh_core(distance, kind):
        return remote(
            fresh.at[distance, kind, 0],
            fresh.at[distance, kind, 1],
            nc_send.at[distance, kind],
            nc_recv.at[distance, kind],
            at(other=True),
        )

    chain = {}
    shared = {}
    for kind in range(2):
        chain[0, kind] = go(fresh_next(0, kind))
    for kind in range(2):
        shared[0, kind] = go(fresh_core(0, kind))

    def prefix_step(step):
        for direction in (1, -1):
            if (direction, step - 1) in flow:
                flow[direction, step - 1].wait_recv()
            if step < zs // 2 - (0 if direction == 1 else 1):
                flow[direction, step] = go(prefix_z(direction, step))

    def fresh_step(distance, kind):
        chain[distance - 1, kind].wait_recv()
        if distance < PAST:
            chain[distance, kind] = go(fresh_next(distance, kind))
        shared[distance, kind] = go(fresh_core(distance, kind))

    prefix_step(1)
    queries = jnp.dot(normed, w_query_ref[...], preferred_element_type=jnp.float32)
    for j in range(heads):
        query[j] = (turned(queries[:, j * HD : (j + 1) * HD]) * HD ** (-0.5)).astype(jnp.bfloat16)
    lanes = table.shape[2]
    def quarter_of(ref):
        return pltpu.roll(ref[...], (xs - head) % xs * part, 1)[:, :lanes]

    row = lax.broadcasted_iota(jnp.int32, (zs * 2 * ys, lanes), 0)
    wanted = quarter_of(routes_ref)
    wanted = jnp.where(lax.broadcasted_iota(jnp.int32, wanted.shape, 1) < part, wanted, -1)
    given = quarter_of(weights_ref)
    group = row % (2 * ys)
    expert = ((y + group % ys) % ys) * zs + row // (2 * ys)
    hit = jnp.zeros((zs * 2 * ys, lanes), jnp.float32)
    weight = jnp.zeros((zs * 2 * ys, lanes), jnp.float32)
    for k in range(routes_ref.shape[0]):
        same = wanted[k : k + 1, :] == expert
        hit = hit + jnp.where(same, 1.0, 0.0)
        weight = weight + jnp.where(same, given[k : k + 1, :], 0.0)
    before = jnp.where(
        lax.broadcasted_iota(jnp.int32, (lanes, lanes), 0)
        < lax.broadcasted_iota(jnp.int32, (lanes, lanes), 1),
        1.0,
        0.0,
    )
    rank = jnp.dot(
        hit.astype(jnp.bfloat16),
        before.astype(jnp.bfloat16),
        preferred_element_type=jnp.float32,
    )
    code = jnp.where(group < ys, jnp.where(hit > 0.5, rank, -1.0), weight)
    table[...] = code.reshape(zs, 2 * ys, lanes)
    tables[0] = table[z]
    table_copies = {}
    for d in range(1, zs):
        table_copies[d] = go(
            remote(
                table.at[(z + d) % zs],
                tables.at[PLACE[zs - d]],
                tsend.at[d],
                trecv.at[zs - d],
                at(dz=d),
            )
        )

    best[...] = jnp.full(best.shape, -1e30, jnp.float32)
    total[...] = jnp.zeros(total.shape, jnp.float32)
    accum[...] = jnp.zeros(accum.shape, jnp.float32)

    def attend(keys, values, distance=None):
        length = keys.shape[0]
        turned_values = jnp.transpose(values)
        if distance is not None:
            place = lax.broadcasted_iota(jnp.int32, (length, 1), 0)
            own_block = (blk - CORES * distance) * count
            other_block = (blk + 1 - 2 * core - CORES * distance) * count
            where = jnp.where(place < count, own_block + place, other_block + place - count)

        def one_head(j, carry):
            scores = lax.dot_general(
                keys, query[j], (((1,), (1,)), ((), ())), preferred_element_type=jnp.float32
            )
            if distance is not None:
                valid = where >= begin[...]
                if distance == 0:
                    valid = valid & (where <= lane_token)
                scores = jnp.where(valid, scores, -1e30)
            old = best[j]
            new = jnp.maximum(old, jnp.max(scores, axis=0, keepdims=True))
            weights = jnp.exp(scores - new)
            rescale = jnp.exp(old - new)
            best[j] = new
            total[j] = total[j] * rescale + jnp.sum(weights, axis=0, keepdims=True)
            accum[j] = accum[j] * rescale + jnp.dot(
                turned_values, weights.astype(jnp.bfloat16), preferred_element_type=jnp.float32
            )
            return carry

        lax.fori_loop(0, heads, one_head, 0)

    def attend_fresh(distance):
        for kind in range(2):
            shared[distance, kind].wait_recv()
        attend(
            fresh[distance, 0].reshape(CORES * count, HD),
            fresh[distance, 1].reshape(CORES * count, HD),
            distance,
        )

    def attend_cached(*names):
        pieces = []
        for side, held, batch in names:
            if side == 1:
                onchip[held, batch].wait_recv()
            piece = cached[side, held, batches[batch]]
            piece = piece.reshape(batches[batch].size * prefix_ref.shape[0], 2 * HD)
            pieces.append(piece)
        whole = jnp.concatenate(pieces, axis=0)
        attend(whole[:, :HD], whole[:, HD:])

    ride = {}
    onchip = {}

    def prefix_share(held, batch):
        onchip[held, batch] = go(prefix_core(held, batch))

    def prefix_row(batch):
        for direction in (1, -1):
            ride[(-direction) % ys, batch] = go(prefix_y(0, direction, batch))
        prefix_share(0, batch)

    def prefix_arrived(batch):
        ride[ys - 1, batch].wait_recv()
        if batch == 0:
            ride[2, batch] = go(prefix_y(ys - 1, 1, batch))
        ride[1, batch].wait_recv()
        if batch == 1:
            ride[2, batch] = go(prefix_y(1, -1, batch))
        prefix_share(ys - 1, batch)
        prefix_share(1, batch)

    attend_fresh(0)
    prefix_step(2)
    prefix_row(0)
    fresh_step(1, 0)
    fresh_step(1, 1)
    attend_cached((0, 0, 0), (1, 0, 0))
    prefix_step(3)
    attend_fresh(1)
    fresh_step(2, 0)
    fresh_step(2, 1)
    prefix_step(4)
    prefix_row(1)
    prefix_arrived(0)
    attend_cached((0, ys - 1, 0), (0, 1, 0))
    attend_cached((0, 0, 1), (1, 0, 1))
    fresh_step(3, 0)
    fresh_step(3, 1)
    attend_fresh(2)
    prefix_arrived(1)
    out_ring[3].wait_recv()
    relay_right = go(weights_x(3, 1))
    out_ring[1].wait_recv()
    relay_left = go(weights_x(1, -1))
    out_shared = {held: go(weights_core(held)) for held in (3, 1)}
    attend_cached((1, ys - 1, 0), (1, 1, 0))
    fresh_step(4, 0)
    fresh_step(4, 1)
    attend_cached((0, ys - 1, 1), (0, 1, 1))
    ride[2, 0].wait_recv()
    prefix_share(2, 0)
    attend_cached((1, ys - 1, 1), (1, 1, 1))
    ride[2, 1].wait_recv()
    prefix_share(2, 1)
    attend_fresh(3)
    weight_copies = [
        go(remote(gateup_ref.at[0], gate_up.at[1], ws_send.at[0], ws_recv.at[0], at(other=True))),
        go(remote(down_ref.at[0], down.at[1], ws_send.at[1], ws_recv.at[1], at(other=True))),
    ]
    attend_cached((0, 2, 0), (0, 2, 1))
    attend_fresh(4)
    relay_right.wait_recv()
    relay_left.wait_recv()
    out_shared[2] = go(weights_core(2))
    attend_cached((1, 2, 0), (1, 2, 1))

    for j in range(heads):
        value = jnp.transpose(accum[j] / total[j]).astype(jnp.bfloat16)
        context[:, :, j * HD : (j + 1) * HD] = value.reshape(xs, part, HD)
    crossing = {}
    for dx in (2, 1, 3):
        crossing[xs - dx] = go(
            remote(
                context.at[(head + dx) % xs],
                contexts.at[xs - dx],
                cx_send.at[dx],
                cx_recv.at[xs - dx],
                at(dx=dx),
            )
        )
    contexts[0] = context[head]
    out_copy.wait()

    def term(held):
        return jnp.dot(contexts[held], out_weights[held], preferred_element_type=jnp.float32)

    value = hidden_ref[pl.ds(pl.multiple_of(head * part, part), part)].astype(jnp.float32)
    attn = term(0)
    for held in (3, 1, 2):
        out_shared[held].wait_recv()
        crossing[held].wait_recv()
        attn = attn + term(held)
    middle = (value + attn).astype(jnp.bfloat16)
    mid_ref[...] = middle
    wide = middle.astype(jnp.float32)
    scale = lax.rsqrt(jnp.mean(wide * wide, axis=-1, keepdims=True) + 1e-05)
    tokens[0] = (wide * scale * moe_gain_ref[...].reshape(1, width)).astype(jnp.bfloat16)
    half_units = down.shape[1]
    split = width // 2
    chunk = ROWS_BLOCK // 2

    def token_copy(direction, step, piece):
        held = (-step * direction) % zs
        there = (held - direction) % zs
        number = step * 2 + piece
        side = 0 if direction == 1 else 1
        return pltpu.make_async_remote_copy(
            src_ref=tokens.at[PLACE[held], pl.ds(piece * chunk, chunk)],
            dst_ref=tokens.at[PLACE[there], pl.ds(piece * chunk, chunk)],
            send_sem=zsend.at[side, number],
            recv_sem=zrecv.at[side, number],
            device_id=at(dz=direction),
            device_id_type=MESH,
        )

    reach = zs // 2
    flow = {}
    for direction in (1, -1):
        for step in range(reach):
            for piece in range(2):
                if step < reach - 1 or piece == (0 if direction == 1 else 1):
                    flow[direction, step, piece] = token_copy(direction, step, piece)

    for piece in range(2):
        go(flow[1, 0, piece])
        go(flow[-1, 0, piece])

    slot = lax.broadcasted_iota(jnp.int32, (ys * PIECE, lanes), 0) % PIECE
    slot = slot.astype(jnp.float32)

    def spread(place, first):
        return jnp.concatenate(
            [
                jnp.broadcast_to(tables[place, first + dy : first + dy + 1, :], (PIECE, lanes))
                for dy in range(ys)
            ],
            axis=0,
        )

    def side_of(place):
        return 1 if (place + place // zs) % 2 == 0 else -1

    def y_copies(source, target, way, number, send, recv):
        def direct(place, dy):
            return remote(
                source.at[place, dy],
                target.at[place, ys - dy],
                send.at[place, dy],
                recv.at[place, ys - dy],
                at(dy=dy),
            )

        def first_leg(place):
            return remote(
                source.at[place, 2],
                way.at[place],
                vsend.at[number, place],
                vrecv.at[number, place],
                at(dy=side_of(place)),
            )

        def second_leg(place):
            return remote(
                way.at[place],
                target.at[place, 2],
                send.at[place, 2],
                recv.at[place, 2],
                at(dy=side_of(place)),
            )

        def start(place):
            go(direct(place, 2) if place % zs == zs - 1 else first_leg(place))
            go(direct(place, 1))
            go(direct(place, ys - 1))

        def relay(*places):
            for place in places:
                first_leg(place).wait_recv()
                go(second_leg(place))

        def arrived(place):
            direct(place, 1).wait_recv()
            direct(place, ys - 1).wait_recv()
            (direct(place, 2) if place % zs == zs - 1 else second_leg(place)).wait_recv()

        return start, relay, arrived

    send_pieces, relay_pieces, pieces_here = y_copies(packed, rows, way_out, 0, ysend, yrecv)
    send_backs, relay_backs, backs_here = y_copies(outs, backs, way_back, 1, bsend, brecv)

    def pack(place):
        if place > 0:
            table_copies[(zs - ORDER[place])].wait_recv()
        chosen = jnp.where(spread(place, 0) == slot, 1.0, 0.0).astype(jnp.bfloat16)
        value = jnp.dot(
            chosen[:, :ROWS_BLOCK], tokens[place], preferred_element_type=jnp.float32
        ).astype(jnp.bfloat16)
        value = value.reshape(ys, PIECE, width)
        packed[place, 1:] = value[1:]
        rows[place, 0] = value[0]
        send_pieces(place)

    def experts(first, count):
        for place in range(first, first + count):
            pieces_here(place)
        taken = rows[first : first + count].reshape(count * ys * PIECE, width)
        hidden = []
        for side in range(2):
            both = jnp.dot(taken, gate_up[side], preferred_element_type=jnp.float32)
            both = jax.nn.relu(both[:, :half_units]) * both[:, half_units:]
            hidden.append(both.astype(jnp.bfloat16))
        for columns in range(2):
            span = slice(columns * split, (columns + 1) * split)
            value = jnp.dot(hidden[0], down[0, :, span], preferred_element_type=jnp.float32)
            value = value + jnp.dot(
                hidden[1], down[1, :, span], preferred_element_type=jnp.float32
            )
            value = value.astype(jnp.bfloat16).reshape(count, ys, PIECE, split)
            base = columns * zs + first
            outs[base : base + count, 1:] = value[:, 1:]
            backs[base : base + count, 0] = value[:, 0]
        for place in reversed(range(first, first + count)):
            send_backs(place)

    def combine(place):
        backs_here(place)
        mixing = jnp.where(
            spread(place % zs, 0) == slot, spread(place % zs, ys), 0.0
        ).astype(jnp.bfloat16)[:, :ROWS_BLOCK]
        partial[place] = lax.dot_general(
            mixing,
            backs[place].reshape(ys * PIECE, split),
            (((0,), (0,)), ((), ())),
            preferred_element_type=jnp.float32,
        )

    def tokens_step(step):
        for piece in range(2):
            for direction in (1, -1):
                if (direction, step - 1, piece) in flow:
                    flow[direction, step - 1, piece].wait_recv()
                if (direction, step, piece) in flow:
                    go(flow[direction, step, piece])

    pack(0)
    tokens_step(1)
    relay_pieces(0)
    pack(1)
    pack(2)
    for copy in own_copies:
        copy.wait()
    for copy in weight_copies:
        copy.wait_recv()
    tokens_step(2)
    relay_pieces(1, 2)
    pack(3)
    pack(4)
    tokens_step(3)
    relay_pieces(3, 4)
    pack(5)
    pack(6)
    experts(0, 3)
    tokens_step(4)
    relay_pieces(5, 6)
    pack(7)
    relay_backs(0, 1, 2)
    experts(3, 2)
    combine(0)
    combine(1)
    combine(2)
    relay_backs(3, 4)
    experts(5, 3)
    for place in reversed(range(zs)):
        send_backs(zs + place)
    combine(3)
    combine(4)
    relay_backs(6, 5)

    returned = {}

    def pass_on(columns, direction, distance, piece):
        held = distance if direction == 1 else zs - distance
        number = distance * 2 + piece
        side = columns * 2 + (0 if direction == 1 else 1)
        value = partial[columns * zs + PLACE[held], pl.ds(piece * chunk, chunk)]
        before_it = returned.get((columns, direction, distance + 1, piece))
        if before_it is not None:
            before_it.wait_recv()
            value = value + got[side, number + 2].astype(jnp.float32)
        sums[side, number] = value.astype(jnp.bfloat16)
        returned[columns, direction, distance, piece] = go(
            remote(
                sums.at[side, number],
                got.at[side, number],
                ssend.at[side, number],
                srecv.at[side, number],
                at(dz=direction),
            )
        )

    def far_sums(columns):
        combine(columns * zs + PLACE[reach])
        pass_on(columns, 1, reach, 0)
        pass_on(columns, -1, reach, 1)
        combine(columns * zs + PLACE[reach - 1])
        pass_on(columns, 1, reach - 1, 1)
        combine(columns * zs + PLACE[zs - reach + 1])
        pass_on(columns, -1, reach - 1, 0)

    def near_sums(columns, distance):
        if distance < reach - 1:
            pass_on(columns, 1, distance, 1)
            pass_on(columns, -1, distance, 0)
        pass_on(columns, 1, distance, 0)
        pass_on(columns, -1, distance, 1)

    def finish(columns):
        share = width // xs
        for piece in (1, 0):
            spot = pl.ds(piece * chunk, chunk)
            for direction in (1, -1):
                returned[columns, direction, 1, piece].wait_recv()
            value = (
                mid_ref[spot, columns * split : (columns + 1) * split].astype(jnp.float32)
                + partial[columns * zs, spot]
                + got[columns * 2, 2 + piece].astype(jnp.float32)
                + got[columns * 2 + 1, 2 + piece].astype(jnp.float32)
            ).astype(jnp.bfloat16)
            for number in range(split // share):
                final[columns * (split // share) + number, spot] = value[
                    :, number * share : (number + 1) * share
                ]

    far_sums(0)
    relay_backs(zs + 6, zs + 5)
    near_sums(0, 3)
    relay_backs(zs + 4, zs + 3)
    near_sums(0, 2)
    relay_backs(zs + 2, zs + 1, zs)
    far_sums(1)
    near_sums(0, 1)
    combine(zs + 4)
    combine(zs + 3)
    near_sums(1, 3)
    combine(zs + 2)
    combine(zs + 1)
    combine(zs)
    finish(0)
    near_sums(1, 2)
    near_sums(1, 1)
    finish(1)

    last = []
    for dx in range(1, xs):
        copy = pltpu.make_async_remote_copy(
            src_ref=final.at[(head + dx) % xs],
            dst_ref=landed.at[head],
            send_sem=xsend.at[dx],
            recv_sem=xrecv.at[xs - dx],
            device_id=at(dx=dx),
            device_id_type=MESH,
        )
        go(copy)
        last.append(copy)
    out_ref[head] = final[head]
    for dx in range(1, xs):
        last[xs - dx - 1].wait_recv()
        out_ref[(head + dx) % xs] = landed[(head + dx) % xs]

    for copy in sent:
        copy.wait_send()


def layer(
    sizes,
    hidden,
    gain,
    w_query,
    w_keyval,
    prefix,
    w_out,
    moe_gain,
    w_gateup,
    w_down,
    routes,
    weights,
    lengths,
):
    xs, ys, zs = sizes
    count, width = hidden.shape
    heads = w_query.shape[1] // HD
    part = count // xs
    lanes = 128
    bf16, f32 = jnp.bfloat16, jnp.float32
    half = np.arange(HD // 2, dtype=np.float32)
    freqs = (10000.0 ** (-2.0 * half / HD)).astype(np.float32)
    freqs = jnp.asarray(np.concatenate([freqs, freqs])[None, :])
    dma = pltpu.SemaphoreType.DMA
    vmem = pl.BlockSpec(memory_space=pltpu.VMEM)
    smem = pl.BlockSpec(memory_space=pltpu.SMEM)
    hbm = pl.BlockSpec(memory_space=pl.ANY)
    out = pl.pallas_call(
        functools.partial(layer_kernel, sizes),
        out_shape=jax.ShapeDtypeStruct((xs, part, width // xs), bf16),
        in_specs=[smem, vmem, vmem, vmem, vmem, hbm, vmem, hbm, vmem, vmem, vmem, hbm, hbm],
        out_specs=vmem,
        scratch_shapes=[
            pltpu.VMEM(w_keyval.shape[1:], bf16),
            pltpu.VMEM((CORES, ys, zs, prefix.shape[0], 2 * HD), bf16),
            pltpu.VMEM((PAST + 1, 2, CORES, count, HD), bf16),
            pltpu.VMEM((xs,) + w_out.shape, bf16),
            pltpu.VMEM((heads, count, HD), bf16),
            pltpu.VMEM((1, count), jnp.int32),
            pltpu.VMEM((heads, 1, count), f32),
            pltpu.VMEM((heads, 1, count), f32),
            pltpu.VMEM((heads, HD, count), f32),
            pltpu.VMEM((xs, part, heads * HD), bf16),
            pltpu.VMEM((xs, part, heads * HD), bf16),
            pltpu.VMEM((part, width), bf16),
            pltpu.VMEM((zs, part, width), bf16),
            pltpu.VMEM((zs, 2 * ys, lanes), f32),
            pltpu.VMEM((zs, 2 * ys, lanes), f32),
            pltpu.VMEM((zs, ys, PIECE, width), bf16),
            pltpu.VMEM((zs, ys, PIECE, width), bf16),
            pltpu.VMEM((2 * zs, ys, PIECE, width // 2), bf16),
            pltpu.VMEM((2 * zs, ys, PIECE, width // 2), bf16),
            pltpu.VMEM((zs, PIECE, width), bf16),
            pltpu.VMEM((2 * zs, PIECE, width // 2), bf16),
            pltpu.VMEM((2,) + w_gateup.shape[1:], bf16),
            pltpu.VMEM((2,) + w_down.shape[1:], bf16),
            pltpu.VMEM((2 * zs, part, width // 2), f32),
            pltpu.VMEM((4, zs + 2, part // 2, width // 2), bf16),
            pltpu.VMEM((4, zs + 2, part // 2, width // 2), bf16),
            pltpu.VMEM((xs, part, width // xs), bf16),
            pltpu.VMEM((xs, part, width // xs), bf16),
            dma((4,)),
            dma((2, zs // 2)),
            dma((2, zs // 2)),
            dma((ys, 2)),
            dma((ys, 2)),
            dma((ys, 2)),
            dma((ys, 2)),
            dma((PAST, 2)),
            dma((PAST, 2)),
            dma((PAST + 1, 2)),
            dma((PAST + 1, 2)),
            dma((xs,)),
            dma((xs,)),
            dma((xs,)),
            dma((xs,)),
            dma((xs,)),
            dma((xs,)),
            dma((2,)),
            dma((2,)),
            dma((zs,)),
            dma((zs,)),
            dma((2, zs)),
            dma((2, zs)),
            dma((zs, ys)),
            dma((zs, ys)),
            dma((2 * zs, ys)),
            dma((2 * zs, ys)),
            dma((2, 2 * zs)),
            dma((2, 2 * zs)),
            dma((4, zs + 2)),
            dma((4, zs + 2)),
            dma((xs,)),
            dma((xs,)),
        ],
        compiler_params=pltpu.CompilerParams(
            collective_id=0, has_side_effects=True, vmem_limit_bytes=62 * 2**20
        ),
    )(
        lengths,
        hidden,
        gain,
        freqs,
        w_query,
        w_keyval,
        prefix,
        w_out,
        moe_gain,
        routes.T,
        weights.T,
        w_gateup,
        w_down,
    )
    return out.reshape(count, width // xs)


def shards(
    hidden_in,
    attn_gain,
    w_query,
    w_keyval,
    prefix_cache,
    w_out,
    moe_gain,
    w_gateup,
    w_down,
    routes,
    route_weights,
    lengths,
):
    chips_z = 8
    sizes = (lax.axis_size("head"), lax.axis_size("blk") // (CORES * chips_z), chips_z)
    return layer(
        sizes,
        hidden_in,
        attn_gain,
        w_query,
        w_keyval,
        prefix_cache,
        w_out,
        moe_gain,
        w_gateup,
        w_down,
        routes,
        route_weights,
        lengths,
    )


def solution(mesh):
    return jax.shard_map(
        shards,
        mesh=mesh,
        in_specs=(
            P("blk", None),
            P(),
            P(None, "head"),
            P(),
            P("blk", None, None),
            P("head", None),
            P(),
            P("blk", None, None),
            P("blk", None, None),
            P("blk", None),
            P("blk", None),
            P(),
        ),
        out_specs=P("blk", "head"),
        check_vma=False,
    )
```

```python
import functools
import jax
import jax.numpy as jnp
import numpy as np
from jax import lax
from jax.experimental import pallas as pl
from jax.experimental.pallas import tpu as pltpu
from jax.sharding import PartitionSpec as P

KVH = 2
HD = 128
PAST = 4
SPLIT = 4
MESH = pl.DeviceIdType.MESH
CORES = 2
ROWS_BLOCK = 64
PIECE = 16
ORDER = (0, 7, 1, 6, 2, 5, 3, 4)
PLACE = {rel: at for at, rel in enumerate(ORDER)}


def layer_kernel(
    sizes,
    lengths_ref,
    hidden_ref,
    gain_ref,
    freqs_ref,
    w_query_ref,
    w_keyval_ref,
    prefix_ref,
    w_out_ref,
    moe_gain_ref,
    routes_ref,
    weights_ref,
    gateup_ref,
    down_ref,
    out_ref,
    w_kv,
    cached,
    fresh,
    out_weights,
    query,
    begin,
    best,
    total,
    accum,
    context,
    terms,
    terms_in,
    mid_ref,
    tokens,
    table,
    tables,
    packed,
    rows,
    outs,
    backs,
    way_out,
    way_back,
    gate_up,
    down,
    partial,
    sums,
    got,
    final,
    landed,
    local_sem,
    pz_send,
    pz_recv,
    py_send,
    py_recv,
    pc_send,
    pc_recv,
    nz_send,
    nz_recv,
    nc_send,
    nc_recv,
    cx_send,
    cx_recv,
    ws_send,
    ws_recv,
    tsend,
    trecv,
    zsend,
    zrecv,
    ysend,
    yrecv,
    bsend,
    brecv,
    vsend,
    vrecv,
    ssend,
    srecv,
    xsend,
    xrecv,
):
    xs, ys, zs = sizes
    head = lax.axis_index("head")
    blk = lax.axis_index("blk")
    core = blk % CORES
    chip = blk // CORES
    z = chip % zs
    y = chip // zs
    count, width = hidden_ref.shape
    heads = query.shape[0]
    part = count // xs

    def at(dx=0, dy=0, dz=0, other=False):
        cc = 1 - core if other else core
        return (
            (head + dx) % xs,
            (((y + dy) % ys) * zs + (z + dz) % zs) * CORES + cc,
        )

    def along(step):
        return (head, ((chip + step) % (ys * zs)) * CORES + core)

    peers = (
        [at(other=True)]
        + [at(dz=d) for d in range(1, zs)]
        + [at(dy=d) for d in range(1, ys)]
        + [at(dx=d) for d in range(1, xs)]
        + [along(1), along(ys * zs - 1)]
    )
    barrier = pltpu.get_barrier_semaphore()
    for peer in peers:
        pl.semaphore_signal(barrier, inc=1, device_id=peer, device_id_type=MESH)

    def remote(source, target, send, recv, device):
        return pltpu.make_async_remote_copy(
            src_ref=source,
            dst_ref=target,
            send_sem=send,
            recv_sem=recv,
            device_id=device,
            device_id_type=MESH,
        )

    kv_copy = pltpu.make_async_copy(w_keyval_ref.at[head // (xs // KVH)], w_kv, local_sem.at[0])
    kv_copy.start()
    out_copy = pltpu.make_async_copy(w_out_ref, out_weights, local_sem.at[1])
    out_copy.start()
    own_copies = [
        pltpu.make_async_copy(gateup_ref.at[0], gate_up.at[0], local_sem.at[2]),
        pltpu.make_async_copy(down_ref.at[0], down.at[0], local_sem.at[3]),
    ]
    for copy in own_copies:
        copy.start()
    kv_head = head // (xs // KVH)
    piece = prefix_ref[:, 0, :]
    for g in range(1, KVH):
        piece = jnp.where(kv_head == g, prefix_ref[:, g, :], piece)
    cached[0, 0, 0] = piece
    pl.semaphore_wait(barrier, len(peers))

    sent = []

    def go(copy):
        copy.start()
        sent.append(copy)
        return copy

    def prefix_z(direction, step):
        held = (-step * direction) % zs
        there = (held - direction) % zs
        side = 0 if direction == 1 else 1
        return remote(
            cached.at[0, 0, PLACE[held]],
            cached.at[0, 0, PLACE[there]],
            pz_send.at[side, step],
            pz_recv.at[side, step],
            at(dz=direction),
        )

    batches = (pl.ds(0, SPLIT), pl.ds(SPLIT, zs - SPLIT))

    def prefix_y(held, direction, batch):
        there = (held - direction) % ys
        return remote(
            cached.at[0, held, batches[batch]],
            cached.at[0, there, batches[batch]],
            py_send.at[there, batch],
            py_recv.at[there, batch],
            at(dy=direction),
        )

    def prefix_core(held, batch):
        return remote(
            cached.at[0, held, batches[batch]],
            cached.at[1, held, batches[batch]],
            pc_send.at[held, batch],
            pc_recv.at[held, batch],
            at(other=True),
        )

    flow = {}
    flow[1, 0] = go(prefix_z(1, 0))
    flow[-1, 0] = go(prefix_z(-1, 0))

    token = blk * count + lax.broadcasted_iota(jnp.int32, (count, HD), 0)
    start = jnp.zeros((count, HD), jnp.int32)
    end = jnp.int32(0)
    for r in range(lengths_ref.shape[0]):
        end = end + lengths_ref[r]
        start = jnp.where(token >= end, end, start)
    lane_token = blk * count + lax.broadcasted_iota(jnp.int32, (1, count), 1)
    lane_start = jnp.zeros((1, count), jnp.int32)
    end = jnp.int32(0)
    for r in range(lengths_ref.shape[0]):
        end = end + lengths_ref[r]
        lane_start = jnp.where(lane_token >= end, end, lane_start)
    begin[...] = lane_start
    prefix_total = cached.shape[0] * ys * zs * prefix_ref.shape[0]
    angle = (prefix_total + token - start).astype(jnp.float32) * freqs_ref[...]
    cosine = jnp.cos(angle)
    sine = jnp.sin(angle)
    lane = lax.broadcasted_iota(jnp.int32, (count, HD), 1)
    sine = jnp.where(lane < HD // 2, -sine, sine)

    def turned(vectors):
        return vectors * cosine + pltpu.roll(vectors, HD // 2, 1) * sine

    wide = hidden_ref[...].astype(jnp.float32)
    scale = lax.rsqrt(jnp.mean(wide * wide, axis=-1, keepdims=True) + 1e-05)
    normed = (wide * scale * gain_ref[...].reshape(1, width)).astype(jnp.bfloat16)
    kv_copy.wait()
    keyval = jnp.dot(normed, w_kv[...], preferred_element_type=jnp.float32)
    fresh[0, 0, 0] = turned(keyval[:, :HD]).astype(jnp.bfloat16)
    fresh[0, 1, 0] = keyval[:, HD:].astype(jnp.bfloat16)

    def fresh_next(distance, kind):
        return remote(
            fresh.at[distance, kind, 0],
            fresh.at[distance + 1, kind, 0],
            nz_send.at[distance, kind],
            nz_recv.at[distance, kind],
            along(1),
        )

    def fresh_core(distance, kind):
        return remote(
            fresh.at[distance, kind, 0],
            fresh.at[distance, kind, 1],
            nc_send.at[distance, kind],
            nc_recv.at[distance, kind],
            at(other=True),
        )

    chain = {}
    shared = {}
    for kind in range(2):
        chain[0, kind] = go(fresh_next(0, kind))
    for kind in range(2):
        shared[0, kind] = go(fresh_core(0, kind))

    def prefix_step(step):
        for direction in (1, -1):
            if (direction, step - 1) in flow:
                flow[direction, step - 1].wait_recv()
            if step < zs // 2 - (0 if direction == 1 else 1):
                flow[direction, step] = go(prefix_z(direction, step))

    def fresh_step(distance, kind):
        chain[distance - 1, kind].wait_recv()
        if distance < PAST:
            chain[distance, kind] = go(fresh_next(distance, kind))
        shared[distance, kind] = go(fresh_core(distance, kind))

    prefix_step(1)
    queries = jnp.dot(normed, w_query_ref[...], preferred_element_type=jnp.float32)
    for j in range(heads):
        query[j] = (turned(queries[:, j * HD : (j + 1) * HD]) * HD ** (-0.5)).astype(jnp.bfloat16)
    lanes = table.shape[2]
    def quarter_of(ref):
        return pltpu.roll(ref[...], (xs - head) % xs * part, 1)[:, :lanes]

    row = lax.broadcasted_iota(jnp.int32, (zs * 2 * ys, lanes), 0)
    wanted = quarter_of(routes_ref)
    wanted = jnp.where(lax.broadcasted_iota(jnp.int32, wanted.shape, 1) < part, wanted, -1)
    given = quarter_of(weights_ref)
    group = row % (2 * ys)
    expert = ((y + group % ys) % ys) * zs + row // (2 * ys)
    hit = jnp.zeros((zs * 2 * ys, lanes), jnp.float32)
    weight = jnp.zeros((zs * 2 * ys, lanes), jnp.float32)
    for k in range(routes_ref.shape[0]):
        same = wanted[k : k + 1, :] == expert
        hit = hit + jnp.where(same, 1.0, 0.0)
        weight = weight + jnp.where(same, given[k : k + 1, :], 0.0)
    before = jnp.where(
        lax.broadcasted_iota(jnp.int32, (lanes, lanes), 0)
        < lax.broadcasted_iota(jnp.int32, (lanes, lanes), 1),
        1.0,
        0.0,
    )
    rank = jnp.dot(
        hit.astype(jnp.bfloat16),
        before.astype(jnp.bfloat16),
        preferred_element_type=jnp.float32,
    )
    code = jnp.where(group < ys, jnp.where(hit > 0.5, rank, -1.0), weight)
    table[...] = code.reshape(zs, 2 * ys, lanes)
    tables[0] = table[z]
    table_copies = {}
    for d in range(1, zs):
        table_copies[d] = go(
            remote(
                table.at[(z + d) % zs],
                tables.at[PLACE[zs - d]],
                tsend.at[d],
                trecv.at[zs - d],
                at(dz=d),
            )
        )

    best[...] = jnp.full(best.shape, -1e30, jnp.float32)
    total[...] = jnp.zeros(total.shape, jnp.float32)
    accum[...] = jnp.zeros(accum.shape, jnp.float32)

    def attend(keys, values, distance=None):
        length = keys.shape[0]
        turned_values = jnp.transpose(values)
        if distance is not None:
            place = lax.broadcasted_iota(jnp.int32, (length, 1), 0)
            own_block = (blk - CORES * distance) * count
            other_block = (blk + 1 - 2 * core - CORES * distance) * count
            where = jnp.where(place < count, own_block + place, other_block + place - count)

        def one_head(j, carry):
            scores = lax.dot_general(
                keys, query[j], (((1,), (1,)), ((), ())), preferred_element_type=jnp.float32
            )
            if distance is not None:
                valid = where >= begin[...]
                if distance == 0:
                    valid = valid & (where <= lane_token)
                scores = jnp.where(valid, scores, -1e30)
            old = best[j]
            new = jnp.maximum(old, jnp.max(scores, axis=0, keepdims=True))
            weights = jnp.exp(scores - new)
            rescale = jnp.exp(old - new)
            best[j] = new
            total[j] = total[j] * rescale + jnp.sum(weights, axis=0, keepdims=True)
            accum[j] = accum[j] * rescale + jnp.dot(
                turned_values, weights.astype(jnp.bfloat16), preferred_element_type=jnp.float32
            )
            return carry

        lax.fori_loop(0, heads, one_head, 0)

    def attend_fresh(distance):
        for kind in range(2):
            shared[distance, kind].wait_recv()
        attend(
            fresh[distance, 0].reshape(CORES * count, HD),
            fresh[distance, 1].reshape(CORES * count, HD),
            distance,
        )

    def attend_cached(*names):
        pieces = []
        for side, held, batch in names:
            if side == 1:
                onchip[held, batch].wait_recv()
            piece = cached[side, held, batches[batch]]
            piece = piece.reshape(batches[batch].size * prefix_ref.shape[0], 2 * HD)
            pieces.append(piece)
        whole = jnp.concatenate(pieces, axis=0)
        attend(whole[:, :HD], whole[:, HD:])

    ride = {}
    onchip = {}

    def prefix_share(held, batch):
        onchip[held, batch] = go(prefix_core(held, batch))

    def prefix_row(batch):
        for direction in (1, -1):
            ride[(-direction) % ys, batch] = go(prefix_y(0, direction, batch))
        prefix_share(0, batch)

    def prefix_arrived(batch):
        ride[ys - 1, batch].wait_recv()
        if batch == 0:
            ride[2, batch] = go(prefix_y(ys - 1, 1, batch))
        ride[1, batch].wait_recv()
        if batch == 1:
            ride[2, batch] = go(prefix_y(1, -1, batch))
        prefix_share(ys - 1, batch)
        prefix_share(1, batch)

    attend_fresh(0)
    prefix_step(2)
    prefix_row(0)
    fresh_step(1, 0)
    fresh_step(1, 1)
    attend_cached((0, 0, 0), (1, 0, 0))
    prefix_step(3)
    attend_fresh(1)
    fresh_step(2, 0)
    fresh_step(2, 1)
    prefix_step(4)
    prefix_row(1)
    prefix_arrived(0)
    attend_cached((0, ys - 1, 0), (0, 1, 0))
    attend_cached((0, 0, 1), (1, 0, 1))
    fresh_step(3, 0)
    fresh_step(3, 1)
    attend_fresh(2)
    prefix_arrived(1)
    attend_cached((1, ys - 1, 0), (1, 1, 0))
    fresh_step(4, 0)
    fresh_step(4, 1)
    attend_cached((0, ys - 1, 1), (0, 1, 1))
    ride[2, 0].wait_recv()
    prefix_share(2, 0)
    attend_cached((1, ys - 1, 1), (1, 1, 1))
    ride[2, 1].wait_recv()
    prefix_share(2, 1)
    attend_fresh(3)
    weight_copies = [
        go(remote(gateup_ref.at[0], gate_up.at[1], ws_send.at[0], ws_recv.at[0], at(other=True))),
        go(remote(down_ref.at[0], down.at[1], ws_send.at[1], ws_recv.at[1], at(other=True))),
    ]
    attend_cached((0, 2, 0), (0, 2, 1))
    attend_fresh(4)
    attend_cached((1, 2, 0), (1, 2, 1))

    for j in range(heads):
        value = jnp.transpose(accum[j] / total[j]).astype(jnp.bfloat16)
        context[:, :, j * HD : (j + 1) * HD] = value.reshape(xs, part, HD)
    out_copy.wait()
    piece_rows = part // 2

    def term(dx):
        return jnp.dot(
            context[(head + dx) % xs], out_weights[...], preferred_element_type=jnp.float32
        )

    def send_terms(number, value, dx):
        terms[number] = value.astype(jnp.bfloat16)
        return go(
            remote(
                terms.at[number],
                terms_in.at[number],
                cx_send.at[number],
                cx_recv.at[number],
                at(dx=dx),
            )
        )

    value = term(2)
    crossing = [send_terms(0, value[:piece_rows], 1), send_terms(1, value[piece_rows:], -1)]
    right = term(1)
    crossing.append(send_terms(2, right[piece_rows:], 1))
    left = term(-1)
    crossing.append(send_terms(3, left[:piece_rows], -1))
    crossing[0].wait_recv()
    value = right[:piece_rows] + terms_in[0].astype(jnp.float32)
    crossing.append(send_terms(4, value, 1))
    crossing[1].wait_recv()
    value = left[piece_rows:] + terms_in[1].astype(jnp.float32)
    crossing.append(send_terms(5, value, -1))
    value = hidden_ref[pl.ds(pl.multiple_of(head * part, part), part)].astype(jnp.float32)
    value = value + term(0)
    for number in range(2, 6):
        crossing[number].wait_recv()
    attn = jnp.concatenate(
        [
            terms_in[3].astype(jnp.float32) + terms_in[4].astype(jnp.float32),
            terms_in[2].astype(jnp.float32) + terms_in[5].astype(jnp.float32),
        ],
        axis=0,
    )
    middle = (value + attn).astype(jnp.bfloat16)
    mid_ref[...] = middle
    wide = middle.astype(jnp.float32)
    scale = lax.rsqrt(jnp.mean(wide * wide, axis=-1, keepdims=True) + 1e-05)
    tokens[0] = (wide * scale * moe_gain_ref[...].reshape(1, width)).astype(jnp.bfloat16)
    half_units = down.shape[1]
    split = width // 2
    chunk = ROWS_BLOCK // 2

    def token_copy(direction, step, piece):
        held = (-step * direction) % zs
        there = (held - direction) % zs
        number = step * 2 + piece
        side = 0 if direction == 1 else 1
        return pltpu.make_async_remote_copy(
            src_ref=tokens.at[PLACE[held], pl.ds(piece * chunk, chunk)],
            dst_ref=tokens.at[PLACE[there], pl.ds(piece * chunk, chunk)],
            send_sem=zsend.at[side, number],
            recv_sem=zrecv.at[side, number],
            device_id=at(dz=direction),
            device_id_type=MESH,
        )

    reach = zs // 2
    flow = {}
    for direction in (1, -1):
        for step in range(reach):
            for piece in range(2):
                if step < reach - 1 or piece == (0 if direction == 1 else 1):
                    flow[direction, step, piece] = token_copy(direction, step, piece)

    for piece in range(2):
        go(flow[1, 0, piece])
        go(flow[-1, 0, piece])

    slot = lax.broadcasted_iota(jnp.int32, (ys * PIECE, lanes), 0) % PIECE
    slot = slot.astype(jnp.float32)

    def spread(place, first):
        return jnp.concatenate(
            [
                jnp.broadcast_to(tables[place, first + dy : first + dy + 1, :], (PIECE, lanes))
                for dy in range(ys)
            ],
            axis=0,
        )

    def side_of(place):
        return 1 if (place + place // zs) % 2 == 0 else -1

    def y_copies(source, target, way, number, send, recv):
        def direct(place, dy):
            return remote(
                source.at[place, dy],
                target.at[place, ys - dy],
                send.at[place, dy],
                recv.at[place, ys - dy],
                at(dy=dy),
            )

        def first_leg(place):
            return remote(
                source.at[place, 2],
                way.at[place],
                vsend.at[number, place],
                vrecv.at[number, place],
                at(dy=side_of(place)),
            )

        def second_leg(place):
            return remote(
                way.at[place],
                target.at[place, 2],
                send.at[place, 2],
                recv.at[place, 2],
                at(dy=side_of(place)),
            )

        def start(place):
            go(direct(place, 2) if place % zs == zs - 1 else first_leg(place))
            go(direct(place, 1))
            go(direct(place, ys - 1))

        def relay(*places):
            for place in places:
                first_leg(place).wait_recv()
                go(second_leg(place))

        def arrived(place):
            direct(place, 1).wait_recv()
            direct(place, ys - 1).wait_recv()
            (direct(place, 2) if place % zs == zs - 1 else second_leg(place)).wait_recv()

        return start, relay, arrived

    send_pieces, relay_pieces, pieces_here = y_copies(packed, rows, way_out, 0, ysend, yrecv)
    send_backs, relay_backs, backs_here = y_copies(outs, backs, way_back, 1, bsend, brecv)

    def pack(place):
        if place > 0:
            table_copies[(zs - ORDER[place])].wait_recv()
        chosen = jnp.where(spread(place, 0) == slot, 1.0, 0.0).astype(jnp.bfloat16)
        value = jnp.dot(
            chosen[:, :ROWS_BLOCK], tokens[place], preferred_element_type=jnp.float32
        ).astype(jnp.bfloat16)
        value = value.reshape(ys, PIECE, width)
        packed[place, 1:] = value[1:]
        rows[place, 0] = value[0]
        send_pieces(place)

    def experts(first, count):
        for place in range(first, first + count):
            pieces_here(place)
        taken = rows[first : first + count].reshape(count * ys * PIECE, width)
        hidden = []
        for side in range(2):
            both = jnp.dot(taken, gate_up[side], preferred_element_type=jnp.float32)
            both = jax.nn.relu(both[:, :half_units]) * both[:, half_units:]
            hidden.append(both.astype(jnp.bfloat16))
        for columns in range(2):
            span = slice(columns * split, (columns + 1) * split)
            value = jnp.dot(hidden[0], down[0, :, span], preferred_element_type=jnp.float32)
            value = value + jnp.dot(
                hidden[1], down[1, :, span], preferred_element_type=jnp.float32
            )
            value = value.astype(jnp.bfloat16).reshape(count, ys, PIECE, split)
            base = columns * zs + first
            outs[base : base + count, 1:] = value[:, 1:]
            backs[base : base + count, 0] = value[:, 0]
        for place in reversed(range(first, first + count)):
            send_backs(place)

    def combine(place):
        backs_here(place)
        mixing = jnp.where(
            spread(place % zs, 0) == slot, spread(place % zs, ys), 0.0
        ).astype(jnp.bfloat16)[:, :ROWS_BLOCK]
        partial[place] = lax.dot_general(
            mixing,
            backs[place].reshape(ys * PIECE, split),
            (((0,), (0,)), ((), ())),
            preferred_element_type=jnp.float32,
        )

    def tokens_step(step):
        for piece in range(2):
            for direction in (1, -1):
                if (direction, step - 1, piece) in flow:
                    flow[direction, step - 1, piece].wait_recv()
                if (direction, step, piece) in flow:
                    go(flow[direction, step, piece])

    pack(0)
    tokens_step(1)
    relay_pieces(0)
    pack(1)
    pack(2)
    for copy in own_copies:
        copy.wait()
    for copy in weight_copies:
        copy.wait_recv()
    tokens_step(2)
    relay_pieces(1, 2)
    pack(3)
    pack(4)
    tokens_step(3)
    relay_pieces(3, 4)
    pack(5)
    pack(6)
    experts(0, 3)
    tokens_step(4)
    relay_pieces(5, 6)
    pack(7)
    relay_backs(0, 1, 2)
    experts(3, 2)
    combine(0)
    combine(1)
    combine(2)
    relay_backs(3, 4)
    experts(5, 3)
    for place in reversed(range(zs)):
        send_backs(zs + place)
    combine(3)
    combine(4)
    relay_backs(6, 5)

    returned = {}

    def pass_on(columns, direction, distance, piece):
        held = distance if direction == 1 else zs - distance
        number = distance * 2 + piece
        side = columns * 2 + (0 if direction == 1 else 1)
        value = partial[columns * zs + PLACE[held], pl.ds(piece * chunk, chunk)]
        before_it = returned.get((columns, direction, distance + 1, piece))
        if before_it is not None:
            before_it.wait_recv()
            value = value + got[side, number + 2].astype(jnp.float32)
        sums[side, number] = value.astype(jnp.bfloat16)
        returned[columns, direction, distance, piece] = go(
            remote(
                sums.at[side, number],
                got.at[side, number],
                ssend.at[side, number],
                srecv.at[side, number],
                at(dz=direction),
            )
        )

    def far_sums(columns):
        combine(columns * zs + PLACE[reach])
        pass_on(columns, 1, reach, 0)
        pass_on(columns, -1, reach, 1)
        combine(columns * zs + PLACE[reach - 1])
        pass_on(columns, 1, reach - 1, 1)
        combine(columns * zs + PLACE[zs - reach + 1])
        pass_on(columns, -1, reach - 1, 0)

    def near_sums(columns, distance):
        if distance < reach - 1:
            pass_on(columns, 1, distance, 1)
            pass_on(columns, -1, distance, 0)
        pass_on(columns, 1, distance, 0)
        pass_on(columns, -1, distance, 1)

    def finish(columns):
        share = width // xs
        for piece in (1, 0):
            spot = pl.ds(piece * chunk, chunk)
            for direction in (1, -1):
                returned[columns, direction, 1, piece].wait_recv()
            value = (
                mid_ref[spot, columns * split : (columns + 1) * split].astype(jnp.float32)
                + partial[columns * zs, spot]
                + got[columns * 2, 2 + piece].astype(jnp.float32)
                + got[columns * 2 + 1, 2 + piece].astype(jnp.float32)
            ).astype(jnp.bfloat16)
            for number in range(split // share):
                final[columns * (split // share) + number, spot] = value[
                    :, number * share : (number + 1) * share
                ]

    far_sums(0)
    relay_backs(zs + 6, zs + 5)
    near_sums(0, 3)
    relay_backs(zs + 4, zs + 3)
    near_sums(0, 2)
    relay_backs(zs + 2, zs + 1, zs)
    far_sums(1)
    near_sums(0, 1)
    combine(zs + 4)
    combine(zs + 3)
    near_sums(1, 3)
    combine(zs + 2)
    combine(zs + 1)
    combine(zs)
    finish(0)
    near_sums(1, 2)
    near_sums(1, 1)
    finish(1)

    last = []
    for dx in range(1, xs):
        copy = pltpu.make_async_remote_copy(
            src_ref=final.at[(head + dx) % xs],
            dst_ref=landed.at[head],
            send_sem=xsend.at[dx],
            recv_sem=xrecv.at[xs - dx],
            device_id=at(dx=dx),
            device_id_type=MESH,
        )
        go(copy)
        last.append(copy)
    out_ref[head] = final[head]
    for dx in range(1, xs):
        last[xs - dx - 1].wait_recv()
        out_ref[(head + dx) % xs] = landed[(head + dx) % xs]

    for copy in sent:
        copy.wait_send()


def layer(
    sizes,
    hidden,
    gain,
    w_query,
    w_keyval,
    prefix,
    w_out,
    moe_gain,
    w_gateup,
    w_down,
    routes,
    weights,
    lengths,
):
    xs, ys, zs = sizes
    count, width = hidden.shape
    heads = w_query.shape[1] // HD
    part = count // xs
    lanes = 128
    bf16, f32 = jnp.bfloat16, jnp.float32
    half = np.arange(HD // 2, dtype=np.float32)
    freqs = (10000.0 ** (-2.0 * half / HD)).astype(np.float32)
    freqs = jnp.asarray(np.concatenate([freqs, freqs])[None, :])
    dma = pltpu.SemaphoreType.DMA
    vmem = pl.BlockSpec(memory_space=pltpu.VMEM)
    smem = pl.BlockSpec(memory_space=pltpu.SMEM)
    hbm = pl.BlockSpec(memory_space=pl.ANY)
    out = pl.pallas_call(
        functools.partial(layer_kernel, sizes),
        out_shape=jax.ShapeDtypeStruct((xs, part, width // xs), bf16),
        in_specs=[smem, vmem, vmem, vmem, vmem, hbm, vmem, hbm, vmem, vmem, vmem, hbm, hbm],
        out_specs=vmem,
        scratch_shapes=[
            pltpu.VMEM(w_keyval.shape[1:], bf16),
            pltpu.VMEM((CORES, ys, zs, prefix.shape[0], 2 * HD), bf16),
            pltpu.VMEM((PAST + 1, 2, CORES, count, HD), bf16),
            pltpu.VMEM(w_out.shape, bf16),
            pltpu.VMEM((heads, count, HD), bf16),
            pltpu.VMEM((1, count), jnp.int32),
            pltpu.VMEM((heads, 1, count), f32),
            pltpu.VMEM((heads, 1, count), f32),
            pltpu.VMEM((heads, HD, count), f32),
            pltpu.VMEM((xs, part, heads * HD), bf16),
            pltpu.VMEM((6, part // 2, width), bf16),
            pltpu.VMEM((6, part // 2, width), bf16),
            pltpu.VMEM((part, width), bf16),
            pltpu.VMEM((zs, part, width), bf16),
            pltpu.VMEM((zs, 2 * ys, lanes), f32),
            pltpu.VMEM((zs, 2 * ys, lanes), f32),
            pltpu.VMEM((zs, ys, PIECE, width), bf16),
            pltpu.VMEM((zs, ys, PIECE, width), bf16),
            pltpu.VMEM((2 * zs, ys, PIECE, width // 2), bf16),
            pltpu.VMEM((2 * zs, ys, PIECE, width // 2), bf16),
            pltpu.VMEM((zs, PIECE, width), bf16),
            pltpu.VMEM((2 * zs, PIECE, width // 2), bf16),
            pltpu.VMEM((2,) + w_gateup.shape[1:], bf16),
            pltpu.VMEM((2,) + w_down.shape[1:], bf16),
            pltpu.VMEM((2 * zs, part, width // 2), f32),
            pltpu.VMEM((4, zs + 2, part // 2, width // 2), bf16),
            pltpu.VMEM((4, zs + 2, part // 2, width // 2), bf16),
            pltpu.VMEM((xs, part, width // xs), bf16),
            pltpu.VMEM((xs, part, width // xs), bf16),
            dma((4,)),
            dma((2, zs // 2)),
            dma((2, zs // 2)),
            dma((ys, 2)),
            dma((ys, 2)),
            dma((ys, 2)),
            dma((ys, 2)),
            dma((PAST, 2)),
            dma((PAST, 2)),
            dma((PAST + 1, 2)),
            dma((PAST + 1, 2)),
            dma((6,)),
            dma((6,)),
            dma((2,)),
            dma((2,)),
            dma((zs,)),
            dma((zs,)),
            dma((2, zs)),
            dma((2, zs)),
            dma((zs, ys)),
            dma((zs, ys)),
            dma((2 * zs, ys)),
            dma((2 * zs, ys)),
            dma((2, 2 * zs)),
            dma((2, 2 * zs)),
            dma((4, zs + 2)),
            dma((4, zs + 2)),
            dma((xs,)),
            dma((xs,)),
        ],
        compiler_params=pltpu.CompilerParams(
            collective_id=0, has_side_effects=True, vmem_limit_bytes=62 * 2**20
        ),
    )(
        lengths,
        hidden,
        gain,
        freqs,
        w_query,
        w_keyval,
        prefix,
        w_out,
        moe_gain,
        routes.T,
        weights.T,
        w_gateup,
        w_down,
    )
    return out.reshape(count, width // xs)


def shards(
    hidden_in,
    attn_gain,
    w_query,
    w_keyval,
    prefix_cache,
    w_out,
    moe_gain,
    w_gateup,
    w_down,
    routes,
    route_weights,
    lengths,
):
    chips_z = 8
    sizes = (lax.axis_size("head"), lax.axis_size("blk") // (CORES * chips_z), chips_z)
    return layer(
        sizes,
        hidden_in,
        attn_gain,
        w_query,
        w_keyval,
        prefix_cache,
        w_out,
        moe_gain,
        w_gateup,
        w_down,
        routes,
        route_weights,
        lengths,
    )


def solution(mesh):
    return jax.shard_map(
        shards,
        mesh=mesh,
        in_specs=(
            P("blk", None),
            P(),
            P(None, "head"),
            P(),
            P("blk", None, None),
            P("head", None),
            P(),
            P("blk", None, None),
            P("blk", None, None),
            P("blk", None),
            P("blk", None),
            P(),
        ),
        out_specs=P("blk", "head"),
        check_vma=False,
    )
```

```python
import functools
import jax
import jax.numpy as jnp
import numpy as np
from jax import lax
from jax.experimental import pallas as pl
from jax.experimental.pallas import tpu as pltpu
from jax.sharding import PartitionSpec as P

KVH = 2
HD = 128
PAST = 4
SPLIT = 4
MESH = pl.DeviceIdType.MESH
CORES = 2
ROWS_BLOCK = 64
PIECE = 16
ORDER = (0, 7, 1, 6, 2, 5, 3, 4)
PLACE = {rel: at for at, rel in enumerate(ORDER)}


def layer_kernel(
    sizes,
    lengths_ref,
    hidden_ref,
    gain_ref,
    freqs_ref,
    w_query_ref,
    w_keyval_ref,
    prefix_ref,
    w_out_ref,
    moe_gain_ref,
    routes_ref,
    weights_ref,
    gateup_ref,
    down_ref,
    out_ref,
    w_kv,
    cached,
    fresh,
    out_weights,
    query,
    begin,
    best,
    total,
    accum,
    context,
    contexts,
    mid_ref,
    tokens,
    table,
    tables,
    packed,
    rows,
    outs,
    backs,
    way_out,
    way_back,
    gate_up,
    down,
    partial,
    sums,
    got,
    final,
    local_sem,
    pz_send,
    pz_recv,
    py_send,
    py_recv,
    pc_send,
    pc_recv,
    nz_send,
    nz_recv,
    nc_send,
    nc_recv,
    wx_send,
    wx_recv,
    wc_send,
    wc_recv,
    cx_send,
    cx_recv,
    ws_send,
    ws_recv,
    tsend,
    trecv,
    zsend,
    zrecv,
    ysend,
    yrecv,
    bsend,
    brecv,
    vsend,
    vrecv,
    ssend,
    srecv,
    xsend,
    xrecv,
):
    xs, ys, zs = sizes
    head = lax.axis_index("head")
    blk = lax.axis_index("blk")
    core = blk % CORES
    chip = blk // CORES
    z = chip % zs
    y = chip // zs
    count, width = hidden_ref.shape
    heads = query.shape[0]
    part = count // xs
    half = w_out_ref.shape[0] // CORES

    def at(dx=0, dy=0, dz=0, other=False):
        cc = 1 - core if other else core
        return (
            (head + dx) % xs,
            (((y + dy) % ys) * zs + (z + dz) % zs) * CORES + cc,
        )

    def along(step):
        return (head, ((chip + step) % (ys * zs)) * CORES + core)

    peers = (
        [at(other=True)]
        + [at(dz=d) for d in range(1, zs)]
        + [at(dy=d) for d in range(1, ys)]
        + [at(dx=d) for d in range(1, xs)]
        + [along(1), along(ys * zs - 1)]
    )
    barrier = pltpu.get_barrier_semaphore()
    for peer in peers:
        pl.semaphore_signal(barrier, inc=1, device_id=peer, device_id_type=MESH)

    def remote(source, target, send, recv, device):
        return pltpu.make_async_remote_copy(
            src_ref=source,
            dst_ref=target,
            send_sem=send,
            recv_sem=recv,
            device_id=device,
            device_id_type=MESH,
        )

    kv_copy = pltpu.make_async_copy(w_keyval_ref.at[head // (xs // KVH)], w_kv, local_sem.at[0])
    kv_copy.start()
    out_copy = pltpu.make_async_copy(w_out_ref, out_weights.at[0], local_sem.at[1])
    out_copy.start()
    own_copies = [
        pltpu.make_async_copy(gateup_ref.at[0], gate_up.at[0], local_sem.at[2]),
        pltpu.make_async_copy(down_ref.at[0], down.at[0], local_sem.at[3]),
    ]
    for copy in own_copies:
        copy.start()
    kv_head = head // (xs // KVH)
    piece = prefix_ref[:, 0, :]
    for g in range(1, KVH):
        piece = jnp.where(kv_head == g, prefix_ref[:, g, :], piece)
    cached[0, 0, 0] = piece
    pl.semaphore_wait(barrier, len(peers))

    sent = []

    def go(copy):
        copy.start()
        sent.append(copy)
        return copy

    def prefix_z(direction, step):
        held = (-step * direction) % zs
        there = (held - direction) % zs
        side = 0 if direction == 1 else 1
        return remote(
            cached.at[0, 0, PLACE[held]],
            cached.at[0, 0, PLACE[there]],
            pz_send.at[side, step],
            pz_recv.at[side, step],
            at(dz=direction),
        )

    batches = (pl.ds(0, SPLIT), pl.ds(SPLIT, zs - SPLIT))

    def prefix_y(held, direction, batch):
        there = (held - direction) % ys
        return remote(
            cached.at[0, held, batches[batch]],
            cached.at[0, there, batches[batch]],
            py_send.at[there, batch],
            py_recv.at[there, batch],
            at(dy=direction),
        )

    def prefix_core(held, batch):
        return remote(
            cached.at[0, held, batches[batch]],
            cached.at[1, held, batches[batch]],
            pc_send.at[held, batch],
            pc_recv.at[held, batch],
            at(other=True),
        )

    flow = {}
    flow[1, 0] = go(prefix_z(1, 0))
    flow[-1, 0] = go(prefix_z(-1, 0))

    mine = pl.ds(pl.multiple_of(core * half, 64), half)

    def weights_x(held, direction):
        there = (held - direction) % xs
        rows = mine
        if held != 0:
            offset = 0 if direction == 1 else half // 2
            rows = pl.ds(pl.multiple_of(core * half + offset, 32), half // 2)
        number = there if held == 0 else (0 if direction == 1 else 2)
        source = w_out_ref.at[rows] if held == 0 else out_weights.at[held, rows]
        return remote(
            source,
            out_weights.at[there, rows],
            wx_send.at[number],
            wx_recv.at[number],
            at(dx=direction),
        )

    def weights_core(held):
        return remote(
            out_weights.at[held, mine],
            out_weights.at[held, mine],
            wc_send.at[held],
            wc_recv.at[held],
            at(other=True),
        )

    out_ring = {3: go(weights_x(0, 1)), 1: go(weights_x(0, -1))}

    token = blk * count + lax.broadcasted_iota(jnp.int32, (count, HD), 0)
    start = jnp.zeros((count, HD), jnp.int32)
    end = jnp.int32(0)
    for r in range(lengths_ref.shape[0]):
        end = end + lengths_ref[r]
        start = jnp.where(token >= end, end, start)
    lane_token = blk * count + lax.broadcasted_iota(jnp.int32, (1, count), 1)
    lane_start = jnp.zeros((1, count), jnp.int32)
    end = jnp.int32(0)
    for r in range(lengths_ref.shape[0]):
        end = end + lengths_ref[r]
        lane_start = jnp.where(lane_token >= end, end, lane_start)
    begin[...] = lane_start
    prefix_total = cached.shape[0] * ys * zs * prefix_ref.shape[0]
    angle = (prefix_total + token - start).astype(jnp.float32) * freqs_ref[...]
    cosine = jnp.cos(angle)
    sine = jnp.sin(angle)
    lane = lax.broadcasted_iota(jnp.int32, (count, HD), 1)
    sine = jnp.where(lane < HD // 2, -sine, sine)

    def turned(vectors):
        return vectors * cosine + pltpu.roll(vectors, HD // 2, 1) * sine

    wide = hidden_ref[...].astype(jnp.float32)
    scale = lax.rsqrt(jnp.mean(wide * wide, axis=-1, keepdims=True) + 1e-05)
    normed = (wide * scale * gain_ref[...].reshape(1, width)).astype(jnp.bfloat16)
    kv_copy.wait()
    keyval = jnp.dot(normed, w_kv[...], preferred_element_type=jnp.float32)
    fresh[0, 0, 0] = turned(keyval[:, :HD]).astype(jnp.bfloat16)
    fresh[0, 1, 0] = keyval[:, HD:].astype(jnp.bfloat16)

    def fresh_next(distance, kind):
        return remote(
            fresh.at[distance, kind, 0],
            fresh.at[distance + 1, kind, 0],
            nz_send.at[distance, kind],
            nz_recv.at[distance, kind],
            along(1),
        )

    def fresh_core(distance, kind):
        return remote(
            fresh.at[distance, kind, 0],
            fresh.at[distance, kind, 1],
            nc_send.at[distance, kind],
            nc_recv.at[distance, kind],
            at(other=True),
        )

    chain = {}
    shared = {}
    for kind in range(2):
        chain[0, kind] = go(fresh_next(0, kind))
    for kind in range(2):
        shared[0, kind] = go(fresh_core(0, kind))

    def prefix_step(step):
        for direction in (1, -1):
            if (direction, step - 1) in flow:
                flow[direction, step - 1].wait_recv()
            if step < zs // 2 - (0 if direction == 1 else 1):
                flow[direction, step] = go(prefix_z(direction, step))

    def fresh_step(distance, kind):
        chain[distance - 1, kind].wait_recv()
        if distance < PAST:
            chain[distance, kind] = go(fresh_next(distance, kind))
        shared[distance, kind] = go(fresh_core(distance, kind))

    prefix_step(1)
    queries = jnp.dot(normed, w_query_ref[...], preferred_element_type=jnp.float32)
    for j in range(heads):
        query[j] = (turned(queries[:, j * HD : (j + 1) * HD]) * HD ** (-0.5)).astype(jnp.bfloat16)
    lanes = table.shape[2]
    def quarter_of(ref):
        return pltpu.roll(ref[...], (xs - head) % xs * part, 1)[:, :lanes]

    row = lax.broadcasted_iota(jnp.int32, (zs * 2 * ys, lanes), 0)
    wanted = quarter_of(routes_ref)
    wanted = jnp.where(lax.broadcasted_iota(jnp.int32, wanted.shape, 1) < part, wanted, -1)
    given = quarter_of(weights_ref)
    group = row % (2 * ys)
    expert = ((y + group % ys) % ys) * zs + row // (2 * ys)
    hit = jnp.zeros((zs * 2 * ys, lanes), jnp.float32)
    weight = jnp.zeros((zs * 2 * ys, lanes), jnp.float32)
    for k in range(routes_ref.shape[0]):
        same = wanted[k : k + 1, :] == expert
        hit = hit + jnp.where(same, 1.0, 0.0)
        weight = weight + jnp.where(same, given[k : k + 1, :], 0.0)
    before = jnp.where(
        lax.broadcasted_iota(jnp.int32, (lanes, lanes), 0)
        < lax.broadcasted_iota(jnp.int32, (lanes, lanes), 1),
        1.0,
        0.0,
    )
    rank = jnp.dot(
        hit.astype(jnp.bfloat16),
        before.astype(jnp.bfloat16),
        preferred_element_type=jnp.float32,
    )
    code = jnp.where(group < ys, jnp.where(hit > 0.5, rank, -1.0), weight)
    table[...] = code.reshape(zs, 2 * ys, lanes)
    tables[0] = table[z]
    table_copies = {}
    for d in range(1, zs):
        table_copies[d] = go(
            remote(
                table.at[(z + d) % zs],
                tables.at[PLACE[zs - d]],
                tsend.at[d],
                trecv.at[zs - d],
                at(dz=d),
            )
        )

    best[...] = jnp.full(best.shape, -1e30, jnp.float32)
    total[...] = jnp.zeros(total.shape, jnp.float32)
    accum[...] = jnp.zeros(accum.shape, jnp.float32)

    def attend(keys, values, distance=None):
        length = keys.shape[0]
        turned_values = jnp.transpose(values)
        if distance is not None:
            place = lax.broadcasted_iota(jnp.int32, (length, 1), 0)
            own_block = (blk - CORES * distance) * count
            other_block = (blk + 1 - 2 * core - CORES * distance) * count
            where = jnp.where(place < count, own_block + place, other_block + place - count)

        def one_head(j, carry):
            scores = lax.dot_general(
                keys, query[j], (((1,), (1,)), ((), ())), preferred_element_type=jnp.float32
            )
            if distance is not None:
                valid = where >= begin[...]
                if distance == 0:
                    valid = valid & (where <= lane_token)
                scores = jnp.where(valid, scores, -1e30)
            old = best[j]
            new = jnp.maximum(old, jnp.max(scores, axis=0, keepdims=True))
            weights = jnp.exp(scores - new)
            rescale = jnp.exp(old - new)
            best[j] = new
            total[j] = total[j] * rescale + jnp.sum(weights, axis=0, keepdims=True)
            accum[j] = accum[j] * rescale + jnp.dot(
                turned_values, weights.astype(jnp.bfloat16), preferred_element_type=jnp.float32
            )
            return carry

        lax.fori_loop(0, heads, one_head, 0)

    def attend_fresh(distance):
        for kind in range(2):
            shared[distance, kind].wait_recv()
        attend(
            fresh[distance, 0].reshape(CORES * count, HD),
            fresh[distance, 1].reshape(CORES * count, HD),
            distance,
        )

    def attend_cached(*names):
        pieces = []
        for side, held, batch in names:
            if side == 1:
                onchip[held, batch].wait_recv()
            piece = cached[side, held, batches[batch]]
            piece = piece.reshape(batches[batch].size * prefix_ref.shape[0], 2 * HD)
            pieces.append(piece)
        whole = jnp.concatenate(pieces, axis=0)
        attend(whole[:, :HD], whole[:, HD:])

    ride = {}
    onchip = {}

    def prefix_share(held, batch):
        onchip[held, batch] = go(prefix_core(held, batch))

    def prefix_row(batch):
        for direction in (1, -1):
            ride[(-direction) % ys, batch] = go(prefix_y(0, direction, batch))
        prefix_share(0, batch)

    def prefix_arrived(batch):
        ride[ys - 1, batch].wait_recv()
        if batch == 0:
            ride[2, batch] = go(prefix_y(ys - 1, 1, batch))
        ride[1, batch].wait_recv()
        if batch == 1:
            ride[2, batch] = go(prefix_y(1, -1, batch))
        prefix_share(ys - 1, batch)
        prefix_share(1, batch)

    attend_fresh(0)
    prefix_step(2)
    prefix_row(0)
    fresh_step(1, 0)
    fresh_step(1, 1)
    attend_cached((0, 0, 0), (1, 0, 0))
    prefix_step(3)
    attend_fresh(1)
    fresh_step(2, 0)
    fresh_step(2, 1)
    prefix_step(4)
    prefix_row(1)
    prefix_arrived(0)
    attend_cached((0, ys - 1, 0), (0, 1, 0))
    attend_cached((0, 0, 1), (1, 0, 1))
    fresh_step(3, 0)
    fresh_step(3, 1)
    attend_fresh(2)
    prefix_arrived(1)
    out_ring[3].wait_recv()
    relay_right = go(weights_x(3, 1))
    out_ring[1].wait_recv()
    relay_left = go(weights_x(1, -1))
    out_shared = {held: go(weights_core(held)) for held in (3, 1)}
    attend_cached((1, ys - 1, 0), (1, 1, 0))
    fresh_step(4, 0)
    fresh_step(4, 1)
    attend_cached((0, ys - 1, 1), (0, 1, 1))
    ride[2, 0].wait_recv()
    prefix_share(2, 0)
    attend_cached((1, ys - 1, 1), (1, 1, 1))
    ride[2, 1].wait_recv()
    prefix_share(2, 1)
    attend_fresh(3)
    weight_copies = [
        go(remote(gateup_ref.at[0], gate_up.at[1], ws_send.at[0], ws_recv.at[0], at(other=True))),
        go(remote(down_ref.at[0], down.at[1], ws_send.at[1], ws_recv.at[1], at(other=True))),
    ]
    attend_cached((0, 2, 0), (0, 2, 1))
    attend_fresh(4)
    relay_right.wait_recv()
    relay_left.wait_recv()
    out_shared[2] = go(weights_core(2))
    attend_cached((1, 2, 0), (1, 2, 1))

    for j in range(heads):
        value = jnp.transpose(accum[j] / total[j]).astype(jnp.bfloat16)
        context[:, :, j * HD : (j + 1) * HD] = value.reshape(xs, part, HD)
    crossing = {}
    for dx in (2, 1, 3):
        crossing[xs - dx] = go(
            remote(
                context.at[(head + dx) % xs],
                contexts.at[xs - dx],
                cx_send.at[dx],
                cx_recv.at[xs - dx],
                at(dx=dx),
            )
        )
    contexts[0] = context[head]
    out_copy.wait()

    def term(held):
        return jnp.dot(contexts[held], out_weights[held], preferred_element_type=jnp.float32)

    value = hidden_ref[pl.ds(pl.multiple_of(head * part, part), part)].astype(jnp.float32)
    attn = term(0)
    for held in (3, 1, 2):
        out_shared[held].wait_recv()
        crossing[held].wait_recv()
        attn = attn + term(held)
    middle = (value + attn).astype(jnp.bfloat16)
    mid_ref[...] = middle
    wide = middle.astype(jnp.float32)
    scale = lax.rsqrt(jnp.mean(wide * wide, axis=-1, keepdims=True) + 1e-05)
    tokens[0] = (wide * scale * moe_gain_ref[...].reshape(1, width)).astype(jnp.bfloat16)
    half_units = down.shape[1]
    split = width // 2
    chunk = ROWS_BLOCK // 2

    def token_copy(direction, step, piece):
        held = (-step * direction) % zs
        there = (held - direction) % zs
        number = step * 2 + piece
        side = 0 if direction == 1 else 1
        return pltpu.make_async_remote_copy(
            src_ref=tokens.at[PLACE[held], pl.ds(piece * chunk, chunk)],
            dst_ref=tokens.at[PLACE[there], pl.ds(piece * chunk, chunk)],
            send_sem=zsend.at[side, number],
            recv_sem=zrecv.at[side, number],
            device_id=at(dz=direction),
            device_id_type=MESH,
        )

    reach = zs // 2
    flow = {}
    for direction in (1, -1):
        for step in range(reach):
            for piece in range(2):
                if step < reach - 1 or piece == (0 if direction == 1 else 1):
                    flow[direction, step, piece] = token_copy(direction, step, piece)

    for piece in range(2):
        go(flow[1, 0, piece])
        go(flow[-1, 0, piece])

    slot = lax.broadcasted_iota(jnp.int32, (ys * PIECE, lanes), 0) % PIECE
    slot = slot.astype(jnp.float32)

    def spread(place, first):
        return jnp.concatenate(
            [
                jnp.broadcast_to(tables[place, first + dy : first + dy + 1, :], (PIECE, lanes))
                for dy in range(ys)
            ],
            axis=0,
        )

    def side_of(place):
        return 1 if (place + place // zs) % 2 == 0 else -1

    def y_copies(source, target, way, number, send, recv):
        def direct(place, dy):
            return remote(
                source.at[place, dy],
                target.at[place, ys - dy],
                send.at[place, dy],
                recv.at[place, ys - dy],
                at(dy=dy),
            )

        def first_leg(place):
            return remote(
                source.at[place, 2],
                way.at[place],
                vsend.at[number, place],
                vrecv.at[number, place],
                at(dy=side_of(place)),
            )

        def second_leg(place):
            return remote(
                way.at[place],
                target.at[place, 2],
                send.at[place, 2],
                recv.at[place, 2],
                at(dy=side_of(place)),
            )

        def start(place):
            go(direct(place, 2) if place % zs == zs - 1 else first_leg(place))
            go(direct(place, 1))
            go(direct(place, ys - 1))

        def relay(*places):
            for place in places:
                first_leg(place).wait_recv()
                go(second_leg(place))

        def arrived(place):
            direct(place, 1).wait_recv()
            direct(place, ys - 1).wait_recv()
            (direct(place, 2) if place % zs == zs - 1 else second_leg(place)).wait_recv()

        return start, relay, arrived

    send_pieces, relay_pieces, pieces_here = y_copies(packed, rows, way_out, 0, ysend, yrecv)
    send_backs, relay_backs, backs_here = y_copies(outs, backs, way_back, 1, bsend, brecv)

    def pack(place):
        if place > 0:
            table_copies[(zs - ORDER[place])].wait_recv()
        chosen = jnp.where(spread(place, 0) == slot, 1.0, 0.0).astype(jnp.bfloat16)
        value = jnp.dot(
            chosen[:, :ROWS_BLOCK], tokens[place], preferred_element_type=jnp.float32
        ).astype(jnp.bfloat16)
        value = value.reshape(ys, PIECE, width)
        packed[place, 1:] = value[1:]
        rows[place, 0] = value[0]
        send_pieces(place)

    def experts(first, count):
        for place in range(first, first + count):
            pieces_here(place)
        taken = rows[first : first + count].reshape(count * ys * PIECE, width)
        hidden = []
        for side in range(2):
            both = jnp.dot(taken, gate_up[side], preferred_element_type=jnp.float32)
            both = jax.nn.relu(both[:, :half_units]) * both[:, half_units:]
            hidden.append(both.astype(jnp.bfloat16))
        for columns in range(2):
            span = slice(columns * split, (columns + 1) * split)
            value = jnp.dot(hidden[0], down[0, :, span], preferred_element_type=jnp.float32)
            value = value + jnp.dot(
                hidden[1], down[1, :, span], preferred_element_type=jnp.float32
            )
            value = value.astype(jnp.bfloat16).reshape(count, ys, PIECE, split)
            base = columns * zs + first
            outs[base : base + count, 1:] = value[:, 1:]
            backs[base : base + count, 0] = value[:, 0]
        for place in reversed(range(first, first + count)):
            send_backs(place)

    def combine(place):
        backs_here(place)
        mixing = jnp.where(
            spread(place % zs, 0) == slot, spread(place % zs, ys), 0.0
        ).astype(jnp.bfloat16)[:, :ROWS_BLOCK]
        partial[place] = lax.dot_general(
            mixing,
            backs[place].reshape(ys * PIECE, split),
            (((0,), (0,)), ((), ())),
            preferred_element_type=jnp.float32,
        )

    def tokens_step(step):
        for piece in range(2):
            for direction in (1, -1):
                if (direction, step - 1, piece) in flow:
                    flow[direction, step - 1, piece].wait_recv()
                if (direction, step, piece) in flow:
                    go(flow[direction, step, piece])

    pack(0)
    tokens_step(1)
    relay_pieces(0)
    pack(1)
    pack(2)
    for copy in own_copies:
        copy.wait()
    for copy in weight_copies:
        copy.wait_recv()
    tokens_step(2)
    relay_pieces(1, 2)
    pack(3)
    pack(4)
    tokens_step(3)
    relay_pieces(3, 4)
    pack(5)
    pack(6)
    experts(0, 3)
    tokens_step(4)
    relay_pieces(5, 6)
    pack(7)
    relay_backs(0, 1, 2)
    experts(3, 2)
    combine(0)
    combine(1)
    combine(2)
    relay_backs(3, 4)
    experts(5, 3)
    for place in reversed(range(zs)):
        send_backs(zs + place)
    combine(3)
    combine(4)
    relay_backs(6, 5)

    returned = {}

    def pass_on(columns, direction, distance, piece):
        held = distance if direction == 1 else zs - distance
        number = distance * 2 + piece
        side = columns * 2 + (0 if direction == 1 else 1)
        value = partial[columns * zs + PLACE[held], pl.ds(piece * chunk, chunk)]
        before_it = returned.get((columns, direction, distance + 1, piece))
        if before_it is not None:
            before_it.wait_recv()
            value = value + got[side, number + 2].astype(jnp.float32)
        sums[side, number] = value.astype(jnp.bfloat16)
        returned[columns, direction, distance, piece] = go(
            remote(
                sums.at[side, number],
                got.at[side, number],
                ssend.at[side, number],
                srecv.at[side, number],
                at(dz=direction),
            )
        )

    def far_sums(columns):
        combine(columns * zs + PLACE[reach])
        pass_on(columns, 1, reach, 0)
        pass_on(columns, -1, reach, 1)
        combine(columns * zs + PLACE[reach - 1])
        pass_on(columns, 1, reach - 1, 1)
        combine(columns * zs + PLACE[zs - reach + 1])
        pass_on(columns, -1, reach - 1, 0)

    def near_sums(columns, distance):
        if distance < reach - 1:
            pass_on(columns, 1, distance, 1)
            pass_on(columns, -1, distance, 0)
        pass_on(columns, 1, distance, 0)
        pass_on(columns, -1, distance, 1)

    def last_copy(dx, piece):
        spot = pl.ds(piece * chunk, chunk)
        return remote(
            final.at[(head + dx) % xs, spot],
            out_ref.at[head, spot],
            xsend.at[dx, piece],
            xrecv.at[xs - dx, piece],
            at(dx=dx),
        )

    def finish(columns):
        share = width // xs
        for piece in (1, 0):
            spot = pl.ds(piece * chunk, chunk)
            for direction in (1, -1):
                returned[columns, direction, 1, piece].wait_recv()
            value = (
                mid_ref[spot, columns * split : (columns + 1) * split].astype(jnp.float32)
                + partial[columns * zs, spot]
                + got[columns * 2, 2 + piece].astype(jnp.float32)
                + got[columns * 2 + 1, 2 + piece].astype(jnp.float32)
            ).astype(jnp.bfloat16)
            for number in range(split // share):
                final[columns * (split // share) + number, spot] = value[
                    :, number * share : (number + 1) * share
                ]
            for dx in range(1, xs):

                @pl.when((head + dx) % xs // (split // share) == columns)
                def _():
                    last_copy(dx, piece).start()


    far_sums(0)
    relay_backs(zs + 6, zs + 5)
    near_sums(0, 3)
    relay_backs(zs + 4, zs + 3)
    near_sums(0, 2)
    relay_backs(zs + 2, zs + 1, zs)
    far_sums(1)
    near_sums(0, 1)
    combine(zs + 4)
    combine(zs + 3)
    near_sums(1, 3)
    combine(zs + 2)
    combine(zs + 1)
    combine(zs)
    finish(0)
    near_sums(1, 2)
    near_sums(1, 1)
    finish(1)

    out_ref[head] = final[head]
    for piece in (1, 0):
        for dx in range(1, xs):
            last_copy(dx, piece).wait()

    for copy in sent:
        copy.wait_send()


def layer(
    sizes,
    hidden,
    gain,
    w_query,
    w_keyval,
    prefix,
    w_out,
    moe_gain,
    w_gateup,
    w_down,
    routes,
    weights,
    lengths,
):
    xs, ys, zs = sizes
    count, width = hidden.shape
    heads = w_query.shape[1] // HD
    part = count // xs
    lanes = 128
    bf16, f32 = jnp.bfloat16, jnp.float32
    half = np.arange(HD // 2, dtype=np.float32)
    freqs = (10000.0 ** (-2.0 * half / HD)).astype(np.float32)
    freqs = jnp.asarray(np.concatenate([freqs, freqs])[None, :])
    dma = pltpu.SemaphoreType.DMA
    vmem = pl.BlockSpec(memory_space=pltpu.VMEM)
    smem = pl.BlockSpec(memory_space=pltpu.SMEM)
    hbm = pl.BlockSpec(memory_space=pl.ANY)
    out = pl.pallas_call(
        functools.partial(layer_kernel, sizes),
        out_shape=jax.ShapeDtypeStruct((xs, part, width // xs), bf16),
        in_specs=[smem, vmem, vmem, vmem, vmem, hbm, vmem, hbm, vmem, vmem, vmem, hbm, hbm],
        out_specs=vmem,
        scratch_shapes=[
            pltpu.VMEM(w_keyval.shape[1:], bf16),
            pltpu.VMEM((CORES, ys, zs, prefix.shape[0], 2 * HD), bf16),
            pltpu.VMEM((PAST + 1, 2, CORES, count, HD), bf16),
            pltpu.VMEM((xs,) + w_out.shape, bf16),
            pltpu.VMEM((heads, count, HD), bf16),
            pltpu.VMEM((1, count), jnp.int32),
            pltpu.VMEM((heads, 1, count), f32),
            pltpu.VMEM((heads, 1, count), f32),
            pltpu.VMEM((heads, HD, count), f32),
            pltpu.VMEM((xs, part, heads * HD), bf16),
            pltpu.VMEM((xs, part, heads * HD), bf16),
            pltpu.VMEM((part, width), bf16),
            pltpu.VMEM((zs, part, width), bf16),
            pltpu.VMEM((zs, 2 * ys, lanes), f32),
            pltpu.VMEM((zs, 2 * ys, lanes), f32),
            pltpu.VMEM((zs, ys, PIECE, width), bf16),
            pltpu.VMEM((zs, ys, PIECE, width), bf16),
            pltpu.VMEM((2 * zs, ys, PIECE, width // 2), bf16),
            pltpu.VMEM((2 * zs, ys, PIECE, width // 2), bf16),
            pltpu.VMEM((zs, PIECE, width), bf16),
            pltpu.VMEM((2 * zs, PIECE, width // 2), bf16),
            pltpu.VMEM((2,) + w_gateup.shape[1:], bf16),
            pltpu.VMEM((2,) + w_down.shape[1:], bf16),
            pltpu.VMEM((2 * zs, part, width // 2), f32),
            pltpu.VMEM((4, zs + 2, part // 2, width // 2), bf16),
            pltpu.VMEM((4, zs + 2, part // 2, width // 2), bf16),
            pltpu.VMEM((xs, part, width // xs), bf16),
            dma((4,)),
            dma((2, zs // 2)),
            dma((2, zs // 2)),
            dma((ys, 2)),
            dma((ys, 2)),
            dma((ys, 2)),
            dma((ys, 2)),
            dma((PAST, 2)),
            dma((PAST, 2)),
            dma((PAST + 1, 2)),
            dma((PAST + 1, 2)),
            dma((xs,)),
            dma((xs,)),
            dma((xs,)),
            dma((xs,)),
            dma((xs,)),
            dma((xs,)),
            dma((2,)),
            dma((2,)),
            dma((zs,)),
            dma((zs,)),
            dma((2, zs)),
            dma((2, zs)),
            dma((zs, ys)),
            dma((zs, ys)),
            dma((2 * zs, ys)),
            dma((2 * zs, ys)),
            dma((2, 2 * zs)),
            dma((2, 2 * zs)),
            dma((4, zs + 2)),
            dma((4, zs + 2)),
            dma((xs, 2)),
            dma((xs, 2)),
        ],
        compiler_params=pltpu.CompilerParams(
            collective_id=0, has_side_effects=True, vmem_limit_bytes=62 * 2**20
        ),
    )(
        lengths,
        hidden,
        gain,
        freqs,
        w_query,
        w_keyval,
        prefix,
        w_out,
        moe_gain,
        routes.T,
        weights.T,
        w_gateup,
        w_down,
    )
    return out.reshape(count, width // xs)


def shards(
    hidden_in,
    attn_gain,
    w_query,
    w_keyval,
    prefix_cache,
    w_out,
    moe_gain,
    w_gateup,
    w_down,
    routes,
    route_weights,
    lengths,
):
    chips_z = 8
    sizes = (lax.axis_size("head"), lax.axis_size("blk") // (CORES * chips_z), chips_z)
    return layer(
        sizes,
        hidden_in,
        attn_gain,
        w_query,
        w_keyval,
        prefix_cache,
        w_out,
        moe_gain,
        w_gateup,
        w_down,
        routes,
        route_weights,
        lengths,
    )


def solution(mesh):
    return jax.shard_map(
        shards,
        mesh=mesh,
        in_specs=(
            P("blk", None),
            P(),
            P(None, "head"),
            P(),
            P("blk", None, None),
            P("head", None),
            P(),
            P("blk", None, None),
            P("blk", None, None),
            P("blk", None),
            P("blk", None),
            P(),
        ),
        out_specs=P("blk", "head"),
        check_vma=False,
    )
```
